32 devices in a mesh: groups: 2 (over y), srv: 4 (over z), hid: 2 (over x), rep: 2 (over core).
Axes of the slice: x: 2, y: 2, z: 4, core: 2. Of those that a mesh axis runs over, the one named last changes fastest.
Arguments:
- layer_input: bfloat16 [2048, 4096], P(('groups', 'srv'), ('hid', 'rep')), parts along dimension 0, may hold values from -12 to 12
- query_weight: bfloat16 [4096, 4096], P('srv', ('hid', 'rep')), may hold values from -0.09375 to 0.09375
- key_weight: bfloat16 [4096, 1024], P('srv', ('hid', 'rep')), may hold values from -0.09375 to 0.09375
- value_weight: bfloat16 [4096, 1024], P('srv', ('hid', 'rep')), may hold values from -0.09375 to 0.09375
- out_grad: bfloat16 [2048, 4096], P(('groups', 'srv'), ('hid', 'rep')), parts along dimension 0, may hold values from -6 to 6
- doc_ids: int32 [2048], P('groups'), parts along dimension 0, may hold values from 0 to 7, never falling along the last dimension, each value on 1 to 512 neighbouring positions
Outputs:
- input_grad: bfloat16 [2048, 4096], P(('groups', 'srv'), ('hid', 'rep')), parts along dimension 0
- query_weight_grad: float32 [8192, 4096], P(('groups', 'srv'), ('hid', 'rep')), parts along dimension 0
- key_weight_grad: float32 [8192, 1024], P(('groups', 'srv'), ('hid', 'rep')), parts along dimension 0
- value_weight_grad: float32 [8192, 1024], P(('groups', 'srv'), ('hid', 'rep')), parts along dimension 0
The draws below stay inside these ranges and needn't reach their ends.
There are 2 independent parts, one for each index of `groups`. The reference program is written for one: setup_inputs(seed, part) draws one part's arguments, and reference() takes and returns one part's arrays. A program takes and returns all parts, laid end to end along the dimension named above; an argument that names none is the same for every part. Nothing has to cross between parts.
Inputs may be any that keep to these rules, and one draw needn't show every extreme that they name: `doc_ids`: document numbers never fall along the tokens; every document holds at most 512 tokens and one holds exactly 512.
All inputs are finite; a program needn't handle non-finite values.
Results may differ from the reference program's by a relative error of at most 0.011.
Values may be sent and summed in bfloat16 or wider, within the bound.
No kernel may reach another device: no remote copies, remote signals or barrier semaphores. Data moves between devices by JAX's collectives and lax.ppermute only.
A program may use at most 64 MiB of HBM per device.

```python
import math
import jax
import jax.numpy as jnp
import numpy as np
from jax import lax

D = 4096
HQ = 32
HK = 8
DH = 128
DOCS = 8
TOKENS = 1024
MAXDOC = 512


def draw_layer_input(key, part):
    values_drawn = jax.random.normal(jax.random.fold_in(key, 11), (TOKENS, D), jnp.float32)
    values_drawn = jnp.clip(values_drawn, -6.0, 6.0)
    return values_drawn.astype(jnp.bfloat16)


def block_levels(rng, extent, cuts, smallest, largest):
    factor_of = 1.0
    for dim, shards_of in cuts:
        heights = jax.random.uniform(jax.random.fold_in(jax.random.fold_in(rng, 6), dim), (shards_of,), jnp.float32, smallest / len(cuts), largest / len(cuts))
        factor_of = factor_of * jnp.repeat(jnp.exp(heights), extent[dim] // shards_of).reshape((-1,) + (1,) * (len(extent) - 1 - dim))
    return factor_of


def length_profile(count, total, limit, skew):
    weights = [(1 << 20) // math.isqrt(rank ** skew) + 1 for rank in range(2, count + 1)]
    spare, holding = total - limit - (count - 1), [1] * (count - 1)
    while spare > 0:
        movable = [i for i in range(count - 1) if holding[i] < limit]
        whole, remaining = sum([weights[i] for i in movable]), spare
        for i in movable:
            more = min(limit - holding[i], max(1, remaining * weights[i] // whole), spare)
            holding[i] = holding[i] + more
            spare = spare - more
    return np.array([limit] + holding)


def uneven_parts(own_key, number_of, total, limit, skew):
    if number_of == 2:
        one = jax.random.randint(own_key, (), max(1, total - limit), min(limit, total - 1) + 1)
        return jnp.stack([one, total - one])
    sizes = jnp.asarray(length_profile(number_of, total, limit, skew), jnp.int32)
    pairs = (number_of - 1) // 2
    giver, sink = sizes[1:1 + 2 * pairs:2], sizes[2:2 + 2 * pairs:2]
    margin = jnp.minimum(giver - 1, limit - sink)
    shifted = jax.random.randint(jax.random.fold_in(own_key, 1), (pairs,), 0, 1 << 20) % (margin + 1)
    sizes = sizes.at[1:1 + 2 * pairs:2].set(giver - shifted).at[2:2 + 2 * pairs:2].set(sink + shifted)
    return sizes[jax.random.permutation(jax.random.fold_in(own_key, 2), number_of)]


def centred(key, extent, deviation, bound, pieces=(), kind=jnp.bfloat16):
    array = jax.random.normal(key, extent, jnp.float32) * deviation
    if len(pieces) > 0:
        array = block_levels(key, extent, pieces, -0.22, 0.18) * array
    return jnp.clip(array, min=-bound, max=bound).astype(kind)


def setup_inputs(seed: int = 0, part: int = 0) -> dict:
    keys = jax.random.split(jax.random.key(seed), 7)
    own_keys = jax.random.split(jax.random.fold_in(keys[6], part), 7)
    layer_input = draw_layer_input(jax.random.fold_in(jax.random.fold_in(keys[6], part), 71), part)
    query_weight = centred(keys[1], (D, HQ * DH), D ** -0.5, 0.09375, ((0, 4), (1, 4)))
    key_weight = centred(keys[2], (D, HK * DH), D ** -0.5, 0.09375, ((0, 4), (1, 4)))
    value_weight = centred(keys[3], (D, HK * DH), D ** -0.5, 0.09375, ((0, 4), (1, 4)))
    out_grad = centred(own_keys[4], (TOKENS, HQ * DH), 1.0, 6.0, ((0, 4), (1, 4)))
    doc_ids = jnp.searchsorted(jnp.cumsum(uneven_parts(own_keys[5], DOCS, TOKENS, MAXDOC, 2)), jnp.arange(TOKENS), side="right").astype(jnp.int32)
    return dict(layer_input=layer_input, query_weight=query_weight, key_weight=key_weight, value_weight=value_weight, out_grad=out_grad, doc_ids=doc_ids)


NEGATIVE = -1e30


def reference(layer_input, query_weight, key_weight, value_weight, out_grad, doc_ids):
    total_rows = layer_input.shape[0]
    group_size = HQ // HK
    factor_scale = DH ** -0.5
    queries = jnp.dot(layer_input, query_weight, preferred_element_type=jnp.float32).astype(jnp.bfloat16).reshape(total_rows, HQ, DH)
    keys_all = jnp.dot(layer_input, key_weight, preferred_element_type=jnp.float32).astype(jnp.bfloat16).reshape(total_rows, HK, DH)
    values_all = jnp.dot(layer_input, value_weight, preferred_element_type=jnp.float32).astype(jnp.bfloat16).reshape(total_rows, HK, DH)
    cotangent = out_grad.reshape(total_rows, HQ, DH)
    positions = jnp.arange(total_rows, dtype=jnp.int32)
    allowed = (doc_ids[None, :] == doc_ids[:, None]) & (positions[None, :] <= positions[:, None])

    def one_head(head_id):
        pair_id = head_id // group_size
        query_rows = lax.dynamic_index_in_dim(queries, head_id, 1, keepdims=False)
        key_rows = lax.dynamic_index_in_dim(keys_all, pair_id, 1, keepdims=False)
        value_rows = lax.dynamic_index_in_dim(values_all, pair_id, 1, keepdims=False)
        grad_rows = lax.dynamic_index_in_dim(cotangent, head_id, 1, keepdims=False)
        logits = jnp.dot(query_rows, key_rows.T, preferred_element_type=jnp.float32) * factor_scale
        logits = jnp.where(allowed, logits, NEGATIVE)
        weights = jnp.where(allowed, jnp.exp(logits - jnp.max(logits, axis=1, keepdims=True)), 0.0)
        attention = weights / jnp.sum(weights, axis=1, keepdims=True)
        slopes = jnp.dot(grad_rows, value_rows.T, preferred_element_type=jnp.float32)
        inner_sum = jnp.sum(attention * slopes, axis=1, keepdims=True)
        score_grad = (attention * (slopes - inner_sum) * factor_scale).astype(jnp.bfloat16)
        value_grad = jnp.dot(attention.astype(jnp.bfloat16).T, grad_rows, preferred_element_type=jnp.float32)
        key_grad = jnp.dot(score_grad.T, query_rows, preferred_element_type=jnp.float32)
        query_grad = jnp.dot(score_grad, key_rows, preferred_element_type=jnp.float32)
        return query_grad, key_grad, value_grad

    query_grad, key_grad, value_grad = lax.map(one_head, jnp.arange(HQ, dtype=jnp.int32))
    query_grad = jnp.transpose(query_grad.astype(jnp.bfloat16), (1, 0, 2)).reshape(total_rows, HQ * DH)
    key_grad = jnp.sum(key_grad.reshape(HK, group_size, total_rows, DH), axis=1).astype(jnp.bfloat16)
    key_grad = jnp.transpose(key_grad, (1, 0, 2)).reshape(total_rows, HK * DH)
    value_grad = jnp.sum(value_grad.reshape(HK, group_size, total_rows, DH), axis=1).astype(jnp.bfloat16)
    value_grad = jnp.transpose(value_grad, (1, 0, 2)).reshape(total_rows, HK * DH)
    input_grad = jnp.dot(query_grad, query_weight.T, preferred_element_type=jnp.float32)
    input_grad = input_grad + jnp.dot(key_grad, key_weight.T, preferred_element_type=jnp.float32)
    input_grad = input_grad + jnp.dot(value_grad, value_weight.T, preferred_element_type=jnp.float32)
    query_weight_grad = jnp.dot(layer_input.T, query_grad, preferred_element_type=jnp.float32)
    key_weight_grad = jnp.dot(layer_input.T, key_grad, preferred_element_type=jnp.float32)
    value_weight_grad = jnp.dot(layer_input.T, value_grad, preferred_element_type=jnp.float32)
    return input_grad.astype(jnp.bfloat16), query_weight_grad, key_weight_grad, value_weight_grad
```

```python
import functools

import jax
import jax.numpy as jnp
from jax import lax
from jax.experimental import pallas as pl
from jax.experimental.pallas import tpu as pltpu
from jax.sharding import PartitionSpec as P

HQ = 32
HK = 8
DH = 128
BLOCK = 128


NEGATIVE = -1e30


def attend(queries, cotangent, keys_all, values_all, doc_ids, block_id, carried):
    row_count = queries.shape[0]
    factor_scale = queries.shape[-1] ** (-0.5)
    offsets = jnp.arange(row_count, dtype=jnp.int32)
    query_pos = block_id * row_count + offsets
    query_doc = lax.dynamic_slice_in_dim(doc_ids, block_id * row_count, row_count)
    doc_start = jnp.sum((doc_ids < query_doc[0]).astype(jnp.int32))
    lowest = doc_start // row_count
    highest = jnp.where(True, block_id + 1, lowest)

    def scores_at(key_block):
        key_rows = lax.dynamic_slice_in_dim(keys_all, key_block * row_count, row_count, 0)
        value_rows = lax.dynamic_slice_in_dim(values_all, key_block * row_count, row_count, 0)
        key_doc = lax.dynamic_slice_in_dim(doc_ids, key_block * row_count, row_count)
        key_pos = key_block * row_count + offsets
        allowed = (key_doc[None, :] == query_doc[:, None]) & (
            key_pos[None, :] <= query_pos[:, None]
        )
        logits = (
            jnp.einsum("qgnd,kgd->gnqk", queries, key_rows, preferred_element_type=jnp.float32)
            * factor_scale
        )
        logits = jnp.where(allowed, logits, NEGATIVE)
        slopes = jnp.einsum(
            "qgnd,kgd->gnqk", cotangent, value_rows, preferred_element_type=jnp.float32
        )
        return (key_rows, allowed, logits, slopes)

    def first_pass(key_block, loop_state):
        row_peak, row_total, row_inner = loop_state
        key_rows, allowed, logits, slopes = scores_at(key_block)
        new_peak = jnp.maximum(row_peak, jnp.max(logits, axis=-1))
        weights = jnp.where(allowed, jnp.exp(logits - new_peak[..., None]), 0.0)
        factor = jnp.exp(row_peak - new_peak)
        row_total = row_total * factor + jnp.sum(weights, axis=-1)
        row_inner = row_inner * factor + jnp.sum(weights * slopes, axis=-1)
        return (new_peak, row_total, row_inner)

    stat_shape = (queries.shape[1], queries.shape[2], row_count)
    initial = (
        jnp.full(stat_shape, NEGATIVE, jnp.float32),
        jnp.zeros(stat_shape, jnp.float32),
        jnp.zeros(stat_shape, jnp.float32),
    )
    row_peak, row_total, row_inner = lax.fori_loop(lowest, highest, first_pass, initial)
    safe_total = jnp.where(True, row_total, 1.0)
    row_delta = row_inner / safe_total
    log_total = row_peak + jnp.log(safe_total)

    def second_pass(key_block, loop_state):
        query_grad, key_accum, value_accum = loop_state
        key_rows, allowed, logits, slopes = scores_at(key_block)
        attention = jnp.where(allowed, jnp.exp(logits - log_total[..., None]), 0.0)
        score_grad = (attention * (slopes - row_delta[..., None]) * factor_scale).astype(
            jnp.bfloat16
        )
        value_part = jnp.einsum(
            "gnqk,qgnd->kgd",
            attention.astype(jnp.bfloat16),
            cotangent,
            preferred_element_type=jnp.float32,
        )
        key_part = jnp.einsum(
            "gnqk,qgnd->kgd", score_grad, queries, preferred_element_type=jnp.float32
        )
        query_grad = query_grad + jnp.einsum(
            "gnqk,kgd->qgnd", score_grad, key_rows, preferred_element_type=jnp.float32
        )
        first_row = key_block * row_count
        key_accum = lax.dynamic_update_slice_in_dim(
            key_accum,
            lax.dynamic_slice_in_dim(key_accum, first_row, row_count, 0) + key_part,
            first_row,
            0,
        )
        value_accum = lax.dynamic_update_slice_in_dim(
            value_accum,
            lax.dynamic_slice_in_dim(value_accum, first_row, row_count, 0) + value_part,
            first_row,
            0,
        )
        return (query_grad, key_accum, value_accum)

    start_grad = jnp.zeros(queries.shape, jnp.float32)
    query_grad, key_accum, value_accum = lax.fori_loop(
        lowest, highest, second_pass, (start_grad, carried[0], carried[1])
    )
    return (query_grad, (key_accum, value_accum))


def body(layer_input, query_weight, key_weight, value_weight, out_grad, doc_ids):
    tok_rows = layer_input.shape[0]
    query_width = query_weight.shape[1]
    pair_width = key_weight.shape[1]
    key_heads = pair_width // DH
    group_size = HQ // HK
    block_count = tok_rows // BLOCK
    owner_id = lax.axis_index("srv")
    weights_all = lax.all_gather(
        jnp.concatenate([query_weight, key_weight, value_weight], axis=1), "srv", axis=0, tiled=True
    )
    inputs_all = lax.all_gather(layer_input, ("hid", "rep"), axis=1, tiled=True)
    projected = jnp.dot(inputs_all, weights_all, preferred_element_type=jnp.float32).astype(
        jnp.bfloat16
    )
    queries = projected[:, :query_width].reshape(block_count, BLOCK, key_heads, group_size, DH)
    keys_local = projected[:, query_width : query_width + pair_width]
    values_local = projected[:, query_width + pair_width :]
    keys_all, values_all = (
        lax.all_gather(keys_local, "srv", axis=0, tiled=True),
        lax.all_gather(values_local, "srv", axis=0, tiled=True),
    )
    total_rows = keys_all.shape[0]
    keys_all = keys_all.reshape(total_rows, key_heads, DH)
    values_all = values_all.reshape(total_rows, key_heads, DH)
    cotangent = out_grad.reshape(block_count, BLOCK, key_heads, group_size, DH)
    empty_accum = jnp.zeros((total_rows, key_heads, DH), jnp.float32)

    def own_block(position, loop_state):
        answers, carried = loop_state
        grad_q, carried = attend(
            lax.dynamic_index_in_dim(queries, position, 0, keepdims=False),
            lax.dynamic_index_in_dim(cotangent, position, 0, keepdims=False),
            keys_all,
            values_all,
            doc_ids,
            owner_id * block_count + position,
            carried,
        )
        answers = lax.dynamic_update_index_in_dim(answers, grad_q.astype(jnp.bfloat16), position, 0)
        return (answers, carried)

    answers = jnp.zeros(queries.shape, jnp.bfloat16)
    answers, carried = lax.fori_loop(
        0, block_count, own_block, (answers, (empty_accum, empty_accum))
    )
    query_grad = answers.reshape(tok_rows, query_width)
    key_accum, value_accum = carried
    key_sum, value_sum = (
        lax.psum_scatter(key_accum, "srv", scatter_dimension=0, tiled=True),
        lax.psum_scatter(value_accum, "srv", scatter_dimension=0, tiled=True),
    )
    grads_all = jnp.concatenate(
        [
            query_grad,
            key_sum.astype(jnp.bfloat16).reshape(tok_rows, pair_width),
            value_sum.astype(jnp.bfloat16).reshape(tok_rows, pair_width),
        ],
        axis=1,
    )
    input_terms = lax.dot_general(
        grads_all, weights_all, (((1,), (1,)), ((), ())), preferred_element_type=jnp.float32
    )
    input_grad = lax.psum_scatter(
        input_terms, ("hid", "rep"), scatter_dimension=1, tiled=True
    ).astype(jnp.bfloat16)
    columns = lax.all_to_all(inputs_all, "srv", split_axis=1, concat_axis=0, tiled=True)
    weight_grad = lax.dot_general(
        columns,
        lax.all_gather(grads_all, "srv", axis=0, tiled=True),
        (((0,), (0,)), ((), ())),
        preferred_element_type=jnp.float32,
    )
    return (
        input_grad,
        weight_grad[:, :query_width],
        weight_grad[:, query_width : query_width + pair_width],
        weight_grad[:, query_width + pair_width :],
    )


def exchange(array, axis, size):
    return lax.ppermute(array, axis, [(i, (i + 1) % size) for i in range(size)])


def attention_kernel(active_ref, doc_row_ref, doc_col_ref, q_ref, k_ref, v_ref, g_ref, dk_in, dv_in, dq_ref, dk_ref, dv_ref, *, block, window):
    rows, width = q_ref.shape
    scale = width ** (-0.5)
    dk_ref[...] = dk_in[...]
    dv_ref[...] = dv_in[...]

    @pl.when(active_ref[0] == 0)
    def _():
        dq_ref[...] = jnp.zeros_like(dq_ref)

    @pl.when(active_ref[0] != 0)
    def _():
        for first in range(0, rows, block):
            low = max(0, first - window)
            span = first + block - low
            q = q_ref[first : first + block, :]
            g = g_ref[first : first + block, :]
            k = k_ref[low : low + span, :]
            v = v_ref[low : low + span, :]
            nt = (((1,), (1,)), ((), ()))
            logits = lax.dot_general(k, q, nt, preferred_element_type=jnp.float32) * scale
            slopes = lax.dot_general(v, g, nt, preferred_element_type=jnp.float32)
            key_pos = lax.broadcasted_iota(jnp.int32, (span, block), 0) + low
            query_pos = lax.broadcasted_iota(jnp.int32, (span, block), 1) + first
            same = doc_col_ref[low : low + span, :] == doc_row_ref[:, first : first + block]
            allowed = same & (key_pos <= query_pos)
            logits = jnp.where(allowed, logits, NEGATIVE)
            peak = jnp.max(logits, axis=0, keepdims=True)
            weights = jnp.exp(logits - peak)
            total = jnp.sum(weights, axis=0, keepdims=True)
            inner = jnp.sum(weights * slopes, axis=0, keepdims=True) / total
            attention = weights * (1.0 / total)
            score = (attention * (slopes - inner) * scale).astype(jnp.bfloat16)
            dv_ref[low : low + span, :] += jnp.dot(
                attention.astype(jnp.bfloat16), g, preferred_element_type=jnp.float32
            )
            dk_ref[low : low + span, :] += jnp.dot(score, q, preferred_element_type=jnp.float32)
            dq_ref[first : first + block, :] = lax.dot_general(
                score, k, (((0,), (0,)), ((), ())), preferred_element_type=jnp.float32
            ).astype(dq_ref.dtype)


def attend_head(active, doc_row, doc_col, q, k, v, g, head, dk, dv, block, window):
    rows, width = q.shape
    whole = lambda shape: pl.BlockSpec(shape, lambda i, a: (0, 0))
    square = whole((rows, width))
    return pl.pallas_call(
        functools.partial(attention_kernel, block=block, window=window),
        grid_spec=pltpu.PrefetchScalarGridSpec(
            num_scalar_prefetch=1,
            grid=(1,),
            in_specs=[
                whole((1, rows)),
                whole((rows, 1)),
                square,
                square,
                square,
                pl.BlockSpec((rows, width), lambda i, a: (0, head)),
                square,
                square,
            ],
            out_specs=[square, square, square],
        ),
        out_shape=[
            jax.ShapeDtypeStruct((rows, width), jnp.bfloat16),
            jax.ShapeDtypeStruct((rows, width), jnp.float32),
            jax.ShapeDtypeStruct((rows, width), jnp.float32),
        ],
        cost_estimate=pl.CostEstimate(
            flops=6 * rows * rows * width, bytes_accessed=rows * width * 28, transcendentals=rows * rows // 2
        ),
    )(active, doc_row, doc_col, q, k, v, g, dk, dv)


def stationary_body(sizes, layer_input, query_weight, key_weight, value_weight, out_grad, doc_ids):
    planes, across, cores = sizes
    spread = across * cores
    f32, bf16 = jnp.float32, jnp.bfloat16
    tok, width = layer_input.shape
    total = tok * planes
    half_q, half_k = query_weight.shape[1] // 2, key_weight.shape[1] // 2
    heads = half_q // DH
    plane = lax.axis_index("srv")
    column = lax.axis_index("hid") * cores + lax.axis_index("rep")
    near_left = plane < planes // 2
    is_end = (plane == 0) | (plane == planes - 1)
    last = planes - 1
    line = [[(k, k + 1), (last - k, last - k - 1)] for k in range(last)]
    trio = ("srv", "hid", "rep")
    straight = [(t * spread + f, f * spread + t) for t in range(planes) for f in range(spread)]
    crossed = [(t * spread + f, f * spread + (t + cores) % spread) for t in range(planes) for f in range(spread)]
    straight_back = [(b, a) for a, b in straight]
    crossed_back = [(b, a) for a, b in crossed]

    with jax.named_scope("inputs"):
        one = lax.ppermute(layer_input, trio, straight)
        two = lax.ppermute(layer_input, trio, crossed)
        rows_all = jnp.zeros((total, width), bf16)
        own_one, own_two = column, (column + cores) % spread
        mate = lambda t: t - t % cores + (t + 1) % cores
        for block, index in (
            (one, own_one),
            (two, own_two),
            (exchange(one, "rep", cores), mate(own_one)),
            (exchange(two, "rep", cores), mate(own_two)),
        ):
            rows_all = lax.dynamic_update_slice_in_dim(rows_all, block, index * tok, 0)

    far_at, near_at = jnp.where(near_left, 1, 0), jnp.where(near_left, 0, 1)

    def part(array, at, size):
        return lax.dynamic_slice_in_dim(array, at * size, size, 1)

    with jax.named_scope("cotangent"):
        g_near, g_far = part(out_grad, near_at, half_q), part(out_grad, far_at, half_q)
        place = lambda d: jnp.where(plane == 0, d, last - d) * tok
        g_all = lax.dynamic_update_slice_in_dim(jnp.zeros((total, half_q), bf16), g_near, place(0), 0)
        for d in range(1, planes):
            arrived = lax.ppermute(g_near if d < planes // 2 else g_far, "srv", [(d, 0), (last - d, last)])
            g_all = lax.dynamic_update_slice_in_dim(g_all, arrived, place(d), 0)

    w_near = jnp.concatenate([part(key_weight, near_at, half_k), part(value_weight, near_at, half_k), part(query_weight, near_at, half_q)], axis=1)
    w_far = jnp.concatenate([part(key_weight, far_at, half_k), part(value_weight, far_at, half_k), part(query_weight, far_at, half_q)], axis=1)

    spans = [(0, 2 * DH)] + [((2 + h) * DH, (3 + h) * DH) for h in range(heads)]
    arrived_parts = []
    with jax.named_scope("chain"):
        for low, high in spans:
            far = jnp.dot(rows_all, w_far[:, low:high], preferred_element_type=f32)
            near = jnp.dot(rows_all, w_near[:, low:high], preferred_element_type=f32)
            moving = None
            for k in range(last):
                mine = far if k < planes // 2 else near
                if moving is not None:
                    mine = mine + moving.astype(f32)
                moving = lax.ppermute(mine.astype(bf16), "srv", line[k])
            arrived_parts.append((near + moving.astype(f32)).astype(bf16))

    keys, values = arrived_parts[0][:, :DH], arrived_parts[0][:, DH:]
    active = is_end.astype(jnp.int32).reshape(1)
    doc_row, doc_col = doc_ids.reshape(1, total), doc_ids.reshape(total, 1)
    dk = dv = jnp.zeros((total, DH), f32)

    def spread_out(local):
        near, far = local, None
        moving = local
        for k in range(last):
            moving = lax.ppermute(moving, "srv", line[k])
            if k < planes // 2 - 1:
                near = near + moving
            else:
                far = moving if far is None else far + moving
        return near, far

    results = []
    with jax.named_scope("attend"):
        for h in range(heads):
            dq, dk, dv = attend_head(
                active, doc_row, doc_col, arrived_parts[1 + h], keys, values, g_all, h, dk, dv, tok, total // 2
            )
            results.append(spread_out(dq))
        end_f = is_end.astype(f32)
        tail = jnp.concatenate([dk * end_f, dv * end_f], axis=1).astype(bf16)
        results = [spread_out(tail)] + results
    grads_near = jnp.concatenate([r[0] for r in results], axis=1)
    grads_far = jnp.concatenate([r[1] for r in results], axis=1)

    nt = (((1,), (1,)), ((), ()))
    with jax.named_scope("input_grad"):
        terms = lax.dot_general(grads_near, w_near, nt, preferred_element_type=f32) + lax.dot_general(
            grads_far, w_far, nt, preferred_element_type=f32
        )
        terms = terms.reshape(spread // cores, cores, tok, width)
        core = lax.axis_index("rep")
        theirs = lax.dynamic_index_in_dim(terms, 1 - core, 1, keepdims=False).astype(bf16)
        ours = lax.dynamic_index_in_dim(terms, core, 1, keepdims=False)
        summed = (ours + exchange(theirs, "rep", cores).astype(f32)).astype(bf16)
        side = lax.axis_index("hid")
        first = lax.ppermute(lax.dynamic_index_in_dim(summed, side, 0, keepdims=False), trio, straight_back)
        second = lax.ppermute(
            lax.dynamic_index_in_dim(summed, (side + 1) % across, 0, keepdims=False), trio, crossed_back
        )
        input_grad = (first.astype(f32) + second.astype(f32)).astype(bf16)

    with jax.named_scope("weight_grad"):
        tn = (((0,), (0,)), ((), ()))
        left = jnp.where(near_left, grads_near, grads_far)
        right = jnp.where(near_left, grads_far, grads_near)
        merge = lambda lo, hi: jnp.concatenate([left[:, lo:hi], right[:, lo:hi]], axis=1)
        query_out = lax.dot_general(rows_all, merge(2 * DH, 2 * DH + half_q), tn, preferred_element_type=f32)
        key_out = lax.dot_general(rows_all, merge(0, DH), tn, preferred_element_type=f32)
        value_out = lax.dot_general(rows_all, merge(DH, 2 * DH), tn, preferred_element_type=f32)
    return (input_grad, query_out, key_out, value_out)


def solution(mesh):
    in_specs = (
        P(("groups", "srv"), ("hid", "rep")),
        P("srv", ("hid", "rep")),
        P("srv", ("hid", "rep")),
        P("srv", ("hid", "rep")),
        P(("groups", "srv"), ("hid", "rep")),
        P("groups"),
    )
    out_specs = (
        P(("groups", "srv"), ("hid", "rep")),
        P(("groups", "srv"), ("hid", "rep")),
        P(("groups", "srv"), ("hid", "rep")),
        P(("groups", "srv"), ("hid", "rep")),
    )
    sizes = (mesh.shape["srv"], mesh.shape["hid"], mesh.shape["rep"])
    split = HK // (sizes[1] * sizes[2])
    fits = sizes[0] == sizes[1] * sizes[2] and sizes[1] == 2 and sizes[2] == 2 and split == 2
    chosen = functools.partial(stationary_body, sizes) if fits else body
    return jax.shard_map(chosen, mesh=mesh, in_specs=in_specs, out_specs=out_specs, check_vma=False)
```

```python
import functools

import jax
import jax.numpy as jnp
from jax import lax
from jax.experimental import pallas as pl
from jax.experimental.pallas import tpu as pltpu
from jax.sharding import PartitionSpec as P

HQ = 32
HK = 8
DH = 128
BLOCK = 128


NEGATIVE = -1e30


def attend(queries, cotangent, keys_all, values_all, doc_ids, block_id, carried):
    row_count = queries.shape[0]
    factor_scale = queries.shape[-1] ** (-0.5)
    offsets = jnp.arange(row_count, dtype=jnp.int32)
    query_pos = block_id * row_count + offsets
    query_doc = lax.dynamic_slice_in_dim(doc_ids, block_id * row_count, row_count)
    doc_start = jnp.sum((doc_ids < query_doc[0]).astype(jnp.int32))
    lowest = doc_start // row_count
    highest = jnp.where(True, block_id + 1, lowest)

    def scores_at(key_block):
        key_rows = lax.dynamic_slice_in_dim(keys_all, key_block * row_count, row_count, 0)
        value_rows = lax.dynamic_slice_in_dim(values_all, key_block * row_count, row_count, 0)
        key_doc = lax.dynamic_slice_in_dim(doc_ids, key_block * row_count, row_count)
        key_pos = key_block * row_count + offsets
        allowed = (key_doc[None, :] == query_doc[:, None]) & (
            key_pos[None, :] <= query_pos[:, None]
        )
        logits = (
            jnp.einsum("qgnd,kgd->gnqk", queries, key_rows, preferred_element_type=jnp.float32)
            * factor_scale
        )
        logits = jnp.where(allowed, logits, NEGATIVE)
        slopes = jnp.einsum(
            "qgnd,kgd->gnqk", cotangent, value_rows, preferred_element_type=jnp.float32
        )
        return (key_rows, allowed, logits, slopes)

    def first_pass(key_block, loop_state):
        row_peak, row_total, row_inner = loop_state
        key_rows, allowed, logits, slopes = scores_at(key_block)
        new_peak = jnp.maximum(row_peak, jnp.max(logits, axis=-1))
        weights = jnp.where(allowed, jnp.exp(logits - new_peak[..., None]), 0.0)
        factor = jnp.exp(row_peak - new_peak)
        row_total = row_total * factor + jnp.sum(weights, axis=-1)
        row_inner = row_inner * factor + jnp.sum(weights * slopes, axis=-1)
        return (new_peak, row_total, row_inner)

    stat_shape = (queries.shape[1], queries.shape[2], row_count)
    initial = (
        jnp.full(stat_shape, NEGATIVE, jnp.float32),
        jnp.zeros(stat_shape, jnp.float32),
        jnp.zeros(stat_shape, jnp.float32),
    )
    row_peak, row_total, row_inner = lax.fori_loop(lowest, highest, first_pass, initial)
    safe_total = jnp.where(True, row_total, 1.0)
    row_delta = row_inner / safe_total
    log_total = row_peak + jnp.log(safe_total)

    def second_pass(key_block, loop_state):
        query_grad, key_accum, value_accum = loop_state
        key_rows, allowed, logits, slopes = scores_at(key_block)
        attention = jnp.where(allowed, jnp.exp(logits - log_total[..., None]), 0.0)
        score_grad = (attention * (slopes - row_delta[..., None]) * factor_scale).astype(
            jnp.bfloat16
        )
        value_part = jnp.einsum(
            "gnqk,qgnd->kgd",
            attention.astype(jnp.bfloat16),
            cotangent,
            preferred_element_type=jnp.float32,
        )
        key_part = jnp.einsum(
            "gnqk,qgnd->kgd", score_grad, queries, preferred_element_type=jnp.float32
        )
        query_grad = query_grad + jnp.einsum(
            "gnqk,kgd->qgnd", score_grad, key_rows, preferred_element_type=jnp.float32
        )
        first_row = key_block * row_count
        key_accum = lax.dynamic_update_slice_in_dim(
            key_accum,
            lax.dynamic_slice_in_dim(key_accum, first_row, row_count, 0) + key_part,
            first_row,
            0,
        )
        value_accum = lax.dynamic_update_slice_in_dim(
            value_accum,
            lax.dynamic_slice_in_dim(value_accum, first_row, row_count, 0) + value_part,
            first_row,
            0,
        )
        return (query_grad, key_accum, value_accum)

    start_grad = jnp.zeros(queries.shape, jnp.float32)
    query_grad, key_accum, value_accum = lax.fori_loop(
        lowest, highest, second_pass, (start_grad, carried[0], carried[1])
    )
    return (query_grad, (key_accum, value_accum))


def body(layer_input, query_weight, key_weight, value_weight, out_grad, doc_ids):
    tok_rows = layer_input.shape[0]
    query_width = query_weight.shape[1]
    pair_width = key_weight.shape[1]
    key_heads = pair_width // DH
    group_size = HQ // HK
    block_count = tok_rows // BLOCK
    owner_id = lax.axis_index("srv")
    weights_all = lax.all_gather(
        jnp.concatenate([query_weight, key_weight, value_weight], axis=1), "srv", axis=0, tiled=True
    )
    inputs_all = lax.all_gather(layer_input, ("hid", "rep"), axis=1, tiled=True)
    projected = jnp.dot(inputs_all, weights_all, preferred_element_type=jnp.float32).astype(
        jnp.bfloat16
    )
    queries = projected[:, :query_width].reshape(block_count, BLOCK, key_heads, group_size, DH)
    keys_local = projected[:, query_width : query_width + pair_width]
    values_local = projected[:, query_width + pair_width :]
    keys_all, values_all = (
        lax.all_gather(keys_local, "srv", axis=0, tiled=True),
        lax.all_gather(values_local, "srv", axis=0, tiled=True),
    )
    total_rows = keys_all.shape[0]
    keys_all = keys_all.reshape(total_rows, key_heads, DH)
    values_all = values_all.reshape(total_rows, key_heads, DH)
    cotangent = out_grad.reshape(block_count, BLOCK, key_heads, group_size, DH)
    empty_accum = jnp.zeros((total_rows, key_heads, DH), jnp.float32)

    def own_block(position, loop_state):
        answers, carried = loop_state
        grad_q, carried = attend(
            lax.dynamic_index_in_dim(queries, position, 0, keepdims=False),
            lax.dynamic_index_in_dim(cotangent, position, 0, keepdims=False),
            keys_all,
            values_all,
            doc_ids,
            owner_id * block_count + position,
            carried,
        )
        answers = lax.dynamic_update_index_in_dim(answers, grad_q.astype(jnp.bfloat16), position, 0)
        return (answers, carried)

    answers = jnp.zeros(queries.shape, jnp.bfloat16)
    answers, carried = lax.fori_loop(
        0, block_count, own_block, (answers, (empty_accum, empty_accum))
    )
    query_grad = answers.reshape(tok_rows, query_width)
    key_accum, value_accum = carried
    key_sum, value_sum = (
        lax.psum_scatter(key_accum, "srv", scatter_dimension=0, tiled=True),
        lax.psum_scatter(value_accum, "srv", scatter_dimension=0, tiled=True),
    )
    grads_all = jnp.concatenate(
        [
            query_grad,
            key_sum.astype(jnp.bfloat16).reshape(tok_rows, pair_width),
            value_sum.astype(jnp.bfloat16).reshape(tok_rows, pair_width),
        ],
        axis=1,
    )
    input_terms = lax.dot_general(
        grads_all, weights_all, (((1,), (1,)), ((), ())), preferred_element_type=jnp.float32
    )
    input_grad = lax.psum_scatter(
        input_terms, ("hid", "rep"), scatter_dimension=1, tiled=True
    ).astype(jnp.bfloat16)
    columns = lax.all_to_all(inputs_all, "srv", split_axis=1, concat_axis=0, tiled=True)
    weight_grad = lax.dot_general(
        columns,
        lax.all_gather(grads_all, "srv", axis=0, tiled=True),
        (((0,), (0,)), ((), ())),
        preferred_element_type=jnp.float32,
    )
    return (
        input_grad,
        weight_grad[:, :query_width],
        weight_grad[:, query_width : query_width + pair_width],
        weight_grad[:, query_width + pair_width :],
    )


CHUNKS = 8
LAG = 2


def swap(array, axis, size):
    return lax.ppermute(array, axis, [(i, (i + 1) % size) for i in range(size)])


def place_of(plane_ref, planes):
    plane = plane_ref[0]
    at_end = (plane == 0) | (plane == planes - 1)
    far = jnp.where(plane < planes // 2, 1, 0)
    return at_end, far


def stage_kernel(plane_ref, k_ref, v_ref, q_ref, *refs, planes, mode):
    out_ref = refs[-1]
    here = jnp.concatenate([k_ref[...], v_ref[...], q_ref[...]], axis=1)
    if mode == "send":
        out_ref[...] = here.astype(out_ref.dtype)
    elif mode == "pass":
        out_ref[...] = (here + refs[0][...].astype(jnp.float32)).astype(out_ref.dtype)
    else:
        at_end, _ = place_of(plane_ref, planes)
        both = here + refs[0][...].astype(jnp.float32)
        out_ref[...] = jnp.where(at_end, here, both).astype(out_ref.dtype)


def stage(plane, products, received, planes, size, mode, rows, halves):
    widths = [p.shape[1] // 2 for p in products]

    def index(i, p):
        at_end, far = place_of(p, planes)
        half = [far if h else 1 - far for h in halves]
        return jnp.where(at_end, rows[0], rows[1]), jnp.where(at_end, half[0], half[1])

    flat = lambda i, p: (0, 0)
    given = [] if received is None else [received]
    shape = (size, sum(widths))
    return pl.pallas_call(
        functools.partial(stage_kernel, planes=planes, mode=mode),
        grid_spec=pltpu.PrefetchScalarGridSpec(
            num_scalar_prefetch=1,
            grid=(1,),
            in_specs=[pl.BlockSpec((size, w), index) for w in widths] + [pl.BlockSpec(shape, flat) for _ in given],
            out_specs=pl.BlockSpec(shape, flat),
        ),
        out_shape=jax.ShapeDtypeStruct(shape, jnp.bfloat16),
        cost_estimate=pl.CostEstimate(flops=2 * shape[0] * shape[1], bytes_accessed=8 * shape[0] * shape[1], transcendentals=0),
    )(plane, *products, *given)


def finish_kernel(plane_ref, *refs, planes):
    per = (len(refs) - 1) // 4
    out_ref = refs[-1]
    for i in range(per):
        k_ref, v_ref, q_ref, r_ref = refs[4 * i : 4 * i + 4]
        size = r_ref.shape[0]
        here = jnp.concatenate([k_ref[...], v_ref[...], q_ref[...]], axis=1)
        out_ref[i * size : (i + 1) * size, :] = (here + r_ref[...].astype(jnp.float32)).astype(out_ref.dtype)


def finish(plane, pieces, planes, size):
    flat = lambda i, p: (0, 0)
    specs, operands = [], []
    for row, products, received in pieces:
        for p in products:
            specs.append(
                pl.BlockSpec((size, p.shape[1] // 2), lambda i, p, row=row: (row, 1 - place_of(p, planes)[1]))
            )
            operands.append(p)
        specs.append(pl.BlockSpec(received.shape, flat))
        operands.append(received)
    shape = (size * len(pieces), pieces[0][2].shape[1])
    return pl.pallas_call(
        functools.partial(finish_kernel, planes=planes),
        grid_spec=pltpu.PrefetchScalarGridSpec(
            num_scalar_prefetch=1, grid=(1,), in_specs=specs, out_specs=pl.BlockSpec(shape, flat)
        ),
        out_shape=jax.ShapeDtypeStruct(shape, jnp.bfloat16),
        cost_estimate=pl.CostEstimate(flops=2 * shape[0] * shape[1], bytes_accessed=8 * shape[0] * shape[1], transcendentals=0),
    )(plane, *operands)


def terms_kernel(plane_ref, local_ref, one_ref, two_ref, three_ref, wq_ref, wk_ref, wv_ref, *refs, planes):
    gq_ref, gk_ref, gv_ref, out_ref = refs[-4:]
    at_end, far = place_of(plane_ref, planes)
    near_grads = jnp.where(at_end, local_ref[...], one_ref[...])
    far_grads = jnp.where(at_end, three_ref[...], two_ref[...])
    left = jnp.where(far == 1, near_grads, far_grads)
    right = jnp.where(far == 1, far_grads, near_grads)
    nt = (((1,), (1,)), ((), ()))
    total = None
    for low, high, w_ref, g_ref in ((0, DH, wk_ref, gk_ref), (DH, 2 * DH, wv_ref, gv_ref), (2 * DH, left.shape[1], wq_ref, gq_ref)):
        grads = jnp.concatenate([left[:, low:high], right[:, low:high]], axis=1)
        g_ref[...] = grads
        part = lax.dot_general(grads, w_ref[...], nt, preferred_element_type=jnp.float32)
        total = part if total is None else total + part
    out_ref[...] = total


def terms_of(plane, arrays, weights, grads, block_id, total, planes):
    block = arrays[0].shape[0]
    width = weights[0].shape[0]
    flat = lambda i, p: (0, 0)
    here = lambda i, p: (block_id, 0)
    whole = lambda a: pl.BlockSpec(a.shape, flat)
    shapes = [jax.ShapeDtypeStruct((total, w.shape[1]), jnp.bfloat16) for w in weights]
    held = [] if grads is None else list(grads)
    results = pl.pallas_call(
        functools.partial(terms_kernel, planes=planes),
        grid_spec=pltpu.PrefetchScalarGridSpec(
            num_scalar_prefetch=1,
            grid=(1,),
            in_specs=[whole(a) for a in arrays] + [whole(w) for w in weights] + [pl.BlockSpec(memory_space=pl.ANY) for _ in held],
            out_specs=[pl.BlockSpec((block, s.shape[1]), here) for s in shapes] + [pl.BlockSpec((block, width), flat)],
        ),
        out_shape=shapes + [jax.ShapeDtypeStruct((block, width), jnp.float32)],
        input_output_aliases={1 + len(arrays) + len(weights) + i: i for i in range(len(held))},
        cost_estimate=pl.CostEstimate(
            flops=2 * block * width * sum(s.shape[1] for s in shapes), bytes_accessed=6 * width * width, transcendentals=0
        ),
    )(plane, *arrays, *weights, *held)
    return results[:3], results[3]


def attention_kernel(*refs, back, heads, fresh, block_id):
    count = back + 1
    active_ref, doc_row_ref, doc_col_ref, g_ref = refs[:4]
    rows_refs = refs[4 : 4 + count]
    sum_refs = refs[4 + count : 4 + count + (count - fresh)]
    out_ref = refs[4 + count + (count - fresh)]
    left_refs = refs[5 + count + (count - fresh) :]
    block = g_ref.shape[0]
    scale = DH ** (-0.5)
    nt = (((1,), (1,)), ((), ()))
    first = block_id * block
    low = first - back * block

    @pl.when(active_ref[0] != 0)
    def _():
        query_doc = doc_row_ref[:, first : first + block]
        query_pos = lax.broadcasted_iota(jnp.int32, (block, block), 1)
        key_pos = lax.broadcasted_iota(jnp.int32, (block, block), 0)
        allowed = []
        for j in range(count):
            same = doc_col_ref[low + j * block : low + (j + 1) * block, :] == query_doc
            allowed.append(same & (key_pos <= query_pos) if j == back else same)
        dk = [None] * count
        dv = [None] * count
        for h in range(heads):
            at = (2 + h) * DH
            q = rows_refs[back][:, at : at + DH]
            g = g_ref[:, h * DH : (h + 1) * DH]
            logits, slopes = [], []
            for j in range(count):
                k, v = rows_refs[j][:, :DH], rows_refs[j][:, DH : 2 * DH]
                term = lax.dot_general(k, q, nt, preferred_element_type=jnp.float32) * scale
                logits.append(jnp.where(allowed[j], term, NEGATIVE))
                slopes.append(lax.dot_general(v, g, nt, preferred_element_type=jnp.float32))
            peak = functools.reduce(jnp.maximum, [jnp.max(t, axis=0, keepdims=True) for t in logits])
            weights = [jnp.exp(t - peak) for t in logits]
            total = functools.reduce(jnp.add, [jnp.sum(w, axis=0, keepdims=True) for w in weights])
            inner = functools.reduce(jnp.add, [jnp.sum(w * s, axis=0, keepdims=True) for w, s in zip(weights, slopes)])
            inverse = 1.0 / total
            inner = inner * inverse
            dq = None
            for j in range(count):
                attention = weights[j] * inverse
                score = (attention * (slopes[j] - inner) * scale).astype(jnp.bfloat16)
                value_part = jnp.dot(attention.astype(jnp.bfloat16), g, preferred_element_type=jnp.float32)
                key_part = jnp.dot(score, q, preferred_element_type=jnp.float32)
                dv[j] = value_part if dv[j] is None else dv[j] + value_part
                dk[j] = key_part if dk[j] is None else dk[j] + key_part
                part = lax.dot_general(
                    score, rows_refs[j][:, :DH], (((0,), (0,)), ((), ())), preferred_element_type=jnp.float32
                )
                dq = part if dq is None else dq + part
            out_ref[:, at : at + DH] = dq.astype(out_ref.dtype)
        for j in range(count):
            if j >= fresh:
                dk[j] = dk[j] + sum_refs[j - fresh][:, :DH]
                dv[j] = dv[j] + sum_refs[j - fresh][:, DH:]
            if j == back:
                out_ref[:, :DH] = dk[j].astype(out_ref.dtype)
                out_ref[:, DH : 2 * DH] = dv[j].astype(out_ref.dtype)
            else:
                left_refs[j][:, :DH] = dk[j]
                left_refs[j][:, DH:] = dv[j]


def attend_block(active, doc_row, doc_col, g_all, rows, sums, block_id, reach, blocks):
    block = rows[block_id].shape[0]
    heads = g_all.shape[1] // DH
    back = min(reach, block_id)
    low = block_id - back
    held = [sums[j] for j in range(low, block_id + 1) if sums[j] is not None]
    fresh = back + 1 - len(held)
    whole = lambda a: pl.BlockSpec(a.shape, lambda i, s: (0, 0))
    operands = [rows[j] for j in range(low, block_id + 1)] + held
    sum_shape = jax.ShapeDtypeStruct((block, 2 * DH), jnp.float32)
    outs = [jax.ShapeDtypeStruct(rows[block_id].shape, jnp.bfloat16)] + [sum_shape] * back
    results = pl.pallas_call(
        functools.partial(attention_kernel, back=back, heads=heads, fresh=fresh, block_id=block_id),
        grid_spec=pltpu.PrefetchScalarGridSpec(
            num_scalar_prefetch=1,
            grid=(1,),
            in_specs=[whole(doc_row), whole(doc_col), pl.BlockSpec((block, heads * DH), lambda i, s: (block_id, 0))]
            + [whole(a) for a in operands],
            out_specs=[whole(a) for a in outs],
        ),
        out_shape=outs,
        cost_estimate=pl.CostEstimate(
            flops=10 * heads * DH * block * block * (back + 1), bytes_accessed=3 * block * 8 * DH, transcendentals=heads * block * block * 3
        ),
    )(active, doc_row, doc_col, g_all, *operands)
    for j in range(back):
        sums[low + j] = results[1 + j]
    return results[0]


def stationary_body(sizes, layer_input, query_weight, key_weight, value_weight, out_grad, doc_ids):
    planes, across, cores = sizes
    spread = across * cores
    f32, bf16 = jnp.float32, jnp.bfloat16
    tok, width = layer_input.shape
    total = tok * planes
    half_q, half_k = query_weight.shape[1] // 2, key_weight.shape[1] // 2
    plane = lax.axis_index("srv")
    side, core = lax.axis_index("hid"), lax.axis_index("rep")
    column = side * cores + core
    last = planes - 1
    near_left = plane < planes // 2
    is_end = (plane == 0) | (plane == last)
    trio = ("srv", "hid", "rep")
    pairs = [(t, f) for t in range(planes) for f in range(spread)]
    straight = [(t * spread + f, f * spread + t) for t, f in pairs]
    crossed = [(t * spread + f, (f + cores) % spread * spread + t) for t, f in pairs]
    outer = [(0, 1), (1, 0), (2, 3), (3, 2)]
    inner = [(0, 0), (1, 2), (2, 1), (3, 3)]

    with jax.named_scope("inputs"):
        part_rows = tok // across
        mine = lax.dynamic_slice_in_dim(layer_input, side * part_rows, part_rows, 0)
        other = lax.dynamic_slice_in_dim(layer_input, (1 - side) * part_rows, part_rows, 0)
        direct = lax.ppermute(mine, trio, straight)
        relayed = lax.ppermute(swap(other, "hid", across), trio, crossed)
        home = plane // cores
        rows_all = jnp.zeros((total, width), bf16)
        for block, half in ((direct, home), (relayed, 1 - home)):
            turned = swap(block, "hid", across)
            mate = column + cores - 2 * cores * side
            for piece, owner in (
                (block, column),
                (turned, mate),
                (swap(block, "rep", cores), column + 1 - 2 * core),
                (swap(turned, "rep", cores), mate + 1 - 2 * core),
            ):
                rows_all = lax.dynamic_update_slice_in_dim(rows_all, piece, owner * tok + half * part_rows, 0)

    far_at, near_at = jnp.where(near_left, 1, 0), jnp.where(near_left, 0, 1)

    def part(array, at, size):
        return lax.dynamic_slice_in_dim(array, at * size, size, 1)

    with jax.named_scope("cotangent"):
        g_near, g_far, _ = lax.optimization_barrier((part(out_grad, near_at, half_q), part(out_grad, far_at, half_q), relayed))
        place = lambda d: jnp.where(plane == 0, d, last - d) * tok
        g_all = lax.dynamic_update_slice_in_dim(jnp.zeros((total, half_q), bf16), g_near, place(0), 0)
        for d in range(1, planes):
            arrived = lax.ppermute(g_near if d < planes // 2 else g_far, "srv", [(d, 0), (last - d, last)])
            g_all = lax.dynamic_update_slice_in_dim(g_all, arrived, place(d), 0)

    size = total // CHUNKS
    order = list(range(CHUNKS - 1, -1, -1))
    position = plane.astype(jnp.int32).reshape(1)
    blocks = total // tok
    per = CHUNKS // blocks
    weights = (query_weight, key_weight, value_weight)
    with jax.named_scope("chain"):
        products = [jnp.dot(rows_all, w, preferred_element_type=f32) for w in (key_weight, value_weight, query_weight)]
        via_outer, via_inner, rows = {}, {}, {}
        for k in range(CHUNKS + 2 * LAG):
            j = k - 2 * LAG
            if j < 0:
                payload = stage(position, products, None, planes, size, "send", (order[k],) * 2, (1, 1))
            elif k < CHUNKS:
                payload = stage(position, products, via_inner[j], planes, size, "both", (order[k], order[j]), (1, 0))
            else:
                payload = stage(position, products, via_inner[j], planes, size, "pass", (order[j],) * 2, (0, 0))
            via_outer[k] = lax.ppermute(payload, "srv", outer)
            j = k - LAG
            if 0 <= j < CHUNKS:
                payload = stage(position, products, via_outer[j], planes, size, "pass", (order[j],) * 2, (1, 1))
                via_inner[j] = lax.ppermute(payload, "srv", inner)
            j = k - 2 * LAG
            if j >= 0:
                rows[order[j]] = via_outer[k]
        merged = [finish(position, [(b * per + i, products, rows[b * per + i]) for i in range(per)], planes, size) for b in range(blocks)]

    active = is_end.astype(jnp.int32).reshape(1)
    doc_row, doc_col = doc_ids.reshape(1, total), doc_ids.reshape(total, 1)
    with jax.named_scope("attend"):
        sums = [None] * blocks
        local = {}
        for b in range(blocks - 1, -1, -1):
            local[blocks - 1 - b] = attend_block(active, doc_row, doc_col, g_all, merged, sums, b, total // 2 // tok, blocks)
    terms, grads = {}, None
    with jax.named_scope("back"):
        first, second = {}, {}
        for k in range(blocks + 2):
            j = k - 2
            if j < 0:
                payload = local[k]
            elif k < blocks:
                payload = jnp.where(is_end, local[k], second[j])
            else:
                payload = second[j]
            first[k] = lax.ppermute(payload, "srv", outer)
            j = k - 1
            if 0 <= j < blocks:
                second[j] = lax.ppermute(first[j], "srv", inner)
            j = k - 2
            if j >= 0:
                b = blocks - 1 - j
                grads, terms[b] = terms_of(
                    position, (local[j], first[j], second[j], first[k]), weights, grads, b, total, planes
                )

    with jax.named_scope("input_grad"):
        summed = []
        for i in range(blocks // cores):
            even, odd = terms[cores * i], terms[cores * i + 1]
            theirs = jnp.where(core == 0, odd, even).astype(bf16)
            ours = jnp.where(core == 0, even, odd)
            summed.append((ours + swap(theirs, "rep", cores).astype(f32)).astype(bf16))
        one = jnp.where(side == 0, summed[0], summed[1])
        two = jnp.where(side == 0, summed[1], summed[0])
        one = lax.ppermute(one, trio, straight)
        two = lax.ppermute(two, trio, crossed)
        input_grad = (one.astype(f32) + two.astype(f32)).astype(bf16)

    with jax.named_scope("weight_grad"):
        tn = (((0,), (0,)), ((), ()))
        query_out, key_out, value_out = [
            lax.dot_general(rows_all, g, tn, preferred_element_type=f32) for g in grads
        ]
    return (input_grad, query_out, key_out, value_out)


def solution(mesh):
    in_specs = (
        P(("groups", "srv"), ("hid", "rep")),
        P("srv", ("hid", "rep")),
        P("srv", ("hid", "rep")),
        P("srv", ("hid", "rep")),
        P(("groups", "srv"), ("hid", "rep")),
        P("groups"),
    )
    out_specs = (
        P(("groups", "srv"), ("hid", "rep")),
        P(("groups", "srv"), ("hid", "rep")),
        P(("groups", "srv"), ("hid", "rep")),
        P(("groups", "srv"), ("hid", "rep")),
    )
    sizes = (mesh.shape["srv"], mesh.shape["hid"], mesh.shape["rep"])
    split = HK // (sizes[1] * sizes[2])
    fits = sizes[0] == sizes[1] * sizes[2] and sizes[1] == 2 and sizes[2] == 2 and split == 2
    chosen = functools.partial(stationary_body, sizes) if fits else body
    return jax.shard_map(chosen, mesh=mesh, in_specs=in_specs, out_specs=out_specs, check_vma=False)
```

```python
import functools

import jax
import jax.numpy as jnp
from jax import lax
from jax.experimental import pallas as pl
from jax.experimental.pallas import tpu as pltpu
from jax.sharding import PartitionSpec as P


HQ = 32
HK = 8
DH = 128
BLOCK = 128


NEGATIVE = -1e30


def attend(queries, cotangent, keys_all, values_all, doc_ids, block_id, carried):
    row_count = queries.shape[0]
    factor_scale = queries.shape[-1] ** (-0.5)
    offsets = jnp.arange(row_count, dtype=jnp.int32)
    query_pos = block_id * row_count + offsets
    query_doc = lax.dynamic_slice_in_dim(doc_ids, block_id * row_count, row_count)
    doc_start = jnp.sum((doc_ids < query_doc[0]).astype(jnp.int32))
    lowest = doc_start // row_count
    highest = jnp.where(True, block_id + 1, lowest)

    def scores_at(key_block):
        key_rows = lax.dynamic_slice_in_dim(keys_all, key_block * row_count, row_count, 0)
        value_rows = lax.dynamic_slice_in_dim(values_all, key_block * row_count, row_count, 0)
        key_doc = lax.dynamic_slice_in_dim(doc_ids, key_block * row_count, row_count)
        key_pos = key_block * row_count + offsets
        allowed = (key_doc[None, :] == query_doc[:, None]) & (
            key_pos[None, :] <= query_pos[:, None]
        )
        logits = (
            jnp.einsum("qgnd,kgd->gnqk", queries, key_rows, preferred_element_type=jnp.float32)
            * factor_scale
        )
        logits = jnp.where(allowed, logits, NEGATIVE)
        slopes = jnp.einsum(
            "qgnd,kgd->gnqk", cotangent, value_rows, preferred_element_type=jnp.float32
        )
        return (key_rows, allowed, logits, slopes)

    def first_pass(key_block, loop_state):
        row_peak, row_total, row_inner = loop_state
        _, allowed, logits, slopes = scores_at(key_block)
        new_peak = jnp.maximum(row_peak, jnp.max(logits, axis=-1))
        weights = jnp.where(allowed, jnp.exp(logits - new_peak[..., None]), 0.0)
        factor = jnp.exp(row_peak - new_peak)
        row_total = row_total * factor + jnp.sum(weights, axis=-1)
        row_inner = row_inner * factor + jnp.sum(weights * slopes, axis=-1)
        return (new_peak, row_total, row_inner)

    stat_shape = (queries.shape[1], queries.shape[2], row_count)
    initial = (
        jnp.full(stat_shape, NEGATIVE, jnp.float32),
        jnp.zeros(stat_shape, jnp.float32),
        jnp.zeros(stat_shape, jnp.float32),
    )
    row_peak, row_total, row_inner = lax.fori_loop(lowest, highest, first_pass, initial)
    safe_total = jnp.where(True, row_total, 1.0)
    row_delta = row_inner / safe_total
    log_total = row_peak + jnp.log(safe_total)

    def second_pass(key_block, loop_state):
        query_grad, key_accum, value_accum = loop_state
        key_rows, allowed, logits, slopes = scores_at(key_block)
        attention = jnp.where(allowed, jnp.exp(logits - log_total[..., None]), 0.0)
        score_grad = (attention * (slopes - row_delta[..., None]) * factor_scale).astype(
            jnp.bfloat16
        )
        value_part = jnp.einsum(
            "gnqk,qgnd->kgd",
            attention.astype(jnp.bfloat16),
            cotangent,
            preferred_element_type=jnp.float32,
        )
        key_part = jnp.einsum(
            "gnqk,qgnd->kgd", score_grad, queries, preferred_element_type=jnp.float32
        )
        query_grad = query_grad + jnp.einsum(
            "gnqk,kgd->qgnd", score_grad, key_rows, preferred_element_type=jnp.float32
        )
        first_row = key_block * row_count
        key_accum = lax.dynamic_update_slice_in_dim(
            key_accum,
            lax.dynamic_slice_in_dim(key_accum, first_row, row_count, 0) + key_part,
            first_row,
            0,
        )
        value_accum = lax.dynamic_update_slice_in_dim(
            value_accum,
            lax.dynamic_slice_in_dim(value_accum, first_row, row_count, 0) + value_part,
            first_row,
            0,
        )
        return (query_grad, key_accum, value_accum)

    start_grad = jnp.zeros(queries.shape, jnp.float32)
    query_grad, key_accum, value_accum = lax.fori_loop(
        lowest, highest, second_pass, (start_grad, carried[0], carried[1])
    )
    return (query_grad, (key_accum, value_accum))


def body(layer_input, query_weight, key_weight, value_weight, out_grad, doc_ids):
    tok_rows = layer_input.shape[0]
    query_width = query_weight.shape[1]
    pair_width = key_weight.shape[1]
    key_heads = pair_width // DH
    group_size = HQ // HK
    block_count = tok_rows // BLOCK
    owner_id = lax.axis_index("srv")
    weights_all = lax.all_gather(
        jnp.concatenate([query_weight, key_weight, value_weight], axis=1), "srv", axis=0, tiled=True
    )
    inputs_all = lax.all_gather(layer_input, ("hid", "rep"), axis=1, tiled=True)
    projected = jnp.dot(inputs_all, weights_all, preferred_element_type=jnp.float32).astype(
        jnp.bfloat16
    )
    queries = projected[:, :query_width].reshape(block_count, BLOCK, key_heads, group_size, DH)
    keys_local = projected[:, query_width : query_width + pair_width]
    values_local = projected[:, query_width + pair_width :]
    keys_all, values_all = (
        lax.all_gather(keys_local, "srv", axis=0, tiled=True),
        lax.all_gather(values_local, "srv", axis=0, tiled=True),
    )
    total_rows = keys_all.shape[0]
    keys_all = keys_all.reshape(total_rows, key_heads, DH)
    values_all = values_all.reshape(total_rows, key_heads, DH)
    cotangent = out_grad.reshape(block_count, BLOCK, key_heads, group_size, DH)
    empty_accum = jnp.zeros((total_rows, key_heads, DH), jnp.float32)

    def own_block(position, loop_state):
        answers, carried = loop_state
        grad_q, carried = attend(
            lax.dynamic_index_in_dim(queries, position, 0, keepdims=False),
            lax.dynamic_index_in_dim(cotangent, position, 0, keepdims=False),
            keys_all,
            values_all,
            doc_ids,
            owner_id * block_count + position,
            carried,
        )
        answers = lax.dynamic_update_index_in_dim(answers, grad_q.astype(jnp.bfloat16), position, 0)
        return (answers, carried)

    answers = jnp.zeros(queries.shape, jnp.bfloat16)
    answers, carried = lax.fori_loop(
        0, block_count, own_block, (answers, (empty_accum, empty_accum))
    )
    query_grad = answers.reshape(tok_rows, query_width)
    key_accum, value_accum = carried
    key_sum, value_sum = (
        lax.psum_scatter(key_accum, "srv", scatter_dimension=0, tiled=True),
        lax.psum_scatter(value_accum, "srv", scatter_dimension=0, tiled=True),
    )
    grads_all = jnp.concatenate(
        [
            query_grad,
            key_sum.astype(jnp.bfloat16).reshape(tok_rows, pair_width),
            value_sum.astype(jnp.bfloat16).reshape(tok_rows, pair_width),
        ],
        axis=1,
    )
    input_terms = lax.dot_general(
        grads_all, weights_all, (((1,), (1,)), ((), ())), preferred_element_type=jnp.float32
    )
    input_grad = lax.psum_scatter(
        input_terms, ("hid", "rep"), scatter_dimension=1, tiled=True
    ).astype(jnp.bfloat16)
    columns = lax.all_to_all(inputs_all, "srv", split_axis=1, concat_axis=0, tiled=True)
    weight_grad = lax.dot_general(
        columns,
        lax.all_gather(grads_all, "srv", axis=0, tiled=True),
        (((0,), (0,)), ((), ())),
        preferred_element_type=jnp.float32,
    )
    return (
        input_grad,
        weight_grad[:, :query_width],
        weight_grad[:, query_width : query_width + pair_width],
        weight_grad[:, query_width + pair_width :],
    )


def swap(array, axis, size):
    return lax.ppermute(array, axis, [(i, (i + 1) % size) for i in range(size)])


def attention_kernel(*refs, back, heads, fresh, block_id):
    count = back + 1
    active_ref, doc_row_ref, doc_col_ref, g_ref = refs[:4]
    rows_refs = refs[4 : 4 + count]
    sum_refs = refs[4 + count : 4 + count + (count - fresh)]
    out_ref = refs[4 + count + (count - fresh)]
    left_refs = refs[5 + count + (count - fresh) :]
    block = g_ref.shape[0]
    scale = DH ** (-0.5)
    nt = (((1,), (1,)), ((), ()))
    first = block_id * block
    low = first - back * block

    @pl.when(active_ref[0] != 0)
    def _():
        query_doc = doc_row_ref[:, first : first + block]
        query_pos = lax.broadcasted_iota(jnp.int32, (block, block), 1)
        key_pos = lax.broadcasted_iota(jnp.int32, (block, block), 0)
        allowed = []
        for j in range(count):
            same = doc_col_ref[low + j * block : low + (j + 1) * block, :] == query_doc
            allowed.append(same & (key_pos <= query_pos) if j == back else same)
        dk = [None] * count
        dv = [None] * count
        for h in range(heads):
            at = (2 + h) * DH
            q = rows_refs[back][:, at : at + DH]
            g = g_ref[:, h * DH : (h + 1) * DH]
            logits, slopes = [], []
            for j in range(count):
                k, v = rows_refs[j][:, :DH], rows_refs[j][:, DH : 2 * DH]
                term = lax.dot_general(k, q, nt, preferred_element_type=jnp.float32) * scale
                logits.append(jnp.where(allowed[j], term, NEGATIVE))
                slopes.append(lax.dot_general(v, g, nt, preferred_element_type=jnp.float32))
            peak = functools.reduce(jnp.maximum, [jnp.max(t, axis=0, keepdims=True) for t in logits])
            weights = [jnp.exp(t - peak) for t in logits]
            total = functools.reduce(jnp.add, [jnp.sum(w, axis=0, keepdims=True) for w in weights])
            inner = functools.reduce(jnp.add, [jnp.sum(w * s, axis=0, keepdims=True) for w, s in zip(weights, slopes)])
            inverse = 1.0 / total
            inner = inner * inverse
            dq = None
            for j in range(count):
                attention = weights[j] * inverse
                score = (attention * (slopes[j] - inner) * scale).astype(jnp.bfloat16)
                value_part = jnp.dot(attention.astype(jnp.bfloat16), g, preferred_element_type=jnp.float32)
                key_part = jnp.dot(score, q, preferred_element_type=jnp.float32)
                dv[j] = value_part if dv[j] is None else dv[j] + value_part
                dk[j] = key_part if dk[j] is None else dk[j] + key_part
                part = lax.dot_general(
                    score, rows_refs[j][:, :DH], (((0,), (0,)), ((), ())), preferred_element_type=jnp.float32
                )
                dq = part if dq is None else dq + part
            out_ref[:, at : at + DH] = dq.astype(out_ref.dtype)
        for j in range(count):
            if j >= fresh:
                dk[j] = dk[j] + sum_refs[j - fresh][:, :DH]
                dv[j] = dv[j] + sum_refs[j - fresh][:, DH:]
            if j == back:
                out_ref[:, :DH] = dk[j].astype(out_ref.dtype)
                out_ref[:, DH : 2 * DH] = dv[j].astype(out_ref.dtype)
            else:
                left_refs[j][:, :DH] = dk[j]
                left_refs[j][:, DH:] = dv[j]


def attend_block(active, doc_row, doc_col, g_all, rows, sums, block_id, reach):
    block = rows[block_id].shape[0]
    heads = g_all.shape[1] // DH
    back = min(reach, block_id)
    low = block_id - back
    held = [sums[j] for j in range(low, block_id + 1) if sums[j] is not None]
    fresh = back + 1 - len(held)
    whole = lambda a: pl.BlockSpec(a.shape, lambda i, s: (0, 0))
    operands = [rows[j] for j in range(low, block_id + 1)] + held
    sum_shape = jax.ShapeDtypeStruct((block, 2 * DH), jnp.float32)
    outs = [jax.ShapeDtypeStruct(rows[block_id].shape, jnp.bfloat16)] + [sum_shape] * back
    results = pl.pallas_call(
        functools.partial(attention_kernel, back=back, heads=heads, fresh=fresh, block_id=block_id),
        grid_spec=pltpu.PrefetchScalarGridSpec(
            num_scalar_prefetch=1,
            grid=(1,),
            in_specs=[whole(doc_row), whole(doc_col), pl.BlockSpec((block, heads * DH), lambda i, s: (block_id, 0))]
            + [whole(a) for a in operands],
            out_specs=[whole(a) for a in outs],
        ),
        out_shape=outs,
        cost_estimate=pl.CostEstimate(
            flops=10 * heads * DH * block * block * (back + 1), bytes_accessed=3 * block * 8 * DH, transcendentals=heads * block * block * 3
        ),
    )(active, doc_row, doc_col, g_all, *operands)
    for j in range(back):
        sums[low + j] = results[1 + j]
    return results[0]


def stationary_body(sizes, *arrays):
    return stationary(sizes, *arrays)


def stationary(sizes, layer_input, query_weight, key_weight, value_weight, out_grad, doc_ids):
    planes, across, cores = sizes
    spread = across * cores
    f32, bf16 = jnp.float32, jnp.bfloat16
    tok, width = layer_input.shape
    total = tok * planes
    half_q, half_k = query_weight.shape[1] // 2, key_weight.shape[1] // 2
    plane = lax.axis_index("srv")
    side, core = lax.axis_index("hid"), lax.axis_index("rep")
    last = planes - 1
    near_left = plane < planes // 2
    is_end = (plane == 0) | (plane == last)
    trio = ("srv", "hid", "rep")
    pairs = [(t, f) for t in range(planes) for f in range(spread)]
    straight = [(t * spread + f, f * spread + t) for t, f in pairs]
    crossed = [(t * spread + f, (f + cores) % spread * spread + t) for t, f in pairs]

    def climb(early):
        moves = []
        for t, f in pairs:
            x = f // cores
            target = f if (t < planes // 2) == early else (f + cores) % spread
            moves.append((t * spread + f, target * spread + x * cores + t % cores))
        return moves

    rise, fall = climb(True), climb(False)
    line = [[(k, k + 1), (last - k, last - k - 1)] for k in range(last)]

    part_rows = tok // across
    mine = lax.dynamic_slice_in_dim(layer_input, side * part_rows, part_rows, 0)
    other = lax.dynamic_slice_in_dim(layer_input, (1 - side) * part_rows, part_rows, 0)
    other = swap(other, "hid", across)
    low_plane = plane < planes // 2
    one = lax.ppermute(jnp.where(low_plane, mine, other), trio, rise)
    two = lax.ppermute(jnp.where(low_plane, other, mine), trio, fall)
    own_column = side == plane // cores
    low = jnp.where(own_column, one, two)
    high = jnp.where(own_column, two, one)
    held = jnp.concatenate([low, high], axis=0)
    turned = swap(held, "hid", across)
    first_half = jnp.where(side == 0, held, turned).reshape(across, part_rows, width)
    second_half = jnp.where(side == 0, turned, held).reshape(across, part_rows, width)
    pair = jnp.concatenate([first_half, second_half], axis=1)
    mate = swap(pair, "rep", cores)
    even = jnp.where(core == 0, pair, mate)
    odd = jnp.where(core == 0, mate, pair)
    x_rows = [(even if b % cores == 0 else odd)[b // cores] for b in range(planes)]

    far_at, near_at = jnp.where(near_left, 1, 0), jnp.where(near_left, 0, 1)

    def part(array, at, size):
        return lax.dynamic_slice_in_dim(array, at * size, size, 1)

    def gather_half(at):
        return jnp.concatenate([part(key_weight, at, half_k), part(value_weight, at, half_k), part(query_weight, at, half_q)], axis=1)

    w_near, w_far = gather_half(near_at), gather_half(far_at)

    g_near, g_far, _ = lax.optimization_barrier((part(out_grad, near_at, half_q), part(out_grad, far_at, half_q), other))
    g_pieces = [
        lax.ppermute(g_near if d < planes // 2 else g_far, "srv", [(d, 0), (last - d, last)]) for d in range(1, planes)
    ]

    blocks = planes
    merged = [None] * blocks
    for b in range(blocks - 1, -1, -1):
        far_part = jnp.dot(x_rows[b], w_far, preferred_element_type=f32)
        near_part = jnp.dot(x_rows[b], w_near, preferred_element_type=f32)
        moving = None
        for k in range(last):
            mine_now = far_part if k < planes // 2 else near_part
            if moving is not None:
                mine_now = mine_now + moving.astype(f32)
            moving = lax.ppermute(mine_now.astype(bf16), "srv", line[k])
        merged[b] = (near_part + moving.astype(f32)).astype(bf16)

    g_pieces = lax.optimization_barrier((*g_pieces, merged[blocks - 1]))[:-1]
    place = lambda d: jnp.where(plane == 0, d, last - d) * tok
    g_all = lax.dynamic_update_slice_in_dim(jnp.zeros((total, half_q), bf16), g_near, place(0), 0)
    for d in range(1, planes):
        g_all = lax.dynamic_update_slice_in_dim(g_all, g_pieces[d - 1], place(d), 0)
    active = is_end.astype(jnp.int32).reshape(1)
    doc_row, doc_col = doc_ids.reshape(1, total), doc_ids.reshape(total, 1)
    sums = [None] * blocks
    local = {}
    for b in range(blocks - 1, -1, -1):
        local[blocks - 1 - b] = attend_block(active, doc_row, doc_col, g_all, merged, sums, b, total // 2 // tok)
    near, far, terms = {}, {}, {}
    nt = (((1,), (1,)), ((), ()))
    for j in range(blocks):
        b = blocks - 1 - j
        hops = [local[j]]
        for k in range(last):
            hops.append(lax.ppermute(hops[k], "srv", line[k]))
        one_hop, two_hops, three_hops = hops[1:]
        near[b] = jnp.where(is_end, local[j], one_hop)
        far[b] = jnp.where(is_end, three_hops, two_hops)
        terms[b] = lax.dot_general(near[b], w_near, nt, preferred_element_type=f32) + lax.dot_general(
            far[b], w_far, nt, preferred_element_type=f32
        )

    summed = []
    for i in range(blocks // cores):
        even, odd = terms[cores * i], terms[cores * i + 1]
        theirs = jnp.where(core == 0, odd, even).astype(bf16)
        ours = jnp.where(core == 0, even, odd)
        summed.append((ours + swap(theirs, "rep", cores).astype(f32)).astype(bf16))
    one = jnp.where(side == 0, summed[0], summed[1])
    two = jnp.where(side == 0, summed[1], summed[0])
    one = lax.ppermute(one, trio, straight)
    two = lax.ppermute(two, trio, crossed)
    input_grad = (one.astype(f32) + two.astype(f32)).astype(bf16)

    tn = (((0,), (0,)), ((), ()))
    rows_all = jnp.concatenate(x_rows, axis=0)
    left = jnp.concatenate([jnp.where(near_left, near[b], far[b]) for b in range(blocks)], axis=0)
    right = jnp.concatenate([jnp.where(near_left, far[b], near[b]) for b in range(blocks)], axis=0)
    merge = lambda lo, hi: jnp.concatenate([left[:, lo:hi], right[:, lo:hi]], axis=1)
    query_out = lax.dot_general(rows_all, merge(2 * DH, 2 * DH + half_q), tn, preferred_element_type=f32)
    key_out = lax.dot_general(rows_all, merge(0, DH), tn, preferred_element_type=f32)
    value_out = lax.dot_general(rows_all, merge(DH, 2 * DH), tn, preferred_element_type=f32)
    return (input_grad, query_out, key_out, value_out)


def solution(mesh):
    in_specs = (
        P(("groups", "srv"), ("hid", "rep")),
        P("srv", ("hid", "rep")),
        P("srv", ("hid", "rep")),
        P("srv", ("hid", "rep")),
        P(("groups", "srv"), ("hid", "rep")),
        P("groups"),
    )
    out_specs = (
        P(("groups", "srv"), ("hid", "rep")),
        P(("groups", "srv"), ("hid", "rep")),
        P(("groups", "srv"), ("hid", "rep")),
        P(("groups", "srv"), ("hid", "rep")),
    )
    sizes = (mesh.shape["srv"], mesh.shape["hid"], mesh.shape["rep"])
    split = HK // (sizes[1] * sizes[2])
    fits = sizes[0] == sizes[1] * sizes[2] and sizes[1] == 2 and sizes[2] == 2 and split == 2
    chosen = functools.partial(stationary_body, sizes) if fits else body
    return jax.shard_map(chosen, mesh=mesh, in_specs=in_specs, out_specs=out_specs, check_vma=False)
```

```python
import functools

import jax
import jax.numpy as jnp
from jax import lax
from jax.experimental import pallas as pl
from jax.experimental.pallas import tpu as pltpu
from jax.sharding import PartitionSpec as P


HQ = 32
HK = 8
DH = 128
BLOCK = 128


NEGATIVE = -1e30


def attend(queries, cotangent, keys_all, values_all, doc_ids, block_id, carried):
    row_count = queries.shape[0]
    factor_scale = queries.shape[-1] ** (-0.5)
    offsets = jnp.arange(row_count, dtype=jnp.int32)
    query_pos = block_id * row_count + offsets
    query_doc = lax.dynamic_slice_in_dim(doc_ids, block_id * row_count, row_count)
    doc_start = jnp.sum((doc_ids < query_doc[0]).astype(jnp.int32))
    lowest = doc_start // row_count
    highest = jnp.where(True, block_id + 1, lowest)

    def scores_at(key_block):
        key_rows = lax.dynamic_slice_in_dim(keys_all, key_block * row_count, row_count, 0)
        value_rows = lax.dynamic_slice_in_dim(values_all, key_block * row_count, row_count, 0)
        key_doc = lax.dynamic_slice_in_dim(doc_ids, key_block * row_count, row_count)
        key_pos = key_block * row_count + offsets
        allowed = (key_doc[None, :] == query_doc[:, None]) & (
            key_pos[None, :] <= query_pos[:, None]
        )
        logits = (
            jnp.einsum("qgnd,kgd->gnqk", queries, key_rows, preferred_element_type=jnp.float32)
            * factor_scale
        )
        logits = jnp.where(allowed, logits, NEGATIVE)
        slopes = jnp.einsum(
            "qgnd,kgd->gnqk", cotangent, value_rows, preferred_element_type=jnp.float32
        )
        return (key_rows, allowed, logits, slopes)

    def first_pass(key_block, loop_state):
        row_peak, row_total, row_inner = loop_state
        _, allowed, logits, slopes = scores_at(key_block)
        new_peak = jnp.maximum(row_peak, jnp.max(logits, axis=-1))
        weights = jnp.where(allowed, jnp.exp(logits - new_peak[..., None]), 0.0)
        factor = jnp.exp(row_peak - new_peak)
        row_total = row_total * factor + jnp.sum(weights, axis=-1)
        row_inner = row_inner * factor + jnp.sum(weights * slopes, axis=-1)
        return (new_peak, row_total, row_inner)

    stat_shape = (queries.shape[1], queries.shape[2], row_count)
    initial = (
        jnp.full(stat_shape, NEGATIVE, jnp.float32),
        jnp.zeros(stat_shape, jnp.float32),
        jnp.zeros(stat_shape, jnp.float32),
    )
    row_peak, row_total, row_inner = lax.fori_loop(lowest, highest, first_pass, initial)
    safe_total = jnp.where(True, row_total, 1.0)
    row_delta = row_inner / safe_total
    log_total = row_peak + jnp.log(safe_total)

    def second_pass(key_block, loop_state):
        query_grad, key_accum, value_accum = loop_state
        key_rows, allowed, logits, slopes = scores_at(key_block)
        attention = jnp.where(allowed, jnp.exp(logits - log_total[..., None]), 0.0)
        score_grad = (attention * (slopes - row_delta[..., None]) * factor_scale).astype(
            jnp.bfloat16
        )
        value_part = jnp.einsum(
            "gnqk,qgnd->kgd",
            attention.astype(jnp.bfloat16),
            cotangent,
            preferred_element_type=jnp.float32,
        )
        key_part = jnp.einsum(
            "gnqk,qgnd->kgd", score_grad, queries, preferred_element_type=jnp.float32
        )
        query_grad = query_grad + jnp.einsum(
            "gnqk,kgd->qgnd", score_grad, key_rows, preferred_element_type=jnp.float32
        )
        first_row = key_block * row_count
        key_accum = lax.dynamic_update_slice_in_dim(
            key_accum,
            lax.dynamic_slice_in_dim(key_accum, first_row, row_count, 0) + key_part,
            first_row,
            0,
        )
        value_accum = lax.dynamic_update_slice_in_dim(
            value_accum,
            lax.dynamic_slice_in_dim(value_accum, first_row, row_count, 0) + value_part,
            first_row,
            0,
        )
        return (query_grad, key_accum, value_accum)

    start_grad = jnp.zeros(queries.shape, jnp.float32)
    query_grad, key_accum, value_accum = lax.fori_loop(
        lowest, highest, second_pass, (start_grad, carried[0], carried[1])
    )
    return (query_grad, (key_accum, value_accum))


def body(layer_input, query_weight, key_weight, value_weight, out_grad, doc_ids):
    tok_rows = layer_input.shape[0]
    query_width = query_weight.shape[1]
    pair_width = key_weight.shape[1]
    key_heads = pair_width // DH
    group_size = HQ // HK
    block_count = tok_rows // BLOCK
    owner_id = lax.axis_index("srv")
    weights_all = lax.all_gather(
        jnp.concatenate([query_weight, key_weight, value_weight], axis=1), "srv", axis=0, tiled=True
    )
    inputs_all = lax.all_gather(layer_input, ("hid", "rep"), axis=1, tiled=True)
    projected = jnp.dot(inputs_all, weights_all, preferred_element_type=jnp.float32).astype(
        jnp.bfloat16
    )
    queries = projected[:, :query_width].reshape(block_count, BLOCK, key_heads, group_size, DH)
    keys_local = projected[:, query_width : query_width + pair_width]
    values_local = projected[:, query_width + pair_width :]
    keys_all, values_all = (
        lax.all_gather(keys_local, "srv", axis=0, tiled=True),
        lax.all_gather(values_local, "srv", axis=0, tiled=True),
    )
    total_rows = keys_all.shape[0]
    keys_all = keys_all.reshape(total_rows, key_heads, DH)
    values_all = values_all.reshape(total_rows, key_heads, DH)
    cotangent = out_grad.reshape(block_count, BLOCK, key_heads, group_size, DH)
    empty_accum = jnp.zeros((total_rows, key_heads, DH), jnp.float32)

    def own_block(position, loop_state):
        answers, carried = loop_state
        grad_q, carried = attend(
            lax.dynamic_index_in_dim(queries, position, 0, keepdims=False),
            lax.dynamic_index_in_dim(cotangent, position, 0, keepdims=False),
            keys_all,
            values_all,
            doc_ids,
            owner_id * block_count + position,
            carried,
        )
        answers = lax.dynamic_update_index_in_dim(answers, grad_q.astype(jnp.bfloat16), position, 0)
        return (answers, carried)

    answers = jnp.zeros(queries.shape, jnp.bfloat16)
    answers, carried = lax.fori_loop(
        0, block_count, own_block, (answers, (empty_accum, empty_accum))
    )
    query_grad = answers.reshape(tok_rows, query_width)
    key_accum, value_accum = carried
    key_sum, value_sum = (
        lax.psum_scatter(key_accum, "srv", scatter_dimension=0, tiled=True),
        lax.psum_scatter(value_accum, "srv", scatter_dimension=0, tiled=True),
    )
    grads_all = jnp.concatenate(
        [
            query_grad,
            key_sum.astype(jnp.bfloat16).reshape(tok_rows, pair_width),
            value_sum.astype(jnp.bfloat16).reshape(tok_rows, pair_width),
        ],
        axis=1,
    )
    input_terms = lax.dot_general(
        grads_all, weights_all, (((1,), (1,)), ((), ())), preferred_element_type=jnp.float32
    )
    input_grad = lax.psum_scatter(
        input_terms, ("hid", "rep"), scatter_dimension=1, tiled=True
    ).astype(jnp.bfloat16)
    columns = lax.all_to_all(inputs_all, "srv", split_axis=1, concat_axis=0, tiled=True)
    weight_grad = lax.dot_general(
        columns,
        lax.all_gather(grads_all, "srv", axis=0, tiled=True),
        (((0,), (0,)), ((), ())),
        preferred_element_type=jnp.float32,
    )
    return (
        input_grad,
        weight_grad[:, :query_width],
        weight_grad[:, query_width : query_width + pair_width],
        weight_grad[:, query_width + pair_width :],
    )


LOG2E = 1.4426950408889634


def swap(array, axis, size):
    return lax.ppermute(array, axis, [(i, (i + 1) % size) for i in range(size)])


def attention_kernel(*refs, back, heads, block_id, spare, done):
    count = back + 1
    flag_ref, doc_row_ref, doc_col_ref, g_ref = refs[:4]
    rows_refs = refs[4 : 4 + count]
    sum_refs = refs[4 + count : 4 + count + spare]
    outs = refs[4 + count + spare :]
    block = g_ref.shape[0]
    step = block // 2
    scale = DH ** (-0.5)
    nt = (((1,), (1,)), ((), ()))
    first = block_id * block
    low = first - back * block

    def run(start):
        query_pos = lax.broadcasted_iota(jnp.int32, (step, step), 1)
        key_pos = lax.broadcasted_iota(jnp.int32, (step, step), 0)
        tiles = []
        for s in range(2):
            query_doc = doc_row_ref[:, first + s * step : first + (s + 1) * step]
            mine = []
            for j in range(start, count):
                top = step if (j == 0 and back == 2 and s == 1) else 0
                end = step if (j == back and s == 0) else block
                key_doc = doc_col_ref[low + j * block + top : low + j * block + end, :]
                same = key_doc == query_doc
                mine.append((j, top, end, same))
            tiles.append(mine)
        dk = {}
        dv = {}

        def add(store, j, top, end, value):
            for part in range(top // step, end // step):
                piece = value[(part * step - top) : (part + 1) * step - top, :]
                key = (j, part)
                store[key] = piece if key not in store else store[key] + piece

        for h in range(heads):
            at = (2 + h) * DH
            for s in range(2):
                q = rows_refs[back][s * step : (s + 1) * step, at : at + DH]
                g = g_ref[s * step : (s + 1) * step, h * DH : (h + 1) * DH]
                logits, slopes = [], []
                for j, top, end, same in tiles[s]:
                    term = lax.dot_general(rows_refs[j][top:end, :DH], q, nt, preferred_element_type=jnp.float32)
                    term = term * (scale * LOG2E)
                    if j == back:
                        span = end - top
                        query_at = lax.broadcasted_iota(jnp.int32, (span, step), 1) + s * step
                        key_at = lax.broadcasted_iota(jnp.int32, (span, step), 0)
                        same = same & (key_at <= query_at)
                    logits.append(jnp.where(same, term, NEGATIVE))
                    slopes.append(
                        lax.dot_general(rows_refs[j][top:end, DH : 2 * DH], g, nt, preferred_element_type=jnp.float32)
                    )
                peak = functools.reduce(jnp.maximum, [jnp.max(t, axis=0, keepdims=True) for t in logits])
                weights = [jnp.exp2(t - peak) for t in logits]
                total = functools.reduce(jnp.add, [jnp.sum(w, axis=0, keepdims=True) for w in weights])
                inner = functools.reduce(
                    jnp.add, [jnp.sum(w * t, axis=0, keepdims=True) for w, t in zip(weights, slopes)]
                )
                inverse = 1.0 / total
                inner = inner * inverse
                dq = None
                for (j, top, end, _), w, t in zip(tiles[s], weights, slopes):
                    attention = w * inverse
                    score = (attention * (t - inner)).astype(jnp.bfloat16)
                    add(dv, j, top, end, jnp.dot(attention.astype(jnp.bfloat16), g, preferred_element_type=jnp.float32))
                    add(dk, j, top, end, jnp.dot(score, q, preferred_element_type=jnp.float32))
                    part = lax.dot_general(
                        score, rows_refs[j][top:end, :DH], (((0,), (0,)), ((), ())), preferred_element_type=jnp.float32
                    )
                    dq = part if dq is None else dq + part
                target = outs[0]
                column = target.shape[1] - (heads - h) * DH
                target[s * step : (s + 1) * step, column : column + DH] = (dq * scale).astype(target.dtype)
        for j in range(count):
            for part in range(2):
                rows = slice(part * step, (part + 1) * step)
                key = (j, part)
                new_k = dk[key] * scale if key in dk else None
                new_v = dv.get(key)
                if j < spare:
                    old_k, old_v = sum_refs[j][rows, :DH], sum_refs[j][rows, DH:]
                    new_k = old_k if new_k is None else new_k + old_k
                    new_v = old_v if new_v is None else new_v + old_v
                if j in done:
                    ref, column = outs[done[j][0]], done[j][1]
                    ref[rows, column : column + DH] = new_k.astype(ref.dtype)
                    ref[rows, column + DH : column + 2 * DH] = new_v.astype(ref.dtype)
                else:
                    ref = outs[len(outs) - count + j]
                    ref[rows, :DH] = new_k
                    ref[rows, DH:] = new_v

    if back < 2:
        pl.when(flag_ref[0] != 0)(lambda: run(0))
    else:
        wide = flag_ref[block_id]
        pl.when((flag_ref[0] != 0) & (wide != 0))(lambda: run(0))
        pl.when((flag_ref[0] != 0) & (wide == 0))(lambda: run(1))


def attend_block(flags, doc_row, doc_col, g, rows, sums, block_id, reach, blocks):
    block = rows[block_id].shape[0]
    heads = g.shape[1] // DH
    back = min(reach, block_id)
    low = block_id - back
    count = back + 1
    held = [sums[j] for j in range(low, block_id)]
    bf16 = jnp.bfloat16
    final = block_id == blocks - 1
    outs, done = [], {}
    lead = 2 * DH if back == reach else 0
    outs.append(jax.ShapeDtypeStruct((block, lead + heads * DH), bf16))
    if lead:
        done[0] = (0, 0)
    if final:
        rest = [j for j in range(count) if j not in done]
        outs.append(jax.ShapeDtypeStruct((block, len(rest) * 2 * DH), bf16))
        for n, j in enumerate(rest):
            done[j] = (1, n * 2 * DH)
    kept = [j for j in range(count) if j not in done]
    outs += [jax.ShapeDtypeStruct((block, 2 * DH), jnp.float32) for _ in kept]
    vmem = pl.BlockSpec(memory_space=pltpu.VMEM)
    operands = [doc_row, doc_col, g] + [rows[j] for j in range(low, block_id + 1)] + held
    results = pl.pallas_call(
        functools.partial(attention_kernel, back=back, heads=heads, block_id=block_id, spare=len(held), done=done),
        in_specs=[pl.BlockSpec(memory_space=pltpu.SMEM)] + [vmem] * len(operands),
        out_specs=[vmem] * len(outs),
        out_shape=outs,
        cost_estimate=pl.CostEstimate(
            flops=10 * heads * DH * block * block * count, bytes_accessed=3 * block * 8 * DH, transcendentals=heads * block * block * count
        ),
    )(flags, *operands)
    sent = len(outs) - len(kept)
    for n, j in enumerate(kept):
        sums[low + j] = results[sent + n]
    return results[:sent]


def stationary_body(sizes, *arrays):
    return stationary(sizes, *arrays)


def stationary(sizes, layer_input, query_weight, key_weight, value_weight, out_grad, doc_ids):
    planes, across, cores = sizes
    spread = across * cores
    f32, bf16 = jnp.float32, jnp.bfloat16
    tok, width = layer_input.shape
    total = tok * planes
    half_q, half_k = query_weight.shape[1] // 2, key_weight.shape[1] // 2
    plane = lax.axis_index("srv")
    side, core = lax.axis_index("hid"), lax.axis_index("rep")
    last = planes - 1
    blocks = planes
    near_left = plane < planes // 2
    is_end = (plane == 0) | (plane == last)
    trio = ("srv", "hid", "rep")
    pairs = [(t, f) for t in range(planes) for f in range(spread)]
    straight = [(t * spread + f, f * spread + t) for t, f in pairs]
    crossed = [(t * spread + f, (f + cores) % spread * spread + t) for t, f in pairs]

    def climb(early):
        moves = []
        for t, f in pairs:
            x = f // cores
            target = f if (t < planes // 2) == early else (f + cores) % spread
            moves.append((t * spread + f, target * spread + x * cores + t % cores))
        return moves

    rise, fall = climb(True), climb(False)
    line = [[(k, k + 1), (last - k, last - k - 1)] for k in range(last)]
    far_at, near_at = jnp.where(near_left, 1, 0), jnp.where(near_left, 0, 1)

    def part(array, at, size):
        return lax.dynamic_slice_in_dim(array, at * size, size, 1)

    def gather_half(at):
        return jnp.concatenate([part(key_weight, at, half_k), part(value_weight, at, half_k), part(query_weight, at, half_q)], axis=1)

    w_near, w_far = gather_half(near_at), gather_half(far_at)
    g_near, g_far = part(out_grad, near_at, half_q), part(out_grad, far_at, half_q)
    doc_row, doc_col = doc_ids.reshape(1, total), doc_ids.reshape(total, 1)
    wide = [(doc_ids[(b - 1) * tok - 1] == doc_ids[b * tok]) if b >= 2 else is_end for b in range(blocks)]
    flags = jnp.stack([is_end] + wide[1:]).astype(jnp.int32)

    part_rows = tok // across
    mine = lax.dynamic_slice_in_dim(layer_input, side * part_rows, part_rows, 0)
    other = lax.dynamic_slice_in_dim(layer_input, (1 - side) * part_rows, part_rows, 0)
    other = swap(other, "hid", across)
    low_plane = plane < planes // 2
    up, down = jnp.where(low_plane, mine, other), jnp.where(low_plane, other, mine)
    up, down, w_near, w_far, g_near, g_far, doc_col = lax.optimization_barrier(
        (up, down, w_near, w_far, g_near, g_far, doc_col)
    )
    one = lax.ppermute(up, trio, rise)
    two = lax.ppermute(down, trio, fall)
    own_column = side == plane // cores
    low = jnp.where(own_column, one, two)
    high = jnp.where(own_column, two, one)
    held = jnp.concatenate([low, high], axis=0)
    turned = swap(held, "hid", across)
    first_half = jnp.where(side == 0, held, turned).reshape(across, part_rows, width)
    second_half = jnp.where(side == 0, turned, held).reshape(across, part_rows, width)
    pair = jnp.concatenate([first_half, second_half], axis=1)
    mate = swap(pair, "rep", cores)
    even = jnp.where(core == 0, pair, mate)
    odd = jnp.where(core == 0, mate, pair)
    x_rows = [(even if b % cores == 0 else odd)[b // cores] for b in range(planes)]

    g_pieces = []
    for d in range(1, planes):
        g_pieces.append(lax.ppermute(g_near if d < planes // 2 else g_far, "srv", [(d, 0), (last - d, last)]))

    merged = []
    for b in range(blocks):
        far_part = jnp.dot(x_rows[b], w_far, preferred_element_type=f32)
        near_part = jnp.dot(x_rows[b], w_near, preferred_element_type=f32)
        moving = None
        for k in range(last):
            mine_now = far_part if k < planes // 2 else near_part
            if moving is not None:
                mine_now = mine_now + moving.astype(f32)
            moving = lax.ppermute(mine_now.astype(bf16), "srv", line[k])
        merged.append((near_part + moving.astype(f32)).astype(bf16))

    near_q, far_q, near_kv, far_kv = [], [], [], []
    sums = [None] * blocks
    for b in range(blocks):
        g_block = g_pieces[b - 1] if 0 < b else g_near
        g_other = g_pieces[last - b - 1] if b < last else g_near
        g_block, g_other, _ = lax.optimization_barrier((g_block, g_other, merged[b]))
        g = jnp.where(plane == 0, g_block, g_other)
        sent = attend_block(flags, doc_row, doc_col, g, merged, sums, b, total // 2 // tok, blocks)
        for n, array in enumerate(sent):
            hops = [array]
            for k in range(last):
                hops.append(lax.ppermute(hops[k], "srv", line[k]))
            near = jnp.where(is_end, array, hops[1])
            far = jnp.where(is_end, hops[3], hops[2])
            if n == 0:
                lead = array.shape[1] - half_q
                near_q.append(near[:, lead:])
                far_q.append(far[:, lead:])
                if lead:
                    near_kv.append(near[:, :lead])
                    far_kv.append(far[:, :lead])
            else:
                for at in range(0, array.shape[1], 2 * half_k):
                    near_kv.append(near[:, at : at + 2 * half_k])
                    far_kv.append(far[:, at : at + 2 * half_k])

    nt = (((1,), (1,)), ((), ()))
    times = lambda a, w: lax.dot_general(a, w, nt, preferred_element_type=f32)
    split = 2 * half_k
    terms = [
        times(near_q[b], w_near[:, split:])
        + times(far_q[b], w_far[:, split:])
        + times(near_kv[b], w_near[:, :split])
        + times(far_kv[b], w_far[:, :split])
        for b in range(blocks)
    ]
    summed = []
    for i in range(blocks // cores):
        even, odd = terms[cores * i], terms[cores * i + 1]
        theirs = jnp.where(core == 0, odd, even).astype(bf16)
        ours = jnp.where(core == 0, even, odd)
        summed.append((ours + swap(theirs, "rep", cores).astype(f32)).astype(bf16))
    one = jnp.where(side == 0, summed[0], summed[1])
    two = jnp.where(side == 0, summed[1], summed[0])
    one = lax.ppermute(one, trio, straight)
    two = lax.ppermute(two, trio, crossed)
    input_grad = (one.astype(f32) + two.astype(f32)).astype(bf16)

    tn = (((0,), (0,)), ((), ()))
    rows_all = jnp.concatenate(x_rows, axis=0)

    def gathered(near, far, lo, hi):
        left = jnp.concatenate([jnp.where(near_left, n[:, lo:hi], f[:, lo:hi]) for n, f in zip(near, far)], axis=0)
        right = jnp.concatenate([jnp.where(near_left, f[:, lo:hi], n[:, lo:hi]) for n, f in zip(near, far)], axis=0)
        return jnp.concatenate([left, right], axis=1)

    query_out = lax.dot_general(rows_all, gathered(near_q, far_q, 0, half_q), tn, preferred_element_type=f32)
    key_out = lax.dot_general(rows_all, gathered(near_kv, far_kv, 0, half_k), tn, preferred_element_type=f32)
    value_out = lax.dot_general(rows_all, gathered(near_kv, far_kv, half_k, 2 * half_k), tn, preferred_element_type=f32)
    return (input_grad, query_out, key_out, value_out)


def solution(mesh):
    in_specs = (
        P(("groups", "srv"), ("hid", "rep")),
        P("srv", ("hid", "rep")),
        P("srv", ("hid", "rep")),
        P("srv", ("hid", "rep")),
        P(("groups", "srv"), ("hid", "rep")),
        P("groups"),
    )
    out_specs = (
        P(("groups", "srv"), ("hid", "rep")),
        P(("groups", "srv"), ("hid", "rep")),
        P(("groups", "srv"), ("hid", "rep")),
        P(("groups", "srv"), ("hid", "rep")),
    )
    sizes = (mesh.shape["srv"], mesh.shape["hid"], mesh.shape["rep"])
    split = HK // (sizes[1] * sizes[2])
    fits = sizes[0] == sizes[1] * sizes[2] and sizes[1] == 2 and sizes[2] == 2 and split == 2
    chosen = functools.partial(stationary_body, sizes) if fits else body
    return jax.shard_map(chosen, mesh=mesh, in_specs=in_specs, out_specs=out_specs, check_vma=False)
```

```python
import functools

import jax
import jax.numpy as jnp
from jax import lax
from jax.experimental import pallas as pl
from jax.experimental.pallas import tpu as pltpu
from jax.sharding import PartitionSpec as P


HQ = 32
HK = 8
DH = 128
BLOCK = 128


NEGATIVE = -1e30


def attend(queries, cotangent, keys_all, values_all, doc_ids, block_id, carried):
    row_count = queries.shape[0]
    factor_scale = queries.shape[-1] ** (-0.5)
    offsets = jnp.arange(row_count, dtype=jnp.int32)
    query_pos = block_id * row_count + offsets
    query_doc = lax.dynamic_slice_in_dim(doc_ids, block_id * row_count, row_count)
    doc_start = jnp.sum((doc_ids < query_doc[0]).astype(jnp.int32))
    lowest = doc_start // row_count
    highest = jnp.where(True, block_id + 1, lowest)

    def scores_at(key_block):
        key_rows = lax.dynamic_slice_in_dim(keys_all, key_block * row_count, row_count, 0)
        value_rows = lax.dynamic_slice_in_dim(values_all, key_block * row_count, row_count, 0)
        key_doc = lax.dynamic_slice_in_dim(doc_ids, key_block * row_count, row_count)
        key_pos = key_block * row_count + offsets
        allowed = (key_doc[None, :] == query_doc[:, None]) & (
            key_pos[None, :] <= query_pos[:, None]
        )
        logits = (
            jnp.einsum("qgnd,kgd->gnqk", queries, key_rows, preferred_element_type=jnp.float32)
            * factor_scale
        )
        logits = jnp.where(allowed, logits, NEGATIVE)
        slopes = jnp.einsum(
            "qgnd,kgd->gnqk", cotangent, value_rows, preferred_element_type=jnp.float32
        )
        return (key_rows, allowed, logits, slopes)

    def first_pass(key_block, loop_state):
        row_peak, row_total, row_inner = loop_state
        _, allowed, logits, slopes = scores_at(key_block)
        new_peak = jnp.maximum(row_peak, jnp.max(logits, axis=-1))
        weights = jnp.where(allowed, jnp.exp(logits - new_peak[..., None]), 0.0)
        factor = jnp.exp(row_peak - new_peak)
        row_total = row_total * factor + jnp.sum(weights, axis=-1)
        row_inner = row_inner * factor + jnp.sum(weights * slopes, axis=-1)
        return (new_peak, row_total, row_inner)

    stat_shape = (queries.shape[1], queries.shape[2], row_count)
    initial = (
        jnp.full(stat_shape, NEGATIVE, jnp.float32),
        jnp.zeros(stat_shape, jnp.float32),
        jnp.zeros(stat_shape, jnp.float32),
    )
    row_peak, row_total, row_inner = lax.fori_loop(lowest, highest, first_pass, initial)
    safe_total = jnp.where(True, row_total, 1.0)
    row_delta = row_inner / safe_total
    log_total = row_peak + jnp.log(safe_total)

    def second_pass(key_block, loop_state):
        query_grad, key_accum, value_accum = loop_state
        key_rows, allowed, logits, slopes = scores_at(key_block)
        attention = jnp.where(allowed, jnp.exp(logits - log_total[..., None]), 0.0)
        score_grad = (attention * (slopes - row_delta[..., None]) * factor_scale).astype(
            jnp.bfloat16
        )
        value_part = jnp.einsum(
            "gnqk,qgnd->kgd",
            attention.astype(jnp.bfloat16),
            cotangent,
            preferred_element_type=jnp.float32,
        )
        key_part = jnp.einsum(
            "gnqk,qgnd->kgd", score_grad, queries, preferred_element_type=jnp.float32
        )
        query_grad = query_grad + jnp.einsum(
            "gnqk,kgd->qgnd", score_grad, key_rows, preferred_element_type=jnp.float32
        )
        first_row = key_block * row_count
        key_accum = lax.dynamic_update_slice_in_dim(
            key_accum,
            lax.dynamic_slice_in_dim(key_accum, first_row, row_count, 0) + key_part,
            first_row,
            0,
        )
        value_accum = lax.dynamic_update_slice_in_dim(
            value_accum,
            lax.dynamic_slice_in_dim(value_accum, first_row, row_count, 0) + value_part,
            first_row,
            0,
        )
        return (query_grad, key_accum, value_accum)

    start_grad = jnp.zeros(queries.shape, jnp.float32)
    query_grad, key_accum, value_accum = lax.fori_loop(
        lowest, highest, second_pass, (start_grad, carried[0], carried[1])
    )
    return (query_grad, (key_accum, value_accum))


def body(layer_input, query_weight, key_weight, value_weight, out_grad, doc_ids):
    tok_rows = layer_input.shape[0]
    query_width = query_weight.shape[1]
    pair_width = key_weight.shape[1]
    key_heads = pair_width // DH
    group_size = HQ // HK
    block_count = tok_rows // BLOCK
    owner_id = lax.axis_index("srv")
    weights_all = lax.all_gather(
        jnp.concatenate([query_weight, key_weight, value_weight], axis=1), "srv", axis=0, tiled=True
    )
    inputs_all = lax.all_gather(layer_input, ("hid", "rep"), axis=1, tiled=True)
    projected = jnp.dot(inputs_all, weights_all, preferred_element_type=jnp.float32).astype(
        jnp.bfloat16
    )
    queries = projected[:, :query_width].reshape(block_count, BLOCK, key_heads, group_size, DH)
    keys_local = projected[:, query_width : query_width + pair_width]
    values_local = projected[:, query_width + pair_width :]
    keys_all, values_all = (
        lax.all_gather(keys_local, "srv", axis=0, tiled=True),
        lax.all_gather(values_local, "srv", axis=0, tiled=True),
    )
    total_rows = keys_all.shape[0]
    keys_all = keys_all.reshape(total_rows, key_heads, DH)
    values_all = values_all.reshape(total_rows, key_heads, DH)
    cotangent = out_grad.reshape(block_count, BLOCK, key_heads, group_size, DH)
    empty_accum = jnp.zeros((total_rows, key_heads, DH), jnp.float32)

    def own_block(position, loop_state):
        answers, carried = loop_state
        grad_q, carried = attend(
            lax.dynamic_index_in_dim(queries, position, 0, keepdims=False),
            lax.dynamic_index_in_dim(cotangent, position, 0, keepdims=False),
            keys_all,
            values_all,
            doc_ids,
            owner_id * block_count + position,
            carried,
        )
        answers = lax.dynamic_update_index_in_dim(answers, grad_q.astype(jnp.bfloat16), position, 0)
        return (answers, carried)

    answers = jnp.zeros(queries.shape, jnp.bfloat16)
    answers, carried = lax.fori_loop(
        0, block_count, own_block, (answers, (empty_accum, empty_accum))
    )
    query_grad = answers.reshape(tok_rows, query_width)
    key_accum, value_accum = carried
    key_sum, value_sum = (
        lax.psum_scatter(key_accum, "srv", scatter_dimension=0, tiled=True),
        lax.psum_scatter(value_accum, "srv", scatter_dimension=0, tiled=True),
    )
    grads_all = jnp.concatenate(
        [
            query_grad,
            key_sum.astype(jnp.bfloat16).reshape(tok_rows, pair_width),
            value_sum.astype(jnp.bfloat16).reshape(tok_rows, pair_width),
        ],
        axis=1,
    )
    input_terms = lax.dot_general(
        grads_all, weights_all, (((1,), (1,)), ((), ())), preferred_element_type=jnp.float32
    )
    input_grad = lax.psum_scatter(
        input_terms, ("hid", "rep"), scatter_dimension=1, tiled=True
    ).astype(jnp.bfloat16)
    columns = lax.all_to_all(inputs_all, "srv", split_axis=1, concat_axis=0, tiled=True)
    weight_grad = lax.dot_general(
        columns,
        lax.all_gather(grads_all, "srv", axis=0, tiled=True),
        (((0,), (0,)), ((), ())),
        preferred_element_type=jnp.float32,
    )
    return (
        input_grad,
        weight_grad[:, :query_width],
        weight_grad[:, query_width : query_width + pair_width],
        weight_grad[:, query_width + pair_width :],
    )


LOG2E = 1.4426950408889634


def swap(array, axis, size):
    return lax.ppermute(array, axis, [(i, (i + 1) % size) for i in range(size)])


def attention_kernel(flag_ref, *refs, back, heads, block_id, held):
    count = back + 1
    start_hbm, new_hbm, old_hbm, ga_hbm, gb_hbm = refs[:5]
    pair_hbm = refs[5 : 5 + count]
    sum_hbm = refs[5 + count : 5 + count + held]
    outs = refs[5 + count + held : 6 + count + held + back]
    start_ref, new_ref, old_ref, g_ref, pair_ref, sum_ref, q_ref, out_ref, left_ref, sems = refs[6 + count + held + back :]
    block = g_ref.shape[0]
    scale = DH ** (-0.5)
    nt = (((1,), (1,)), ((), ()))
    first = block_id * block
    low = first - back * block

    @pl.when(flag_ref[0] != 0)
    def _():
        copies = [(start_hbm, start_ref), (new_hbm, new_ref), (old_hbm, old_ref)]
        copies += [(pair_hbm[j][0].at[pl.ds(pair_hbm[j][1], block)], pair_ref.at[j]) for j in range(count)]
        copies += [(sum_hbm[n], sum_ref.at[n]) for n in range(held)]
        moves = [pltpu.make_async_copy(a, b, sems.at[n]) for n, (a, b) in enumerate(copies)]
        for move in moves:
            move.start()
        from_first = pltpu.make_async_copy(ga_hbm, g_ref, sems.at[len(moves)])
        from_last = pltpu.make_async_copy(gb_hbm, g_ref, sems.at[len(moves)])

        @pl.when(flag_ref[1] != 0)
        def _():
            from_first.start()

        @pl.when(flag_ref[1] == 0)
        def _():
            from_last.start()

        for move in moves:
            move.wait()
        from_first.wait()
        q_ref[...] = (new_ref[...] + old_ref[...].astype(jnp.float32)).astype(q_ref.dtype)
        begin = start_ref[:, first : first + block]
        query_pos = lax.broadcasted_iota(jnp.int32, (block, block), 1)
        key_pos = lax.broadcasted_iota(jnp.int32, (block, block), 0)
        allowed = []
        for j in range(count):
            inside = key_pos >= begin - (low + j * block)
            allowed.append(inside & (key_pos <= query_pos) if j == back else inside)
        keys_t = [pair_ref[j][:, :DH].T for j in range(count)]
        dk, dv = [None] * count, [None] * count

        def front(h):
            q = q_ref[:, h * DH : (h + 1) * DH]
            g = g_ref[:, h * DH : (h + 1) * DH]
            logits, slopes = [], []
            for j in range(count):
                k, v = pair_ref[j][:, :DH], pair_ref[j][:, DH:]
                term = lax.dot_general(k, q, nt, preferred_element_type=jnp.float32) * (scale * LOG2E)
                logits.append(jnp.where(allowed[j], term, NEGATIVE))
                slopes.append(lax.dot_general(v, g, nt, preferred_element_type=jnp.float32))
            return q, g, logits, slopes

        ahead = front(0)
        for h in range(heads):
            q, g, logits, slopes = ahead
            if h + 1 < heads:
                ahead = front(h + 1)
            peak = functools.reduce(jnp.maximum, [jnp.max(t, axis=0, keepdims=True) for t in logits])
            weights = [jnp.exp2(t - peak) for t in logits]
            total = functools.reduce(jnp.add, [jnp.sum(w, axis=0, keepdims=True) for w in weights])
            inner = functools.reduce(jnp.add, [jnp.sum(w * t, axis=0, keepdims=True) for w, t in zip(weights, slopes)])
            inverse = 1.0 / total
            inner = inner * inverse
            dq = None
            for j in range(count):
                attention = weights[j] * inverse
                score = (attention * (slopes[j] - inner)).astype(jnp.bfloat16)
                value_part = jnp.dot(attention.astype(jnp.bfloat16), g, preferred_element_type=jnp.float32)
                key_part = jnp.dot(score, q, preferred_element_type=jnp.float32)
                dv[j] = value_part if dv[j] is None else dv[j] + value_part
                dk[j] = key_part if dk[j] is None else dk[j] + key_part
                part = jnp.dot(keys_t[j], score, preferred_element_type=jnp.float32)
                dq = part if dq is None else dq + part
            out_ref[:, (2 + h) * DH : (3 + h) * DH] = (dq * scale).T.astype(out_ref.dtype)
        fresh = count - held
        for j in range(count):
            new_k, new_v = dk[j] * scale, dv[j]
            if j >= fresh:
                new_k = new_k + sum_ref[j - fresh][:, :DH]
                new_v = new_v + sum_ref[j - fresh][:, DH:]
            if j == back:
                out_ref[:, :DH] = new_k.astype(out_ref.dtype)
                out_ref[:, DH : 2 * DH] = new_v.astype(out_ref.dtype)
            else:
                left_ref[j, :, :DH] = new_k
                left_ref[j, :, DH:] = new_v
        moves = [pltpu.make_async_copy(out_ref, outs[0], sems.at[0])]
        moves += [pltpu.make_async_copy(left_ref.at[j], outs[1 + j], sems.at[1 + j]) for j in range(back)]
        for move in moves:
            move.start()
        for move in moves:
            move.wait()


def attend_block(flags, begins, pairs, fresh_q, moved_q, g_first, g_last, sums, block_id, reach):
    block, width = g_first.shape
    heads = width // DH
    back = min(reach, block_id)
    low = block_id - back
    count = back + 1
    held = [sums[j] for j in range(low, block_id + 1) if sums[j] is not None]
    f32, bf16 = jnp.float32, jnp.bfloat16
    hbm = pl.BlockSpec(memory_space=pl.ANY)
    sum_shape = (block, 2 * DH)
    outs = [jax.ShapeDtypeStruct((block, 2 * DH + width), bf16)] + [jax.ShapeDtypeStruct(sum_shape, f32)] * back
    rows = [pairs[j][1] for j in range(low, block_id + 1)]
    operands = [begins, fresh_q, moved_q, g_first, g_last] + [pairs[j][0] for j in range(low, block_id + 1)] + held

    def kernel(flag_ref, *refs):
        refs = list(refs)
        refs[5 : 5 + count] = list(zip(refs[5 : 5 + count], rows))
        attention_kernel(flag_ref, *refs, back=back, heads=heads, block_id=block_id, held=len(held))

    results = pl.pallas_call(
        kernel,
        in_specs=[pl.BlockSpec(memory_space=pltpu.SMEM)] + [hbm] * len(operands),
        out_specs=[hbm] * len(outs),
        out_shape=outs,
        scratch_shapes=[
            pltpu.VMEM(begins.shape, jnp.int32),
            pltpu.VMEM((block, width), f32),
            pltpu.VMEM((block, width), bf16),
            pltpu.VMEM((block, width), bf16),
            pltpu.VMEM((count,) + sum_shape, bf16),
            pltpu.VMEM((max(1, len(held)),) + sum_shape, f32),
            pltpu.VMEM((block, width), bf16),
            pltpu.VMEM((block, 2 * DH + width), bf16),
            pltpu.VMEM((max(1, back),) + sum_shape, f32),
            pltpu.SemaphoreType.DMA((4 + count + len(held),)),
        ],
        cost_estimate=pl.CostEstimate(
            flops=10 * heads * DH * block * block * count, bytes_accessed=3 * block * 8 * DH, transcendentals=heads * block * block * count
        ),
    )(flags, *operands)
    for j in range(back):
        sums[low + j] = results[1 + j]
    return results[0]


def weight_grad_kernel(plane_ref, *refs, planes, blocks):
    x_hbm = refs[0]
    hops = refs[1 : 1 + blocks * planes]
    out_q, out_k, out_v = refs[1 + blocks * planes : 4 + blocks * planes]
    x_ref, left_ref, right_ref, q_ref, k_ref, v_ref, sems, out_sems = refs[4 + blocks * planes :]
    rows = left_ref.shape[0] // blocks
    tile = q_ref.shape[1]
    half_q = q_ref.shape[2] // 2
    move_x = pltpu.make_async_copy(x_hbm, x_ref, sems.at[0])
    move_x.start()

    def fetch(b, source, target, n):
        return pltpu.make_async_copy(source, target.at[pl.ds(b * rows, rows)], sems.at[n])

    for z in range(planes):

        @pl.when(plane_ref[0] == z)
        def _(z=z):
            for b in range(blocks):
                fetch(b, hops[b * planes + z], left_ref, 1 + 2 * b).start()
                fetch(b, hops[b * planes + planes - 1 - z], right_ref, 2 + 2 * b).start()

    move_x.wait()
    for b in range(blocks):
        fetch(b, hops[b * planes], left_ref, 1 + 2 * b).wait()
        fetch(b, hops[b * planes], right_ref, 2 + 2 * b).wait()

    def store(step, slot):
        at = pl.ds(pl.multiple_of(step * tile, tile), tile)
        return [
            pltpu.make_async_copy(ref.at[slot], out.at[at], out_sems.at[slot, n])
            for n, (ref, out) in enumerate(((q_ref, out_q), (k_ref, out_k), (v_ref, out_v)))
        ]

    steps = x_ref.shape[1] // tile

    def body(step, carry):
        slot = step % 2

        @pl.when(step >= 2)
        def _():
            for move in store(step, slot):
                move.wait()

        x_t = x_ref[:, pl.ds(pl.multiple_of(step * tile, tile), tile)].T
        for side, ref in enumerate((left_ref, right_ref)):
            result = jnp.dot(x_t, ref[...], preferred_element_type=jnp.float32)
            k_ref[slot, :, side * DH : (side + 1) * DH] = result[:, :DH]
            v_ref[slot, :, side * DH : (side + 1) * DH] = result[:, DH : 2 * DH]
            q_ref[slot, :, side * half_q : (side + 1) * half_q] = result[:, 2 * DH :]
        for move in store(step, slot):
            move.start()
        return carry

    lax.fori_loop(0, steps, body, 0)
    for slot in range(2):
        for move in store(slot, slot):
            move.wait()


def weight_grads(plane, x, hops, planes, shapes):
    total, width = x.shape
    blocks = len(hops)
    flat = [array for group in hops for array in group]
    tile = 256
    f32, bf16 = jnp.float32, jnp.bfloat16
    hbm = pl.BlockSpec(memory_space=pl.ANY)
    columns = flat[0].shape[1]
    return pl.pallas_call(
        functools.partial(weight_grad_kernel, planes=planes, blocks=blocks),
        in_specs=[pl.BlockSpec(memory_space=pltpu.SMEM)] + [hbm] * (1 + len(flat)),
        out_specs=[hbm] * 3,
        out_shape=[jax.ShapeDtypeStruct(s, f32) for s in shapes],
        scratch_shapes=[
            pltpu.VMEM((total, width), bf16),
            pltpu.VMEM((total, columns), bf16),
            pltpu.VMEM((total, columns), bf16),
        ]
        + [pltpu.VMEM((2, tile, s[1]), f32) for s in shapes]
        + [pltpu.SemaphoreType.DMA((1 + 2 * blocks,)), pltpu.SemaphoreType.DMA((2, 3))],
        cost_estimate=pl.CostEstimate(flops=4 * total * width * columns, bytes_accessed=8 * total * width, transcendentals=0),
    )(plane.astype(jnp.int32).reshape(1), x, *flat)


def stationary_body(sizes, *arrays):
    return stationary(sizes, *arrays)


def stationary(sizes, layer_input, query_weight, key_weight, value_weight, out_grad, doc_ids):
    planes, across, cores = sizes
    spread = across * cores
    f32, bf16 = jnp.float32, jnp.bfloat16
    tok, width = layer_input.shape
    total = tok * planes
    half_q, half_k = query_weight.shape[1] // 2, key_weight.shape[1] // 2
    plane = lax.axis_index("srv")
    side, core = lax.axis_index("hid"), lax.axis_index("rep")
    last = planes - 1
    blocks = planes
    near_left = plane < planes // 2
    is_end = (plane == 0) | (plane == last)
    trio = ("srv", "hid", "rep")
    pairs = [(t, f) for t in range(planes) for f in range(spread)]
    straight = [(t * spread + f, f * spread + t) for t, f in pairs]
    crossed = [(t * spread + f, (f + cores) % spread * spread + t) for t, f in pairs]

    def climb(early):
        moves = []
        for t, f in pairs:
            x = f // cores
            target = f if (t % 2 == 0) == early else (f + cores) % spread
            moves.append((t * spread + f, target * spread + x * cores + t * cores // planes))
        return moves

    rise, fall = climb(True), climb(False)
    line = [[(k, k + 1), (last - k, last - k - 1)] for k in range(last)]
    far_at, near_at = jnp.where(near_left, 1, 0), jnp.where(near_left, 0, 1)

    def part(array, at, size):
        return lax.dynamic_slice_in_dim(array, at * size, size, 1)

    pair_weight = lambda at: jnp.concatenate([part(key_weight, at, half_k), part(value_weight, at, half_k)], axis=1)
    wp_near, wp_far = pair_weight(near_at), pair_weight(far_at)
    wq_near, wq_far = part(query_weight, near_at, half_q), part(query_weight, far_at, half_q)
    g_near, g_far = part(out_grad, near_at, half_q), part(out_grad, far_at, half_q)
    begins = jnp.sum((doc_ids[None, :] < doc_ids[:, None]).astype(jnp.int32), axis=1).reshape(1, total)
    flags = jnp.stack([is_end, plane == 0]).astype(jnp.int32)

    part_rows = tok // across
    mine = lax.dynamic_slice_in_dim(layer_input, side * part_rows, part_rows, 0)
    other = lax.dynamic_slice_in_dim(layer_input, (1 - side) * part_rows, part_rows, 0)
    other = swap(other, "hid", across)
    even_plane = plane % 2 == 0
    up = lax.ppermute(jnp.where(even_plane, mine, other), trio, rise)
    down = lax.ppermute(jnp.where(even_plane, other, mine), trio, fall)
    wp_near, wp_far, wq_near, wq_far, g_near, g_far, begins, flags, up = lax.optimization_barrier(
        (wp_near, wp_far, wq_near, wq_far, g_near, g_far, begins, flags, up)
    )
    straight_first = jnp.where(side == plane // cores, 0, 1)
    held = planes // cores
    rows_all = jnp.zeros((total, width), bf16)

    def place(rows_all, piece, owner, which, half):
        return lax.dynamic_update_slice_in_dim(rows_all, piece, ((owner * held + which) * across + half) * part_rows, 0)

    for piece, which in ((up, straight_first), (down, 1 - straight_first)):
        turned = swap(piece, "hid", across)
        mate = swap(piece, "rep", cores)
        turned_mate = swap(turned, "rep", cores)
        rows_all = place(rows_all, piece, core, which, side)
        rows_all = place(rows_all, turned, core, 1 - which, 1 - side)
        rows_all = place(rows_all, mate, 1 - core, which, side)
        rows_all = place(rows_all, turned_mate, 1 - core, 1 - which, 1 - side)
    x_rows = [lax.slice_in_dim(rows_all, b * tok, (b + 1) * tok, axis=0) for b in range(planes)]

    g_pieces = []
    for d in range(1, planes):
        g_pieces.append(lax.ppermute(g_near if d < planes // 2 else g_far, "srv", [(d, 0), (last - d, last)]))

    middle = total // 2
    chunks = [(rows_all[middle:], wp_far, wp_near), (rows_all[:middle], wp_far, wp_near)]
    chunks += [(x_rows[b], wq_far, wq_near) for b in range(blocks - 1, -1, -1)]
    landed = []
    for c, (x, w_far, w_near) in enumerate(chunks):
        far_part = jnp.dot(x, w_far, preferred_element_type=f32)
        near_part = jnp.dot(x, w_near, preferred_element_type=f32)
        moving = None
        for k in range(last):
            mine_now = far_part if k < planes // 2 else near_part
            if moving is not None:
                mine_now = mine_now + moving.astype(f32)
            moving = lax.ppermute(mine_now.astype(bf16), "srv", line[k])
        landed.append((near_part + moving.astype(f32)).astype(bf16) if c < 2 else (near_part, moving))

    pairs_at = [(landed[1], b * tok) if b < blocks // 2 else (landed[0], b * tok - middle) for b in range(blocks)]
    all_hops = [None] * blocks
    near_q, far_q, near_kv, far_kv = [[None] * blocks for _ in range(4)]
    sums = [None] * blocks
    lead = 2 * half_k
    g_near, *g_pieces, _ = lax.optimization_barrier((g_near, *g_pieces, landed[0]))
    for b in range(blocks - 1, -1, -1):
        g_first = g_pieces[b - 1] if b > 0 else g_near
        g_last = g_pieces[last - b - 1] if b < last else g_near
        fresh_q, moved_q = landed[2 + blocks - 1 - b]
        local = attend_block(flags, begins, pairs_at, fresh_q, moved_q, g_first, g_last, sums, b, middle // tok)
        hops = [local]
        for k in range(last):
            hops.append(lax.ppermute(hops[k], "srv", line[k]))
        all_hops[b] = hops
        near = jnp.where(is_end, local, hops[1])
        far = jnp.where(is_end, hops[3], hops[2])
        near_q[b], far_q[b], near_kv[b], far_kv[b] = near[:, lead:], far[:, lead:], near[:, :lead], far[:, :lead]

    nt = (((1,), (1,)), ((), ()))
    times = lambda a, w: lax.dot_general(a, w, nt, preferred_element_type=f32)
    terms = []
    for b in range(blocks):
        near_term = times(near_q[b], wq_near) + times(near_kv[b], wp_near)
        terms.append(near_term + times(far_q[b], wq_far) + times(far_kv[b], wp_far))
    summed = []
    for i in range(blocks // cores):
        even, odd = terms[cores * i], terms[cores * i + 1]
        theirs = jnp.where(core == 0, odd, even).astype(bf16)
        ours = jnp.where(core == 0, even, odd)
        summed.append((ours + swap(theirs, "rep", cores).astype(f32)).astype(bf16))
    one = jnp.where(side == 0, summed[0], summed[1])
    two = jnp.where(side == 0, summed[1], summed[0])
    one = lax.ppermute(one, trio, straight)
    two = lax.ppermute(two, trio, crossed)
    input_grad = (one.astype(f32) + two.astype(f32)).astype(bf16)

    shapes = [(width, w.shape[1]) for w in (query_weight, key_weight, value_weight)]
    outs = weight_grads(plane, rows_all, all_hops, planes, shapes)
    return (input_grad, *outs)


def solution(mesh):
    in_specs = (
        P(("groups", "srv"), ("hid", "rep")),
        P("srv", ("hid", "rep")),
        P("srv", ("hid", "rep")),
        P("srv", ("hid", "rep")),
        P(("groups", "srv"), ("hid", "rep")),
        P("groups"),
    )
    out_specs = (
        P(("groups", "srv"), ("hid", "rep")),
        P(("groups", "srv"), ("hid", "rep")),
        P(("groups", "srv"), ("hid", "rep")),
        P(("groups", "srv"), ("hid", "rep")),
    )
    sizes = (mesh.shape["srv"], mesh.shape["hid"], mesh.shape["rep"])
    split = HK // (sizes[1] * sizes[2])
    fits = sizes[0] == sizes[1] * sizes[2] and sizes[1] == 2 and sizes[2] == 2 and split == 2
    chosen = functools.partial(stationary_body, sizes) if fits else body
    return jax.shard_map(chosen, mesh=mesh, in_specs=in_specs, out_specs=out_specs, check_vma=False)
```

```python
import functools

import jax
import jax.numpy as jnp
from jax import lax
from jax.experimental import pallas as pl
from jax.experimental.pallas import tpu as pltpu
from jax.sharding import PartitionSpec as P


HQ = 32
HK = 8
DH = 128
BLOCK = 128


NEGATIVE = -1e30


def attend(queries, cotangent, keys_all, values_all, doc_ids, block_id, carried):
    row_count = queries.shape[0]
    factor_scale = queries.shape[-1] ** (-0.5)
    offsets = jnp.arange(row_count, dtype=jnp.int32)
    query_pos = block_id * row_count + offsets
    query_doc = lax.dynamic_slice_in_dim(doc_ids, block_id * row_count, row_count)
    doc_start = jnp.sum((doc_ids < query_doc[0]).astype(jnp.int32))
    lowest = doc_start // row_count
    highest = jnp.where(True, block_id + 1, lowest)

    def scores_at(key_block):
        key_rows = lax.dynamic_slice_in_dim(keys_all, key_block * row_count, row_count, 0)
        value_rows = lax.dynamic_slice_in_dim(values_all, key_block * row_count, row_count, 0)
        key_doc = lax.dynamic_slice_in_dim(doc_ids, key_block * row_count, row_count)
        key_pos = key_block * row_count + offsets
        allowed = (key_doc[None, :] == query_doc[:, None]) & (
            key_pos[None, :] <= query_pos[:, None]
        )
        logits = (
            jnp.einsum("qgnd,kgd->gnqk", queries, key_rows, preferred_element_type=jnp.float32)
            * factor_scale
        )
        logits = jnp.where(allowed, logits, NEGATIVE)
        slopes = jnp.einsum(
            "qgnd,kgd->gnqk", cotangent, value_rows, preferred_element_type=jnp.float32
        )
        return (key_rows, allowed, logits, slopes)

    def first_pass(key_block, loop_state):
        row_peak, row_total, row_inner = loop_state
        _, allowed, logits, slopes = scores_at(key_block)
        new_peak = jnp.maximum(row_peak, jnp.max(logits, axis=-1))
        weights = jnp.where(allowed, jnp.exp(logits - new_peak[..., None]), 0.0)
        factor = jnp.exp(row_peak - new_peak)
        row_total = row_total * factor + jnp.sum(weights, axis=-1)
        row_inner = row_inner * factor + jnp.sum(weights * slopes, axis=-1)
        return (new_peak, row_total, row_inner)

    stat_shape = (queries.shape[1], queries.shape[2], row_count)
    initial = (
        jnp.full(stat_shape, NEGATIVE, jnp.float32),
        jnp.zeros(stat_shape, jnp.float32),
        jnp.zeros(stat_shape, jnp.float32),
    )
    row_peak, row_total, row_inner = lax.fori_loop(lowest, highest, first_pass, initial)
    safe_total = jnp.where(True, row_total, 1.0)
    row_delta = row_inner / safe_total
    log_total = row_peak + jnp.log(safe_total)

    def second_pass(key_block, loop_state):
        query_grad, key_accum, value_accum = loop_state
        key_rows, allowed, logits, slopes = scores_at(key_block)
        attention = jnp.where(allowed, jnp.exp(logits - log_total[..., None]), 0.0)
        score_grad = (attention * (slopes - row_delta[..., None]) * factor_scale).astype(
            jnp.bfloat16
        )
        value_part = jnp.einsum(
            "gnqk,qgnd->kgd",
            attention.astype(jnp.bfloat16),
            cotangent,
            preferred_element_type=jnp.float32,
        )
        key_part = jnp.einsum(
            "gnqk,qgnd->kgd", score_grad, queries, preferred_element_type=jnp.float32
        )
        query_grad = query_grad + jnp.einsum(
            "gnqk,kgd->qgnd", score_grad, key_rows, preferred_element_type=jnp.float32
        )
        first_row = key_block * row_count
        key_accum = lax.dynamic_update_slice_in_dim(
            key_accum,
            lax.dynamic_slice_in_dim(key_accum, first_row, row_count, 0) + key_part,
            first_row,
            0,
        )
        value_accum = lax.dynamic_update_slice_in_dim(
            value_accum,
            lax.dynamic_slice_in_dim(value_accum, first_row, row_count, 0) + value_part,
            first_row,
            0,
        )
        return (query_grad, key_accum, value_accum)

    start_grad = jnp.zeros(queries.shape, jnp.float32)
    query_grad, key_accum, value_accum = lax.fori_loop(
        lowest, highest, second_pass, (start_grad, carried[0], carried[1])
    )
    return (query_grad, (key_accum, value_accum))


def body(layer_input, query_weight, key_weight, value_weight, out_grad, doc_ids):
    tok_rows = layer_input.shape[0]
    query_width = query_weight.shape[1]
    pair_width = key_weight.shape[1]
    key_heads = pair_width // DH
    group_size = HQ // HK
    block_count = tok_rows // BLOCK
    owner_id = lax.axis_index("srv")
    weights_all = lax.all_gather(
        jnp.concatenate([query_weight, key_weight, value_weight], axis=1), "srv", axis=0, tiled=True
    )
    inputs_all = lax.all_gather(layer_input, ("hid", "rep"), axis=1, tiled=True)
    projected = jnp.dot(inputs_all, weights_all, preferred_element_type=jnp.float32).astype(
        jnp.bfloat16
    )
    queries = projected[:, :query_width].reshape(block_count, BLOCK, key_heads, group_size, DH)
    keys_local = projected[:, query_width : query_width + pair_width]
    values_local = projected[:, query_width + pair_width :]
    keys_all, values_all = (
        lax.all_gather(keys_local, "srv", axis=0, tiled=True),
        lax.all_gather(values_local, "srv", axis=0, tiled=True),
    )
    total_rows = keys_all.shape[0]
    keys_all = keys_all.reshape(total_rows, key_heads, DH)
    values_all = values_all.reshape(total_rows, key_heads, DH)
    cotangent = out_grad.reshape(block_count, BLOCK, key_heads, group_size, DH)
    empty_accum = jnp.zeros((total_rows, key_heads, DH), jnp.float32)

    def own_block(position, loop_state):
        answers, carried = loop_state
        grad_q, carried = attend(
            lax.dynamic_index_in_dim(queries, position, 0, keepdims=False),
            lax.dynamic_index_in_dim(cotangent, position, 0, keepdims=False),
            keys_all,
            values_all,
            doc_ids,
            owner_id * block_count + position,
            carried,
        )
        answers = lax.dynamic_update_index_in_dim(answers, grad_q.astype(jnp.bfloat16), position, 0)
        return (answers, carried)

    answers = jnp.zeros(queries.shape, jnp.bfloat16)
    answers, carried = lax.fori_loop(
        0, block_count, own_block, (answers, (empty_accum, empty_accum))
    )
    query_grad = answers.reshape(tok_rows, query_width)
    key_accum, value_accum = carried
    key_sum, value_sum = (
        lax.psum_scatter(key_accum, "srv", scatter_dimension=0, tiled=True),
        lax.psum_scatter(value_accum, "srv", scatter_dimension=0, tiled=True),
    )
    grads_all = jnp.concatenate(
        [
            query_grad,
            key_sum.astype(jnp.bfloat16).reshape(tok_rows, pair_width),
            value_sum.astype(jnp.bfloat16).reshape(tok_rows, pair_width),
        ],
        axis=1,
    )
    input_terms = lax.dot_general(
        grads_all, weights_all, (((1,), (1,)), ((), ())), preferred_element_type=jnp.float32
    )
    input_grad = lax.psum_scatter(
        input_terms, ("hid", "rep"), scatter_dimension=1, tiled=True
    ).astype(jnp.bfloat16)
    columns = lax.all_to_all(inputs_all, "srv", split_axis=1, concat_axis=0, tiled=True)
    weight_grad = lax.dot_general(
        columns,
        lax.all_gather(grads_all, "srv", axis=0, tiled=True),
        (((0,), (0,)), ((), ())),
        preferred_element_type=jnp.float32,
    )
    return (
        input_grad,
        weight_grad[:, :query_width],
        weight_grad[:, query_width : query_width + pair_width],
        weight_grad[:, query_width + pair_width :],
    )


LOG2E = 1.4426950408889634


def swap(array, axis, size):
    return lax.ppermute(array, axis, [(i, (i + 1) % size) for i in range(size)])


def attention_kernel(flag_ref, *refs, back, heads, block_id, held):
    count = back + 1
    start_hbm, new_hbm, old_hbm, ga_hbm, gb_hbm = refs[:5]
    pair_hbm = refs[5 : 5 + count]
    sum_hbm = refs[5 + count : 5 + count + held]
    outs = refs[5 + count + held : 6 + count + held + back]
    start_ref, new_ref, old_ref, g_ref, pair_ref, sum_ref, q_ref, out_ref, left_ref, sems = refs[6 + count + held + back :]
    block = g_ref.shape[0]
    scale = DH ** (-0.5)
    nt = (((1,), (1,)), ((), ()))
    first = block_id * block
    low = first - back * block

    @pl.when(flag_ref[0] != 0)
    def _():
        copies = [(start_hbm, start_ref), (new_hbm, new_ref), (old_hbm, old_ref)]
        copies += [(pair_hbm[j][0].at[pl.ds(pair_hbm[j][1], block)], pair_ref.at[j]) for j in range(count)]
        copies += [(sum_hbm[n], sum_ref.at[n]) for n in range(held)]
        moves = [pltpu.make_async_copy(a, b, sems.at[n]) for n, (a, b) in enumerate(copies)]
        for move in moves:
            move.start()
        from_first = pltpu.make_async_copy(ga_hbm, g_ref, sems.at[len(moves)])
        from_last = pltpu.make_async_copy(gb_hbm, g_ref, sems.at[len(moves)])

        @pl.when(flag_ref[1] != 0)
        def _():
            from_first.start()

        @pl.when(flag_ref[1] == 0)
        def _():
            from_last.start()

        for move in moves:
            move.wait()
        from_first.wait()
        q_ref[...] = (new_ref[...] + old_ref[...].astype(jnp.float32)).astype(q_ref.dtype)
        begin = start_ref[:, first : first + block]
        query_pos = lax.broadcasted_iota(jnp.int32, (block, block), 1)
        key_pos = lax.broadcasted_iota(jnp.int32, (block, block), 0)
        allowed = []
        for j in range(count):
            inside = key_pos >= begin - (low + j * block)
            allowed.append(inside & (key_pos <= query_pos) if j == back else inside)
        keys_t = [pair_ref[j][:, :DH].T for j in range(count)]
        dk, dv = [None] * count, [None] * count

        def front(h):
            q = q_ref[:, h * DH : (h + 1) * DH]
            g = g_ref[:, h * DH : (h + 1) * DH]
            logits, slopes = [], []
            for j in range(count):
                k, v = pair_ref[j][:, :DH], pair_ref[j][:, DH:]
                term = lax.dot_general(k, q, nt, preferred_element_type=jnp.float32) * (scale * LOG2E)
                logits.append(jnp.where(allowed[j], term, NEGATIVE))
                slopes.append(lax.dot_general(v, g, nt, preferred_element_type=jnp.float32))
            return q, g, logits, slopes

        ahead = front(0)
        for h in range(heads):
            q, g, logits, slopes = ahead
            if h + 1 < heads:
                ahead = front(h + 1)
            peak = functools.reduce(jnp.maximum, [jnp.max(t, axis=0, keepdims=True) for t in logits])
            weights = [jnp.exp2(t - peak) for t in logits]
            total = functools.reduce(jnp.add, [jnp.sum(w, axis=0, keepdims=True) for w in weights])
            inner = functools.reduce(jnp.add, [jnp.sum(w * t, axis=0, keepdims=True) for w, t in zip(weights, slopes)])
            inverse = 1.0 / total
            inner = inner * inverse
            dq = None
            for j in range(count):
                attention = weights[j] * inverse
                score = (attention * (slopes[j] - inner)).astype(jnp.bfloat16)
                value_part = jnp.dot(attention.astype(jnp.bfloat16), g, preferred_element_type=jnp.float32)
                key_part = jnp.dot(score, q, preferred_element_type=jnp.float32)
                dv[j] = value_part if dv[j] is None else dv[j] + value_part
                dk[j] = key_part if dk[j] is None else dk[j] + key_part
                part = jnp.dot(keys_t[j], score, preferred_element_type=jnp.float32)
                dq = part if dq is None else dq + part
            out_ref[:, (2 + h) * DH : (3 + h) * DH] = (dq * scale).T.astype(out_ref.dtype)
        fresh = count - held
        for j in range(count):
            new_k, new_v = dk[j] * scale, dv[j]
            if j >= fresh:
                new_k = new_k + sum_ref[j - fresh][:, :DH]
                new_v = new_v + sum_ref[j - fresh][:, DH:]
            if j == back:
                out_ref[:, :DH] = new_k.astype(out_ref.dtype)
                out_ref[:, DH : 2 * DH] = new_v.astype(out_ref.dtype)
            else:
                left_ref[j, :, :DH] = new_k
                left_ref[j, :, DH:] = new_v
        moves = [pltpu.make_async_copy(out_ref, outs[0], sems.at[0])]
        moves += [pltpu.make_async_copy(left_ref.at[j], outs[1 + j], sems.at[1 + j]) for j in range(back)]
        for move in moves:
            move.start()
        for move in moves:
            move.wait()


def attend_block(flags, begins, pairs, fresh_q, moved_q, g_first, g_last, sums, block_id, reach):
    block, width = g_first.shape
    heads = width // DH
    back = min(reach, block_id)
    low = block_id - back
    count = back + 1
    held = [sums[j] for j in range(low, block_id + 1) if sums[j] is not None]
    f32, bf16 = jnp.float32, jnp.bfloat16
    hbm = pl.BlockSpec(memory_space=pl.ANY)
    sum_shape = (block, 2 * DH)
    outs = [jax.ShapeDtypeStruct((block, 2 * DH + width), bf16)] + [jax.ShapeDtypeStruct(sum_shape, f32)] * back
    rows = [pairs[j][1] for j in range(low, block_id + 1)]
    operands = [begins, fresh_q, moved_q, g_first, g_last] + [pairs[j][0] for j in range(low, block_id + 1)] + held

    def kernel(flag_ref, *refs):
        refs = list(refs)
        refs[5 : 5 + count] = list(zip(refs[5 : 5 + count], rows))
        attention_kernel(flag_ref, *refs, back=back, heads=heads, block_id=block_id, held=len(held))

    results = pl.pallas_call(
        kernel,
        in_specs=[pl.BlockSpec(memory_space=pltpu.SMEM)] + [hbm] * len(operands),
        out_specs=[hbm] * len(outs),
        out_shape=outs,
        scratch_shapes=[
            pltpu.VMEM(begins.shape, jnp.int32),
            pltpu.VMEM((block, width), f32),
            pltpu.VMEM((block, width), bf16),
            pltpu.VMEM((block, width), bf16),
            pltpu.VMEM((count,) + sum_shape, bf16),
            pltpu.VMEM((max(1, len(held)),) + sum_shape, f32),
            pltpu.VMEM((block, width), bf16),
            pltpu.VMEM((block, 2 * DH + width), bf16),
            pltpu.VMEM((max(1, back),) + sum_shape, f32),
            pltpu.SemaphoreType.DMA((4 + count + len(held),)),
        ],
        cost_estimate=pl.CostEstimate(
            flops=10 * heads * DH * block * block * count, bytes_accessed=3 * block * 8 * DH, transcendentals=heads * block * block * count
        ),
    )(flags, *operands)
    for j in range(back):
        sums[low + j] = results[1 + j]
    return results[0]


def weight_grad_kernel(plane_ref, *refs, planes, blocks):
    x_hbm = refs[0]
    hops = refs[1 : 1 + blocks * planes]
    out_q, out_k, out_v = refs[1 + blocks * planes : 4 + blocks * planes]
    x_ref, left_ref, right_ref, q_ref, k_ref, v_ref, sems, out_sems = refs[4 + blocks * planes :]
    rows = left_ref.shape[0] // blocks
    tile = q_ref.shape[1]
    half_q = q_ref.shape[2] // 2
    move_x = pltpu.make_async_copy(x_hbm, x_ref, sems.at[0])
    move_x.start()

    def fetch(b, source, target, n):
        return pltpu.make_async_copy(source, target.at[pl.ds(b * rows, rows)], sems.at[n])

    for z in range(planes):

        @pl.when(plane_ref[0] == z)
        def _(z=z):
            for b in range(blocks):
                fetch(b, hops[b * planes + z], left_ref, 1 + 2 * b).start()
                fetch(b, hops[b * planes + planes - 1 - z], right_ref, 2 + 2 * b).start()

    move_x.wait()
    for b in range(blocks):
        fetch(b, hops[b * planes], left_ref, 1 + 2 * b).wait()
        fetch(b, hops[b * planes], right_ref, 2 + 2 * b).wait()

    def store(step, slot):
        at = pl.ds(pl.multiple_of(step * tile, tile), tile)
        return [
            pltpu.make_async_copy(ref.at[slot], out.at[at], out_sems.at[slot, n])
            for n, (ref, out) in enumerate(((q_ref, out_q), (k_ref, out_k), (v_ref, out_v)))
        ]

    steps = x_ref.shape[1] // tile

    def body(step, carry):
        slot = step % 2

        @pl.when(step >= 2)
        def _():
            for move in store(step, slot):
                move.wait()

        x_t = x_ref[:, pl.ds(pl.multiple_of(step * tile, tile), tile)].T
        for side, ref in enumerate((left_ref, right_ref)):
            result = jnp.dot(x_t, ref[...], preferred_element_type=jnp.float32)
            k_ref[slot, :, side * DH : (side + 1) * DH] = result[:, :DH]
            v_ref[slot, :, side * DH : (side + 1) * DH] = result[:, DH : 2 * DH]
            q_ref[slot, :, side * half_q : (side + 1) * half_q] = result[:, 2 * DH :]
        for move in store(step, slot):
            move.start()
        return carry

    lax.fori_loop(0, steps, body, 0)
    for slot in range(2):
        for move in store(slot, slot):
            move.wait()


def weight_grads(plane, x, hops, planes, shapes):
    total, width = x.shape
    blocks = len(hops)
    flat = [array for group in hops for array in group]
    tile = 256
    f32, bf16 = jnp.float32, jnp.bfloat16
    hbm = pl.BlockSpec(memory_space=pl.ANY)
    columns = flat[0].shape[1]
    return pl.pallas_call(
        functools.partial(weight_grad_kernel, planes=planes, blocks=blocks),
        in_specs=[pl.BlockSpec(memory_space=pltpu.SMEM)] + [hbm] * (1 + len(flat)),
        out_specs=[hbm] * 3,
        out_shape=[jax.ShapeDtypeStruct(s, f32) for s in shapes],
        scratch_shapes=[
            pltpu.VMEM((total, width), bf16),
            pltpu.VMEM((total, columns), bf16),
            pltpu.VMEM((total, columns), bf16),
        ]
        + [pltpu.VMEM((2, tile, s[1]), f32) for s in shapes]
        + [pltpu.SemaphoreType.DMA((1 + 2 * blocks,)), pltpu.SemaphoreType.DMA((2, 3))],
        cost_estimate=pl.CostEstimate(flops=4 * total * width * columns, bytes_accessed=8 * total * width, transcendentals=0),
    )(plane.astype(jnp.int32).reshape(1), x, *flat)


def place_kernel(at_ref, *refs):
    pieces, out_ref, sems = refs[:-2], refs[-2], refs[-1]
    rows = pieces[0].shape[0]
    moves = [
        pltpu.make_async_copy(piece, out_ref.at[pl.ds(pl.multiple_of(at_ref[n] * rows, rows), rows)], sems.at[n])
        for n, piece in enumerate(pieces)
    ]
    for move in moves:
        move.start()
    for move in moves:
        move.wait()


def place_pieces(slots, pieces):
    rows, width = pieces[0].shape
    return pl.pallas_call(
        place_kernel,
        in_specs=[pl.BlockSpec(memory_space=pltpu.SMEM)] + [pl.BlockSpec(memory_space=pl.ANY)] * len(pieces),
        out_specs=pl.BlockSpec(memory_space=pltpu.VMEM),
        out_shape=jax.ShapeDtypeStruct((rows * len(pieces), width), pieces[0].dtype),
        scratch_shapes=[pltpu.SemaphoreType.DMA((len(pieces),))],
        cost_estimate=pl.CostEstimate(flops=0, bytes_accessed=4 * rows * width * len(pieces), transcendentals=0),
    )(slots, *pieces)


def stationary_body(sizes, *arrays):
    return stationary(sizes, *arrays)


def stationary(sizes, layer_input, query_weight, key_weight, value_weight, out_grad, doc_ids):
    planes, across, cores = sizes
    spread = across * cores
    f32, bf16 = jnp.float32, jnp.bfloat16
    tok, width = layer_input.shape
    total = tok * planes
    half_q, half_k = query_weight.shape[1] // 2, key_weight.shape[1] // 2
    plane = lax.axis_index("srv")
    side, core = lax.axis_index("hid"), lax.axis_index("rep")
    last = planes - 1
    blocks = planes
    near_left = plane < planes // 2
    is_end = (plane == 0) | (plane == last)
    trio = ("srv", "hid", "rep")
    pairs = [(t, f) for t in range(planes) for f in range(spread)]
    straight = [(t * spread + f, f * spread + t) for t, f in pairs]
    crossed = [(t * spread + f, (f + cores) % spread * spread + t) for t, f in pairs]

    def climb(early):
        moves = []
        for t, f in pairs:
            x = f // cores
            target = f if (t % 2 == 0) == early else (f + cores) % spread
            moves.append((t * spread + f, target * spread + x * cores + t * cores // planes))
        return moves

    rise, fall = climb(True), climb(False)
    outer = [(0, 1), (1, 0), (last - 1, last), (last, last - 1)]
    line = [[(k, k + 1), (last - k, last - k - 1)] for k in range(last)]
    far_at, near_at = jnp.where(near_left, 1, 0), jnp.where(near_left, 0, 1)

    def part(array, at, size):
        return lax.dynamic_slice_in_dim(array, at * size, size, 1)

    pair_weight = lambda at: jnp.concatenate([part(key_weight, at, half_k), part(value_weight, at, half_k)], axis=1)
    wp_near, wp_far = pair_weight(near_at), pair_weight(far_at)
    wq_near, wq_far = part(query_weight, near_at, half_q), part(query_weight, far_at, half_q)
    g_near, g_far = part(out_grad, near_at, half_q), part(out_grad, far_at, half_q)
    begins = jnp.sum((doc_ids[None, :] < doc_ids[:, None]).astype(jnp.int32), axis=1).reshape(1, total)
    flags = jnp.stack([is_end, plane == 0]).astype(jnp.int32)

    part_rows = tok // across
    mine = lax.dynamic_slice_in_dim(layer_input, side * part_rows, part_rows, 0)
    other = lax.dynamic_slice_in_dim(layer_input, (1 - side) * part_rows, part_rows, 0)
    other = swap(other, "hid", across)
    even_plane = plane % 2 == 0
    up = lax.ppermute(jnp.where(even_plane, mine, other), trio, rise)
    down = lax.ppermute(jnp.where(even_plane, other, mine), trio, fall)
    wp_near, wp_far, wq_near, wq_far, g_near, g_far, begins, flags, up = lax.optimization_barrier(
        (wp_near, wp_far, wq_near, wq_far, g_near, g_far, begins, flags, up)
    )
    straight_first = jnp.where(side == plane // cores, 0, 1)
    held = planes // cores
    slots, pieces = [], []
    slot = lambda owner, which, half: (owner * held + which) * across + half
    for piece, which in ((up, straight_first), (down, 1 - straight_first)):
        turned = swap(piece, "hid", across)
        mate = swap(piece, "rep", cores)
        turned_mate = swap(turned, "rep", cores)
        pieces += [piece, turned, mate, turned_mate]
        slots += [slot(core, which, side), slot(core, 1 - which, 1 - side)]
        slots += [slot(1 - core, which, side), slot(1 - core, 1 - which, 1 - side)]
    slots = jnp.stack(slots).astype(jnp.int32)
    rows_all = place_pieces(slots, pieces)
    x_rows = [lax.slice_in_dim(rows_all, b * tok, (b + 1) * tok, axis=0) for b in range(planes)]

    g_next = lax.ppermute(jnp.where(is_end, g_far, g_near), "srv", outer)
    g_over = lax.ppermute(g_far, "srv", line[1])
    g_end = lax.ppermute(g_next, "srv", line[1])
    riders = {2: g_over, 3: g_end}
    g_pieces = [g_next]

    middle = total // 2
    chunks = [(rows_all[middle:], wp_far, wp_near), (rows_all[:middle], wp_far, wp_near)]
    chunks += [(x_rows[b], wq_far, wq_near) for b in range(blocks - 1, -1, -1)]
    landed = []
    for c, (x, w_far, w_near) in enumerate(chunks):
        far_part = jnp.dot(x, w_far, preferred_element_type=f32)
        near_part = jnp.dot(x, w_near, preferred_element_type=f32)
        moving = None
        for k in range(last):
            mine_now = far_part if k < planes // 2 else near_part
            if moving is not None:
                mine_now = mine_now + moving.astype(f32)
            mine_now = mine_now.astype(bf16)
            if k == 0 and c in riders:
                moving = lax.ppermute(jnp.where(is_end, mine_now, riders[c]), "srv", outer)
                g_pieces.append(moving)
            else:
                moving = lax.ppermute(mine_now, "srv", line[k])
        landed.append((near_part + moving.astype(f32)).astype(bf16) if c < 2 else (near_part, moving))

    pairs_at = [(landed[1], b * tok) if b < blocks // 2 else (landed[0], b * tok - middle) for b in range(blocks)]
    all_hops = [None] * blocks
    near_q, far_q, near_kv, far_kv = [[None] * blocks for _ in range(4)]
    sums = [None] * blocks
    lead = 2 * half_k
    g_near, *g_pieces, _ = lax.optimization_barrier((g_near, *g_pieces, landed[0]))
    for b in range(blocks - 1, -1, -1):
        g_first = g_pieces[b - 1] if b > 0 else g_near
        g_last = g_pieces[last - b - 1] if b < last else g_near
        fresh_q, moved_q = landed[2 + blocks - 1 - b]
        local = attend_block(flags, begins, pairs_at, fresh_q, moved_q, g_first, g_last, sums, b, middle // tok)
        hops = [local]
        for k in range(last):
            hops.append(lax.ppermute(hops[k], "srv", line[k]))
        all_hops[b] = hops
        near = jnp.where(is_end, local, hops[1])
        far = jnp.where(is_end, hops[3], hops[2])
        near_q[b], far_q[b], near_kv[b], far_kv[b] = near[:, lead:], far[:, lead:], near[:, :lead], far[:, :lead]

    nt = (((1,), (1,)), ((), ()))
    times = lambda a, w: lax.dot_general(a, w, nt, preferred_element_type=f32)
    terms = []
    for b in range(blocks):
        near_term = times(near_q[b], wq_near) + times(near_kv[b], wp_near)
        terms.append(near_term + times(far_q[b], wq_far) + times(far_kv[b], wp_far))
    summed = []
    for i in range(blocks // cores):
        even, odd = terms[cores * i], terms[cores * i + 1]
        theirs = jnp.where(core == 0, odd, even).astype(bf16)
        ours = jnp.where(core == 0, even, odd)
        summed.append((ours + swap(theirs, "rep", cores).astype(f32)).astype(bf16))
    parts = []
    for i, block in reversed(list(enumerate(summed))):
        for x in range(across):
            home = [(a, b) for a, b in (straight if x == i else crossed) if a % spread // cores == x]
            parts.append(lax.ppermute(block, trio, home).astype(f32))
    input_grad = functools.reduce(jnp.add, parts).astype(bf16)

    shapes = [(width, w.shape[1]) for w in (query_weight, key_weight, value_weight)]
    outs = weight_grads(plane, rows_all, all_hops, planes, shapes)
    return (input_grad, *outs)


def solution(mesh):
    in_specs = (
        P(("groups", "srv"), ("hid", "rep")),
        P("srv", ("hid", "rep")),
        P("srv", ("hid", "rep")),
        P("srv", ("hid", "rep")),
        P(("groups", "srv"), ("hid", "rep")),
        P("groups"),
    )
    out_specs = (
        P(("groups", "srv"), ("hid", "rep")),
        P(("groups", "srv"), ("hid", "rep")),
        P(("groups", "srv"), ("hid", "rep")),
        P(("groups", "srv"), ("hid", "rep")),
    )
    sizes = (mesh.shape["srv"], mesh.shape["hid"], mesh.shape["rep"])
    split = HK // (sizes[1] * sizes[2])
    fits = sizes[0] == sizes[1] * sizes[2] and sizes[1] == 2 and sizes[2] == 2 and split == 2
    chosen = functools.partial(stationary_body, sizes) if fits else body
    return jax.shard_map(chosen, mesh=mesh, in_specs=in_specs, out_specs=out_specs, check_vma=False)
```

```python
import functools

import jax
import jax.numpy as jnp
from jax import lax
from jax.experimental import pallas as pl
from jax.experimental.pallas import tpu as pltpu
from jax.sharding import PartitionSpec as P


HQ = 32
HK = 8
DH = 128
BLOCK = 128


NEGATIVE = -1e30


def attend(queries, cotangent, keys_all, values_all, doc_ids, block_id, carried):
    row_count = queries.shape[0]
    factor_scale = queries.shape[-1] ** (-0.5)
    offsets = jnp.arange(row_count, dtype=jnp.int32)
    query_pos = block_id * row_count + offsets
    query_doc = lax.dynamic_slice_in_dim(doc_ids, block_id * row_count, row_count)
    doc_start = jnp.sum((doc_ids < query_doc[0]).astype(jnp.int32))
    lowest = doc_start // row_count
    highest = jnp.where(True, block_id + 1, lowest)

    def scores_at(key_block):
        key_rows = lax.dynamic_slice_in_dim(keys_all, key_block * row_count, row_count, 0)
        value_rows = lax.dynamic_slice_in_dim(values_all, key_block * row_count, row_count, 0)
        key_doc = lax.dynamic_slice_in_dim(doc_ids, key_block * row_count, row_count)
        key_pos = key_block * row_count + offsets
        allowed = (key_doc[None, :] == query_doc[:, None]) & (
            key_pos[None, :] <= query_pos[:, None]
        )
        logits = (
            jnp.einsum("qgnd,kgd->gnqk", queries, key_rows, preferred_element_type=jnp.float32)
            * factor_scale
        )
        logits = jnp.where(allowed, logits, NEGATIVE)
        slopes = jnp.einsum(
            "qgnd,kgd->gnqk", cotangent, value_rows, preferred_element_type=jnp.float32
        )
        return (key_rows, allowed, logits, slopes)

    def first_pass(key_block, loop_state):
        row_peak, row_total, row_inner = loop_state
        _, allowed, logits, slopes = scores_at(key_block)
        new_peak = jnp.maximum(row_peak, jnp.max(logits, axis=-1))
        weights = jnp.where(allowed, jnp.exp(logits - new_peak[..., None]), 0.0)
        factor = jnp.exp(row_peak - new_peak)
        row_total = row_total * factor + jnp.sum(weights, axis=-1)
        row_inner = row_inner * factor + jnp.sum(weights * slopes, axis=-1)
        return (new_peak, row_total, row_inner)

    stat_shape = (queries.shape[1], queries.shape[2], row_count)
    initial = (
        jnp.full(stat_shape, NEGATIVE, jnp.float32),
        jnp.zeros(stat_shape, jnp.float32),
        jnp.zeros(stat_shape, jnp.float32),
    )
    row_peak, row_total, row_inner = lax.fori_loop(lowest, highest, first_pass, initial)
    safe_total = jnp.where(True, row_total, 1.0)
    row_delta = row_inner / safe_total
    log_total = row_peak + jnp.log(safe_total)

    def second_pass(key_block, loop_state):
        query_grad, key_accum, value_accum = loop_state
        key_rows, allowed, logits, slopes = scores_at(key_block)
        attention = jnp.where(allowed, jnp.exp(logits - log_total[..., None]), 0.0)
        score_grad = (attention * (slopes - row_delta[..., None]) * factor_scale).astype(
            jnp.bfloat16
        )
        value_part = jnp.einsum(
            "gnqk,qgnd->kgd",
            attention.astype(jnp.bfloat16),
            cotangent,
            preferred_element_type=jnp.float32,
        )
        key_part = jnp.einsum(
            "gnqk,qgnd->kgd", score_grad, queries, preferred_element_type=jnp.float32
        )
        query_grad = query_grad + jnp.einsum(
            "gnqk,kgd->qgnd", score_grad, key_rows, preferred_element_type=jnp.float32
        )
        first_row = key_block * row_count
        key_accum = lax.dynamic_update_slice_in_dim(
            key_accum,
            lax.dynamic_slice_in_dim(key_accum, first_row, row_count, 0) + key_part,
            first_row,
            0,
        )
        value_accum = lax.dynamic_update_slice_in_dim(
            value_accum,
            lax.dynamic_slice_in_dim(value_accum, first_row, row_count, 0) + value_part,
            first_row,
            0,
        )
        return (query_grad, key_accum, value_accum)

    start_grad = jnp.zeros(queries.shape, jnp.float32)
    query_grad, key_accum, value_accum = lax.fori_loop(
        lowest, highest, second_pass, (start_grad, carried[0], carried[1])
    )
    return (query_grad, (key_accum, value_accum))


def body(layer_input, query_weight, key_weight, value_weight, out_grad, doc_ids):
    tok_rows = layer_input.shape[0]
    query_width = query_weight.shape[1]
    pair_width = key_weight.shape[1]
    key_heads = pair_width // DH
    group_size = HQ // HK
    block_count = tok_rows // BLOCK
    owner_id = lax.axis_index("srv")
    weights_all = lax.all_gather(
        jnp.concatenate([query_weight, key_weight, value_weight], axis=1), "srv", axis=0, tiled=True
    )
    inputs_all = lax.all_gather(layer_input, ("hid", "rep"), axis=1, tiled=True)
    projected = jnp.dot(inputs_all, weights_all, preferred_element_type=jnp.float32).astype(
        jnp.bfloat16
    )
    queries = projected[:, :query_width].reshape(block_count, BLOCK, key_heads, group_size, DH)
    keys_local = projected[:, query_width : query_width + pair_width]
    values_local = projected[:, query_width + pair_width :]
    keys_all, values_all = (
        lax.all_gather(keys_local, "srv", axis=0, tiled=True),
        lax.all_gather(values_local, "srv", axis=0, tiled=True),
    )
    total_rows = keys_all.shape[0]
    keys_all = keys_all.reshape(total_rows, key_heads, DH)
    values_all = values_all.reshape(total_rows, key_heads, DH)
    cotangent = out_grad.reshape(block_count, BLOCK, key_heads, group_size, DH)
    empty_accum = jnp.zeros((total_rows, key_heads, DH), jnp.float32)

    def own_block(position, loop_state):
        answers, carried = loop_state
        grad_q, carried = attend(
            lax.dynamic_index_in_dim(queries, position, 0, keepdims=False),
            lax.dynamic_index_in_dim(cotangent, position, 0, keepdims=False),
            keys_all,
            values_all,
            doc_ids,
            owner_id * block_count + position,
            carried,
        )
        answers = lax.dynamic_update_index_in_dim(answers, grad_q.astype(jnp.bfloat16), position, 0)
        return (answers, carried)

    answers = jnp.zeros(queries.shape, jnp.bfloat16)
    answers, carried = lax.fori_loop(
        0, block_count, own_block, (answers, (empty_accum, empty_accum))
    )
    query_grad = answers.reshape(tok_rows, query_width)
    key_accum, value_accum = carried
    key_sum, value_sum = (
        lax.psum_scatter(key_accum, "srv", scatter_dimension=0, tiled=True),
        lax.psum_scatter(value_accum, "srv", scatter_dimension=0, tiled=True),
    )
    grads_all = jnp.concatenate(
        [
            query_grad,
            key_sum.astype(jnp.bfloat16).reshape(tok_rows, pair_width),
            value_sum.astype(jnp.bfloat16).reshape(tok_rows, pair_width),
        ],
        axis=1,
    )
    input_terms = lax.dot_general(
        grads_all, weights_all, (((1,), (1,)), ((), ())), preferred_element_type=jnp.float32
    )
    input_grad = lax.psum_scatter(
        input_terms, ("hid", "rep"), scatter_dimension=1, tiled=True
    ).astype(jnp.bfloat16)
    columns = lax.all_to_all(inputs_all, "srv", split_axis=1, concat_axis=0, tiled=True)
    weight_grad = lax.dot_general(
        columns,
        lax.all_gather(grads_all, "srv", axis=0, tiled=True),
        (((0,), (0,)), ((), ())),
        preferred_element_type=jnp.float32,
    )
    return (
        input_grad,
        weight_grad[:, :query_width],
        weight_grad[:, query_width : query_width + pair_width],
        weight_grad[:, query_width + pair_width :],
    )


LOG2E = 1.4426950408889634


def swap(array, axis, size):
    return lax.ppermute(array, axis, [(i, (i + 1) % size) for i in range(size)])


def attention_kernel(flag_ref, *refs, back, heads, block_id, held, moved_at):
    count = back + 1
    start_hbm, new_hbm, old_hbm, ga_hbm, gb_hbm = refs[:5]
    pair_hbm = refs[5 : 5 + count]
    sum_hbm = refs[5 + count : 5 + count + held]
    outs = refs[5 + count + held : 6 + count + held + back]
    start_ref, new_ref, old_ref, g_ref, pair_ref, sum_ref, q_ref, out_ref, left_ref, sems = refs[6 + count + held + back :]
    block = g_ref.shape[0]
    scale = DH ** (-0.5)
    nt = (((1,), (1,)), ((), ()))
    first = block_id * block
    low = first - back * block

    @pl.when(flag_ref[0] != 0)
    def _():
        moved = old_hbm.at[:, pl.ds(moved_at, old_ref.shape[1])]
        copies = [(start_hbm, start_ref), (new_hbm, new_ref), (moved, old_ref)]
        copies += [(pair_hbm[j][0].at[pl.ds(pair_hbm[j][1], block)], pair_ref.at[j]) for j in range(count)]
        copies += [(sum_hbm[n], sum_ref.at[n]) for n in range(held)]
        moves = [pltpu.make_async_copy(a, b, sems.at[n]) for n, (a, b) in enumerate(copies)]
        for move in moves:
            move.start()
        from_first = pltpu.make_async_copy(ga_hbm, g_ref, sems.at[len(moves)])
        from_last = pltpu.make_async_copy(gb_hbm, g_ref, sems.at[len(moves)])

        @pl.when(flag_ref[1] != 0)
        def _():
            from_first.start()

        @pl.when(flag_ref[1] == 0)
        def _():
            from_last.start()

        for move in moves:
            move.wait()
        from_first.wait()
        q_ref[...] = (new_ref[...] + old_ref[...].astype(jnp.float32)).astype(q_ref.dtype)
        begin = start_ref[:, first : first + block]
        query_pos = lax.broadcasted_iota(jnp.int32, (block, block), 1)
        key_pos = lax.broadcasted_iota(jnp.int32, (block, block), 0)
        allowed = []
        for j in range(count):
            inside = key_pos >= begin - (low + j * block)
            allowed.append(inside & (key_pos <= query_pos) if j == back else inside)
        keys_t = [pair_ref[j][:, :DH].T for j in range(count)]
        dk, dv = [None] * count, [None] * count

        def front(h):
            q = q_ref[:, h * DH : (h + 1) * DH]
            g = g_ref[:, h * DH : (h + 1) * DH]
            logits, slopes = [], []
            for j in range(count):
                k, v = pair_ref[j][:, :DH], pair_ref[j][:, DH:]
                term = lax.dot_general(k, q, nt, preferred_element_type=jnp.float32) * (scale * LOG2E)
                logits.append(jnp.where(allowed[j], term, NEGATIVE))
                slopes.append(lax.dot_general(v, g, nt, preferred_element_type=jnp.float32))
            return q, g, logits, slopes

        ahead = front(0)
        for h in range(heads):
            q, g, logits, slopes = ahead
            if h + 1 < heads:
                ahead = front(h + 1)
            peak = functools.reduce(jnp.maximum, [jnp.max(t, axis=0, keepdims=True) for t in logits])
            weights = [jnp.exp2(t - peak) for t in logits]
            total = functools.reduce(jnp.add, [jnp.sum(w, axis=0, keepdims=True) for w in weights])
            inner = functools.reduce(jnp.add, [jnp.sum(w * t, axis=0, keepdims=True) for w, t in zip(weights, slopes)])
            inverse = 1.0 / total
            inner = inner * inverse
            dq = None
            for j in range(count):
                attention = weights[j] * inverse
                score = (attention * (slopes[j] - inner)).astype(jnp.bfloat16)
                value_part = jnp.dot(attention.astype(jnp.bfloat16), g, preferred_element_type=jnp.float32)
                key_part = jnp.dot(score, q, preferred_element_type=jnp.float32)
                dv[j] = value_part if dv[j] is None else dv[j] + value_part
                dk[j] = key_part if dk[j] is None else dk[j] + key_part
                part = jnp.dot(keys_t[j], score, preferred_element_type=jnp.float32)
                dq = part if dq is None else dq + part
            out_ref[:, (2 + h) * DH : (3 + h) * DH] = (dq * scale).T.astype(out_ref.dtype)
        fresh = count - held
        for j in range(count):
            new_k, new_v = dk[j] * scale, dv[j]
            if j >= fresh:
                new_k = new_k + sum_ref[j - fresh][:, :DH]
                new_v = new_v + sum_ref[j - fresh][:, DH:]
            if j == back:
                out_ref[:, :DH] = new_k.astype(out_ref.dtype)
                out_ref[:, DH : 2 * DH] = new_v.astype(out_ref.dtype)
            else:
                left_ref[j, :, :DH] = new_k
                left_ref[j, :, DH:] = new_v
        moves = [pltpu.make_async_copy(out_ref, outs[0], sems.at[0])]
        moves += [pltpu.make_async_copy(left_ref.at[j], outs[1 + j], sems.at[1 + j]) for j in range(back)]
        for move in moves:
            move.start()
        for move in moves:
            move.wait()


def attend_block(flags, begins, pairs, fresh_q, moved_q, g_first, g_last, sums, block_id, reach):
    block, width = g_first.shape
    heads = width // DH
    back = min(reach, block_id)
    low = block_id - back
    count = back + 1
    held = [sums[j] for j in range(low, block_id + 1) if sums[j] is not None]
    f32, bf16 = jnp.float32, jnp.bfloat16
    hbm = pl.BlockSpec(memory_space=pl.ANY)
    sum_shape = (block, 2 * DH)
    outs = [jax.ShapeDtypeStruct((block, 2 * DH + width), bf16)] + [jax.ShapeDtypeStruct(sum_shape, f32)] * back
    rows = [pairs[j][1] for j in range(low, block_id + 1)]
    operands = [begins, fresh_q, moved_q, g_first, g_last] + [pairs[j][0] for j in range(low, block_id + 1)] + held

    def kernel(flag_ref, *refs):
        refs = list(refs)
        refs[5 : 5 + count] = list(zip(refs[5 : 5 + count], rows))
        attention_kernel(flag_ref, *refs, back=back, heads=heads, block_id=block_id, held=len(held), moved_at=moved_q.shape[1] - width)

    results = pl.pallas_call(
        kernel,
        in_specs=[pl.BlockSpec(memory_space=pltpu.SMEM)] + [hbm] * len(operands),
        out_specs=[hbm] * len(outs),
        out_shape=outs,
        scratch_shapes=[
            pltpu.VMEM(begins.shape, jnp.int32),
            pltpu.VMEM((block, width), f32),
            pltpu.VMEM((block, width), bf16),
            pltpu.VMEM((block, width), bf16),
            pltpu.VMEM((count,) + sum_shape, bf16),
            pltpu.VMEM((max(1, len(held)),) + sum_shape, f32),
            pltpu.VMEM((block, width), bf16),
            pltpu.VMEM((block, 2 * DH + width), bf16),
            pltpu.VMEM((max(1, back),) + sum_shape, f32),
            pltpu.SemaphoreType.DMA((4 + count + len(held),)),
        ],
        cost_estimate=pl.CostEstimate(
            flops=10 * heads * DH * block * block * count, bytes_accessed=3 * block * 8 * DH, transcendentals=heads * block * block * count
        ),
    )(flags, *operands)
    for j in range(back):
        sums[low + j] = results[1 + j]
    return results[0]


def weight_grad_kernel(plane_ref, *refs, planes, blocks):
    x_hbm = refs[0]
    hops = refs[1 : 1 + blocks * planes]
    out_q, out_k, out_v = refs[1 + blocks * planes : 4 + blocks * planes]
    x_ref, left_ref, right_ref, q_ref, k_ref, v_ref, sems, out_sems = refs[4 + blocks * planes :]
    rows = left_ref.shape[0] // blocks
    tile = q_ref.shape[1]
    half_q = q_ref.shape[2] // 2
    move_x = pltpu.make_async_copy(x_hbm, x_ref, sems.at[0])
    move_x.start()

    def fetch(b, source, target, n):
        return pltpu.make_async_copy(source, target.at[pl.ds(b * rows, rows)], sems.at[n])

    for z in range(planes):

        @pl.when(plane_ref[0] == z)
        def _(z=z):
            for b in range(blocks):
                fetch(b, hops[b * planes + z], left_ref, 1 + 2 * b).start()
                fetch(b, hops[b * planes + planes - 1 - z], right_ref, 2 + 2 * b).start()

    move_x.wait()
    for b in range(blocks):
        fetch(b, hops[b * planes], left_ref, 1 + 2 * b).wait()
        fetch(b, hops[b * planes], right_ref, 2 + 2 * b).wait()

    def store(step, slot):
        at = pl.ds(pl.multiple_of(step * tile, tile), tile)
        return [
            pltpu.make_async_copy(ref.at[slot], out.at[at], out_sems.at[slot, n])
            for n, (ref, out) in enumerate(((q_ref, out_q), (k_ref, out_k), (v_ref, out_v)))
        ]

    steps = x_ref.shape[1] // tile

    def body(step, carry):
        slot = step % 2

        @pl.when(step >= 2)
        def _():
            for move in store(step, slot):
                move.wait()

        x_t = x_ref[:, pl.ds(pl.multiple_of(step * tile, tile), tile)].T
        for side, ref in enumerate((left_ref, right_ref)):
            result = jnp.dot(x_t, ref[...], preferred_element_type=jnp.float32)
            k_ref[slot, :, side * DH : (side + 1) * DH] = result[:, :DH]
            v_ref[slot, :, side * DH : (side + 1) * DH] = result[:, DH : 2 * DH]
            q_ref[slot, :, side * half_q : (side + 1) * half_q] = result[:, 2 * DH :]
        for move in store(step, slot):
            move.start()
        return carry

    lax.fori_loop(0, steps, body, 0)
    for slot in range(2):
        for move in store(slot, slot):
            move.wait()


def weight_grads(plane, x, hops, planes, shapes):
    total, width = x.shape
    blocks = len(hops)
    flat = [array for group in hops for array in group]
    tile = 256
    f32, bf16 = jnp.float32, jnp.bfloat16
    hbm = pl.BlockSpec(memory_space=pl.ANY)
    columns = flat[0].shape[1]
    return pl.pallas_call(
        functools.partial(weight_grad_kernel, planes=planes, blocks=blocks),
        in_specs=[pl.BlockSpec(memory_space=pltpu.SMEM)] + [hbm] * (1 + len(flat)),
        out_specs=[hbm] * 3,
        out_shape=[jax.ShapeDtypeStruct(s, f32) for s in shapes],
        scratch_shapes=[
            pltpu.VMEM((total, width), bf16),
            pltpu.VMEM((total, columns), bf16),
            pltpu.VMEM((total, columns), bf16),
        ]
        + [pltpu.VMEM((2, tile, s[1]), f32) for s in shapes]
        + [pltpu.SemaphoreType.DMA((1 + 2 * blocks,)), pltpu.SemaphoreType.DMA((2, 3))],
        cost_estimate=pl.CostEstimate(flops=4 * total * width * columns, bytes_accessed=8 * total * width, transcendentals=0),
    )(plane.astype(jnp.int32).reshape(1), x, *flat)


def place_kernel(at_ref, *refs):
    pieces, out_ref, sems = refs[:-2], refs[-2], refs[-1]
    rows = pieces[0].shape[0]
    moves = [
        pltpu.make_async_copy(piece, out_ref.at[pl.ds(pl.multiple_of(at_ref[n] * rows, rows), rows)], sems.at[n])
        for n, piece in enumerate(pieces)
    ]
    for move in moves:
        move.start()
    for move in moves:
        move.wait()


def place_pieces(slots, pieces):
    rows, width = pieces[0].shape
    return pl.pallas_call(
        place_kernel,
        in_specs=[pl.BlockSpec(memory_space=pltpu.SMEM)] + [pl.BlockSpec(memory_space=pl.ANY)] * len(pieces),
        out_specs=pl.BlockSpec(memory_space=pltpu.VMEM),
        out_shape=jax.ShapeDtypeStruct((rows * len(pieces), width), pieces[0].dtype),
        scratch_shapes=[pltpu.SemaphoreType.DMA((len(pieces),))],
        cost_estimate=pl.CostEstimate(flops=0, bytes_accessed=4 * rows * width * len(pieces), transcendentals=0),
    )(slots, *pieces)


def stationary_body(sizes, *arrays):
    return stationary(sizes, *arrays)


def stationary(sizes, layer_input, query_weight, key_weight, value_weight, out_grad, doc_ids):
    planes, across, cores = sizes
    spread = across * cores
    f32, bf16 = jnp.float32, jnp.bfloat16
    tok, width = layer_input.shape
    total = tok * planes
    half_q, half_k = query_weight.shape[1] // 2, key_weight.shape[1] // 2
    plane = lax.axis_index("srv")
    side, core = lax.axis_index("hid"), lax.axis_index("rep")
    last = planes - 1
    blocks = planes
    near_left = plane < planes // 2
    is_end = (plane == 0) | (plane == last)
    trio = ("srv", "hid", "rep")
    pairs = [(t, f) for t in range(planes) for f in range(spread)]
    straight = [(t * spread + f, f * spread + t) for t, f in pairs]
    crossed = [(t * spread + f, (f + cores) % spread * spread + t) for t, f in pairs]

    def climb(early):
        moves = []
        for t, f in pairs:
            x = f // cores
            target = f if (t % 2 == 0) == early else (f + cores) % spread
            moves.append((t * spread + f, target * spread + x * cores + t * cores // planes))
        return moves

    rise, fall = climb(True), climb(False)
    outer = [(0, 1), (1, 0), (last - 1, last), (last, last - 1)]
    line = [[(k, k + 1), (last - k, last - k - 1)] for k in range(last)]
    far_at, near_at = jnp.where(near_left, 1, 0), jnp.where(near_left, 0, 1)

    def part(array, at, size):
        return lax.dynamic_slice_in_dim(array, at * size, size, 1)

    pair_weight = lambda at: jnp.concatenate([part(key_weight, at, half_k), part(value_weight, at, half_k)], axis=1)
    wp_near, wp_far = pair_weight(near_at), pair_weight(far_at)
    wq_near, wq_far = part(query_weight, near_at, half_q), part(query_weight, far_at, half_q)
    g_near, g_far = part(out_grad, near_at, half_q), part(out_grad, far_at, half_q)
    begins = jnp.sum((doc_ids[None, :] < doc_ids[:, None]).astype(jnp.int32), axis=1).reshape(1, total)
    flags = jnp.stack([is_end, plane == 0]).astype(jnp.int32)

    part_rows = tok // across
    mine = lax.dynamic_slice_in_dim(layer_input, side * part_rows, part_rows, 0)
    other = lax.dynamic_slice_in_dim(layer_input, (1 - side) * part_rows, part_rows, 0)
    other = swap(other, "hid", across)
    even_plane = plane % 2 == 0
    up = lax.ppermute(jnp.where(even_plane, mine, other), trio, rise)
    down = lax.ppermute(jnp.where(even_plane, other, mine), trio, fall)
    wp_near, wp_far, wq_near, wq_far, g_near, g_far, begins, flags, up = lax.optimization_barrier(
        (wp_near, wp_far, wq_near, wq_far, g_near, g_far, begins, flags, up)
    )
    straight_first = jnp.where(side == plane // cores, 0, 1)
    held = planes // cores
    slots, pieces = [], []
    slot = lambda owner, which, half: (owner * held + which) * across + half
    for piece, which in ((up, straight_first), (down, 1 - straight_first)):
        turned = swap(piece, "hid", across)
        mate = swap(piece, "rep", cores)
        turned_mate = swap(turned, "rep", cores)
        pieces += [piece, turned, mate, turned_mate]
        slots += [slot(core, which, side), slot(core, 1 - which, 1 - side)]
        slots += [slot(1 - core, which, side), slot(1 - core, 1 - which, 1 - side)]
    slots = jnp.stack(slots).astype(jnp.int32)
    rows_all = place_pieces(slots, pieces)
    x_rows = [lax.slice_in_dim(rows_all, b * tok, (b + 1) * tok, axis=0) for b in range(planes)]

    g_next = lax.ppermute(jnp.where(is_end, g_far, g_near), "srv", outer)
    g_over = lax.ppermute(g_far, "srv", line[1])
    g_end = lax.ppermute(g_next, "srv", line[1])
    riders = {2: g_over, 3: g_end}
    g_pieces = [g_next]

    middle = total // 2
    chunks = [(rows_all[middle:], wp_far, wp_near), (rows_all[:middle], wp_far, wp_near)]
    chunks += [(x_rows[b], wq_far, wq_near) for b in range(blocks - 1, -1, -1)]
    landed = []
    for c, (x, w_far, w_near) in enumerate(chunks):
        far_part = jnp.dot(x, w_far, preferred_element_type=f32)
        near_part = jnp.dot(x, w_near, preferred_element_type=f32)
        moving = None
        for k in range(last):
            mine_now = far_part if k < planes // 2 else near_part
            if moving is not None:
                mine_now = mine_now + moving.astype(f32)
            mine_now = mine_now.astype(bf16)
            if k == 0 and c in riders:
                moving = lax.ppermute(jnp.where(is_end, mine_now, riders[c]), "srv", outer)
                g_pieces.append(moving)
            elif c == len(chunks) - 1 and k == last - 1:
                moving = mine_now
            else:
                moving = lax.ppermute(mine_now, "srv", line[k])
        landed.append((near_part + moving.astype(f32)).astype(bf16) if c < 2 else (near_part, moving))

    pairs_at = [(landed[1], b * tok) if b < blocks // 2 else (landed[0], b * tok - middle) for b in range(blocks)]
    all_hops = [None] * blocks
    near_q, far_q, near_kv, far_kv = [[None] * blocks for _ in range(4)]
    sums = [None] * blocks
    lead = 2 * half_k
    g_near, *g_pieces, _ = lax.optimization_barrier((g_near, *g_pieces, landed[0]))
    for b in range(blocks - 1, -1, -1):
        g_first = g_pieces[b - 1] if b > 0 else g_near
        g_last = g_pieces[last - b - 1] if b < last else g_near
        fresh_q, moved_q = landed[2 + blocks - 1 - b]
        local = attend_block(flags, begins, pairs_at, fresh_q, moved_q, g_first, g_last, sums, b, middle // tok)
        hops = [local]
        for k in range(last):
            if b == blocks - 1 and k == 0:
                fresh_q, moved_q = landed[-1]
                wider = jnp.pad(moved_q, ((0, 0), (lead, 0)))
                hops.append(lax.ppermute(jnp.where(is_end, local, wider), "srv", outer))
                landed[-1] = (fresh_q, hops[1])
            else:
                hops.append(lax.ppermute(hops[k], "srv", line[k]))
        all_hops[b] = hops
        near = jnp.where(is_end, local, hops[1])
        far = jnp.where(is_end, hops[3], hops[2])
        near_q[b], far_q[b], near_kv[b], far_kv[b] = near[:, lead:], far[:, lead:], near[:, :lead], far[:, :lead]

    nt = (((1,), (1,)), ((), ()))
    times = lambda a, w: lax.dot_general(a, w, nt, preferred_element_type=f32)
    terms = []
    for b in range(blocks):
        near_term = times(near_q[b], wq_near) + times(near_kv[b], wp_near)
        terms.append(near_term + times(far_q[b], wq_far) + times(far_kv[b], wp_far))
    summed = []
    for i in range(blocks // cores):
        even, odd = terms[cores * i], terms[cores * i + 1]
        theirs = jnp.where(core == 0, odd, even).astype(bf16)
        ours = jnp.where(core == 0, even, odd)
        summed.append((ours + swap(theirs, "rep", cores).astype(f32)).astype(bf16))
    parts = []
    for i, block in reversed(list(enumerate(summed))):
        for x in range(across):
            home = [(a, b) for a, b in (straight if x == i else crossed) if a % spread // cores == x]
            parts.append(lax.ppermute(block, trio, home).astype(f32))
    input_grad = functools.reduce(jnp.add, parts).astype(bf16)

    shapes = [(width, w.shape[1]) for w in (query_weight, key_weight, value_weight)]
    outs = weight_grads(plane, rows_all, all_hops, planes, shapes)
    return (input_grad, *outs)


def solution(mesh):
    in_specs = (
        P(("groups", "srv"), ("hid", "rep")),
        P("srv", ("hid", "rep")),
        P("srv", ("hid", "rep")),
        P("srv", ("hid", "rep")),
        P(("groups", "srv"), ("hid", "rep")),
        P("groups"),
    )
    out_specs = (
        P(("groups", "srv"), ("hid", "rep")),
        P(("groups", "srv"), ("hid", "rep")),
        P(("groups", "srv"), ("hid", "rep")),
        P(("groups", "srv"), ("hid", "rep")),
    )
    sizes = (mesh.shape["srv"], mesh.shape["hid"], mesh.shape["rep"])
    split = HK // (sizes[1] * sizes[2])
    fits = sizes[0] == sizes[1] * sizes[2] and sizes[1] == 2 and sizes[2] == 2 and split == 2
    chosen = functools.partial(stationary_body, sizes) if fits else body
    return jax.shard_map(chosen, mesh=mesh, in_specs=in_specs, out_specs=out_specs, check_vma=False)
```

```python
import functools

import jax
import jax.numpy as jnp
from jax import lax
from jax.experimental import pallas as pl
from jax.experimental.pallas import tpu as pltpu
from jax.sharding import PartitionSpec as P


HQ = 32
HK = 8
DH = 128
BLOCK = 128


NEGATIVE = -1e30


def attend(queries, cotangent, keys_all, values_all, doc_ids, block_id, carried):
    row_count = queries.shape[0]
    factor_scale = queries.shape[-1] ** (-0.5)
    offsets = jnp.arange(row_count, dtype=jnp.int32)
    query_pos = block_id * row_count + offsets
    query_doc = lax.dynamic_slice_in_dim(doc_ids, block_id * row_count, row_count)
    doc_start = jnp.sum((doc_ids < query_doc[0]).astype(jnp.int32))
    lowest = doc_start // row_count
    highest = jnp.where(True, block_id + 1, lowest)

    def scores_at(key_block):
        key_rows = lax.dynamic_slice_in_dim(keys_all, key_block * row_count, row_count, 0)
        value_rows = lax.dynamic_slice_in_dim(values_all, key_block * row_count, row_count, 0)
        key_doc = lax.dynamic_slice_in_dim(doc_ids, key_block * row_count, row_count)
        key_pos = key_block * row_count + offsets
        allowed = (key_doc[None, :] == query_doc[:, None]) & (
            key_pos[None, :] <= query_pos[:, None]
        )
        logits = (
            jnp.einsum("qgnd,kgd->gnqk", queries, key_rows, preferred_element_type=jnp.float32)
            * factor_scale
        )
        logits = jnp.where(allowed, logits, NEGATIVE)
        slopes = jnp.einsum(
            "qgnd,kgd->gnqk", cotangent, value_rows, preferred_element_type=jnp.float32
        )
        return (key_rows, allowed, logits, slopes)

    def first_pass(key_block, loop_state):
        row_peak, row_total, row_inner = loop_state
        _, allowed, logits, slopes = scores_at(key_block)
        new_peak = jnp.maximum(row_peak, jnp.max(logits, axis=-1))
        weights = jnp.where(allowed, jnp.exp(logits - new_peak[..., None]), 0.0)
        factor = jnp.exp(row_peak - new_peak)
        row_total = row_total * factor + jnp.sum(weights, axis=-1)
        row_inner = row_inner * factor + jnp.sum(weights * slopes, axis=-1)
        return (new_peak, row_total, row_inner)

    stat_shape = (queries.shape[1], queries.shape[2], row_count)
    initial = (
        jnp.full(stat_shape, NEGATIVE, jnp.float32),
        jnp.zeros(stat_shape, jnp.float32),
        jnp.zeros(stat_shape, jnp.float32),
    )
    row_peak, row_total, row_inner = lax.fori_loop(lowest, highest, first_pass, initial)
    safe_total = jnp.where(True, row_total, 1.0)
    row_delta = row_inner / safe_total
    log_total = row_peak + jnp.log(safe_total)

    def second_pass(key_block, loop_state):
        query_grad, key_accum, value_accum = loop_state
        key_rows, allowed, logits, slopes = scores_at(key_block)
        attention = jnp.where(allowed, jnp.exp(logits - log_total[..., None]), 0.0)
        score_grad = (attention * (slopes - row_delta[..., None]) * factor_scale).astype(
            jnp.bfloat16
        )
        value_part = jnp.einsum(
            "gnqk,qgnd->kgd",
            attention.astype(jnp.bfloat16),
            cotangent,
            preferred_element_type=jnp.float32,
        )
        key_part = jnp.einsum(
            "gnqk,qgnd->kgd", score_grad, queries, preferred_element_type=jnp.float32
        )
        query_grad = query_grad + jnp.einsum(
            "gnqk,kgd->qgnd", score_grad, key_rows, preferred_element_type=jnp.float32
        )
        first_row = key_block * row_count
        key_accum = lax.dynamic_update_slice_in_dim(
            key_accum,
            lax.dynamic_slice_in_dim(key_accum, first_row, row_count, 0) + key_part,
            first_row,
            0,
        )
        value_accum = lax.dynamic_update_slice_in_dim(
            value_accum,
            lax.dynamic_slice_in_dim(value_accum, first_row, row_count, 0) + value_part,
            first_row,
            0,
        )
        return (query_grad, key_accum, value_accum)

    start_grad = jnp.zeros(queries.shape, jnp.float32)
    query_grad, key_accum, value_accum = lax.fori_loop(
        lowest, highest, second_pass, (start_grad, carried[0], carried[1])
    )
    return (query_grad, (key_accum, value_accum))


def body(layer_input, query_weight, key_weight, value_weight, out_grad, doc_ids):
    tok_rows = layer_input.shape[0]
    query_width = query_weight.shape[1]
    pair_width = key_weight.shape[1]
    key_heads = pair_width // DH
    group_size = HQ // HK
    block_count = tok_rows // BLOCK
    owner_id = lax.axis_index("srv")
    weights_all = lax.all_gather(
        jnp.concatenate([query_weight, key_weight, value_weight], axis=1), "srv", axis=0, tiled=True
    )
    inputs_all = lax.all_gather(layer_input, ("hid", "rep"), axis=1, tiled=True)
    projected = jnp.dot(inputs_all, weights_all, preferred_element_type=jnp.float32).astype(
        jnp.bfloat16
    )
    queries = projected[:, :query_width].reshape(block_count, BLOCK, key_heads, group_size, DH)
    keys_local = projected[:, query_width : query_width + pair_width]
    values_local = projected[:, query_width + pair_width :]
    keys_all, values_all = (
        lax.all_gather(keys_local, "srv", axis=0, tiled=True),
        lax.all_gather(values_local, "srv", axis=0, tiled=True),
    )
    total_rows = keys_all.shape[0]
    keys_all = keys_all.reshape(total_rows, key_heads, DH)
    values_all = values_all.reshape(total_rows, key_heads, DH)
    cotangent = out_grad.reshape(block_count, BLOCK, key_heads, group_size, DH)
    empty_accum = jnp.zeros((total_rows, key_heads, DH), jnp.float32)

    def own_block(position, loop_state):
        answers, carried = loop_state
        grad_q, carried = attend(
            lax.dynamic_index_in_dim(queries, position, 0, keepdims=False),
            lax.dynamic_index_in_dim(cotangent, position, 0, keepdims=False),
            keys_all,
            values_all,
            doc_ids,
            owner_id * block_count + position,
            carried,
        )
        answers = lax.dynamic_update_index_in_dim(answers, grad_q.astype(jnp.bfloat16), position, 0)
        return (answers, carried)

    answers = jnp.zeros(queries.shape, jnp.bfloat16)
    answers, carried = lax.fori_loop(
        0, block_count, own_block, (answers, (empty_accum, empty_accum))
    )
    query_grad = answers.reshape(tok_rows, query_width)
    key_accum, value_accum = carried
    key_sum, value_sum = (
        lax.psum_scatter(key_accum, "srv", scatter_dimension=0, tiled=True),
        lax.psum_scatter(value_accum, "srv", scatter_dimension=0, tiled=True),
    )
    grads_all = jnp.concatenate(
        [
            query_grad,
            key_sum.astype(jnp.bfloat16).reshape(tok_rows, pair_width),
            value_sum.astype(jnp.bfloat16).reshape(tok_rows, pair_width),
        ],
        axis=1,
    )
    input_terms = lax.dot_general(
        grads_all, weights_all, (((1,), (1,)), ((), ())), preferred_element_type=jnp.float32
    )
    input_grad = lax.psum_scatter(
        input_terms, ("hid", "rep"), scatter_dimension=1, tiled=True
    ).astype(jnp.bfloat16)
    columns = lax.all_to_all(inputs_all, "srv", split_axis=1, concat_axis=0, tiled=True)
    weight_grad = lax.dot_general(
        columns,
        lax.all_gather(grads_all, "srv", axis=0, tiled=True),
        (((0,), (0,)), ((), ())),
        preferred_element_type=jnp.float32,
    )
    return (
        input_grad,
        weight_grad[:, :query_width],
        weight_grad[:, query_width : query_width + pair_width],
        weight_grad[:, query_width + pair_width :],
    )


LOG2E = 1.4426950408889634


def swap(array, axis, size):
    return lax.ppermute(array, axis, [(i, (i + 1) % size) for i in range(size)])


def attention_kernel(flag_ref, *refs, back, heads, block_id, held, moved_at, relays):
    count = back + 1
    start_hbm, new_hbm, old_hbm, ga_hbm, gb_hbm = refs[:5]
    pair_hbm = refs[5 : 5 + count]
    sum_hbm = refs[5 + count : 5 + count + held]
    relay_hbm = refs[5 + count + held : 5 + count + held + relays]
    outs = refs[5 + count + held + relays : 6 + count + held + relays + back]
    start_ref, new_ref, old_ref, g_ref, pair_ref, sum_ref, q_ref, out_ref, left_ref, sems = refs[-10:]
    block = g_ref.shape[0]
    scale = DH ** (-0.5)
    nt = (((1,), (1,)), ((), ()))
    first = block_id * block
    low = first - back * block

    for relay in relay_hbm:
        @pl.when(flag_ref[0] == 0)
        def _(relay=relay):
            take = pltpu.make_async_copy(relay, old_ref, sems.at[0])
            take.start()
            take.wait()
            give = pltpu.make_async_copy(old_ref, outs[0].at[:, pl.ds(2 * DH, old_ref.shape[1])], sems.at[0])
            give.start()
            give.wait()

    @pl.when(flag_ref[0] != 0)
    def _():
        moved = old_hbm.at[:, pl.ds(moved_at, old_ref.shape[1])]
        copies = [(start_hbm, start_ref), (new_hbm, new_ref), (moved, old_ref)]
        copies += [(pair_hbm[j][0].at[pl.ds(pair_hbm[j][1], block)], pair_ref.at[j]) for j in range(count)]
        copies += [(sum_hbm[n], sum_ref.at[n]) for n in range(held)]
        moves = [pltpu.make_async_copy(a, b, sems.at[n]) for n, (a, b) in enumerate(copies)]
        for move in moves:
            move.start()
        from_first = pltpu.make_async_copy(ga_hbm, g_ref, sems.at[len(moves)])
        from_last = pltpu.make_async_copy(gb_hbm, g_ref, sems.at[len(moves)])

        @pl.when(flag_ref[1] != 0)
        def _():
            from_first.start()

        @pl.when(flag_ref[1] == 0)
        def _():
            from_last.start()

        for move in moves:
            move.wait()
        from_first.wait()
        q_ref[...] = (new_ref[...] + old_ref[...].astype(jnp.float32)).astype(q_ref.dtype)
        begin = start_ref[:, first : first + block]
        query_pos = lax.broadcasted_iota(jnp.int32, (block, block), 1)
        key_pos = lax.broadcasted_iota(jnp.int32, (block, block), 0)
        allowed = []
        for j in range(count):
            inside = key_pos >= begin - (low + j * block)
            allowed.append(inside & (key_pos <= query_pos) if j == back else inside)
        keys_t = [pair_ref[j][:, :DH].T for j in range(count)]
        dk, dv = [None] * count, [None] * count

        def front(h):
            q = q_ref[:, h * DH : (h + 1) * DH]
            g = g_ref[:, h * DH : (h + 1) * DH]
            logits, slopes = [], []
            for j in range(count):
                k, v = pair_ref[j][:, :DH], pair_ref[j][:, DH:]
                term = lax.dot_general(k, q, nt, preferred_element_type=jnp.float32) * (scale * LOG2E)
                logits.append(jnp.where(allowed[j], term, NEGATIVE))
                slopes.append(lax.dot_general(v, g, nt, preferred_element_type=jnp.float32))
            return q, g, logits, slopes

        ahead = front(0)
        for h in range(heads):
            q, g, logits, slopes = ahead
            if h + 1 < heads:
                ahead = front(h + 1)
            peak = functools.reduce(jnp.maximum, [jnp.max(t, axis=0, keepdims=True) for t in logits])
            weights = [jnp.exp2(t - peak) for t in logits]
            total = functools.reduce(jnp.add, [jnp.sum(w, axis=0, keepdims=True) for w in weights])
            inner = functools.reduce(jnp.add, [jnp.sum(w * t, axis=0, keepdims=True) for w, t in zip(weights, slopes)])
            inverse = 1.0 / total
            inner = inner * inverse
            dq = None
            for j in range(count):
                attention = weights[j] * inverse
                score = (attention * (slopes[j] - inner)).astype(jnp.bfloat16)
                value_part = jnp.dot(attention.astype(jnp.bfloat16), g, preferred_element_type=jnp.float32)
                key_part = jnp.dot(score, q, preferred_element_type=jnp.float32)
                dv[j] = value_part if dv[j] is None else dv[j] + value_part
                dk[j] = key_part if dk[j] is None else dk[j] + key_part
                part = jnp.dot(keys_t[j], score, preferred_element_type=jnp.float32)
                dq = part if dq is None else dq + part
            out_ref[:, (2 + h) * DH : (3 + h) * DH] = (dq * scale).T.astype(out_ref.dtype)
        fresh = count - held
        for j in range(count):
            new_k, new_v = dk[j] * scale, dv[j]
            if j >= fresh:
                new_k = new_k + sum_ref[j - fresh][:, :DH]
                new_v = new_v + sum_ref[j - fresh][:, DH:]
            if j == back:
                out_ref[:, :DH] = new_k.astype(out_ref.dtype)
                out_ref[:, DH : 2 * DH] = new_v.astype(out_ref.dtype)
            else:
                left_ref[j, :, :DH] = new_k
                left_ref[j, :, DH:] = new_v
        moves = [pltpu.make_async_copy(out_ref, outs[0], sems.at[0])]
        moves += [pltpu.make_async_copy(left_ref.at[j], outs[1 + j], sems.at[1 + j]) for j in range(back)]
        for move in moves:
            move.start()
        for move in moves:
            move.wait()


def attend_block(flags, begins, pairs, fresh_q, moved_q, g_first, g_last, sums, block_id, reach, relay):
    block, width = g_first.shape
    heads = width // DH
    back = min(reach, block_id)
    low = block_id - back
    count = back + 1
    held = [sums[j] for j in range(low, block_id + 1) if sums[j] is not None]
    f32, bf16 = jnp.float32, jnp.bfloat16
    hbm = pl.BlockSpec(memory_space=pl.ANY)
    sum_shape = (block, 2 * DH)
    outs = [jax.ShapeDtypeStruct((block, 2 * DH + width), bf16)] + [jax.ShapeDtypeStruct(sum_shape, f32)] * back
    rows = [pairs[j][1] for j in range(low, block_id + 1)]
    operands = [begins, fresh_q, moved_q, g_first, g_last] + [pairs[j][0] for j in range(low, block_id + 1)] + held + relay

    def kernel(flag_ref, *refs):
        refs = list(refs)
        refs[5 : 5 + count] = list(zip(refs[5 : 5 + count], rows))
        attention_kernel(flag_ref, *refs, back=back, heads=heads, block_id=block_id, held=len(held), moved_at=moved_q.shape[1] - width, relays=len(relay))

    results = pl.pallas_call(
        kernel,
        in_specs=[pl.BlockSpec(memory_space=pltpu.SMEM)] + [hbm] * len(operands),
        out_specs=[hbm] * len(outs),
        out_shape=outs,
        scratch_shapes=[
            pltpu.VMEM(begins.shape, jnp.int32),
            pltpu.VMEM((block, width), f32),
            pltpu.VMEM((block, width), bf16),
            pltpu.VMEM((block, width), bf16),
            pltpu.VMEM((count,) + sum_shape, bf16),
            pltpu.VMEM((max(1, len(held)),) + sum_shape, f32),
            pltpu.VMEM((block, width), bf16),
            pltpu.VMEM((block, 2 * DH + width), bf16),
            pltpu.VMEM((max(1, back),) + sum_shape, f32),
            pltpu.SemaphoreType.DMA((4 + count + len(held),)),
        ],
        cost_estimate=pl.CostEstimate(
            flops=10 * heads * DH * block * block * count, bytes_accessed=3 * block * 8 * DH, transcendentals=heads * block * block * count
        ),
    )(flags, *operands)
    for j in range(back):
        sums[low + j] = results[1 + j]
    return results[0]


def weight_grad_kernel(plane_ref, *refs, planes, blocks):
    x_hbm = refs[0]
    hops = refs[1 : 1 + blocks * planes]
    out_q, out_k, out_v = refs[1 + blocks * planes : 4 + blocks * planes]
    x_ref, left_ref, right_ref, q_ref, k_ref, v_ref, sems, out_sems = refs[4 + blocks * planes :]
    rows = left_ref.shape[0] // blocks
    tile = q_ref.shape[1]
    half_q = q_ref.shape[2] // 2
    move_x = pltpu.make_async_copy(x_hbm, x_ref, sems.at[0])
    move_x.start()

    def fetch(b, source, target, n):
        return pltpu.make_async_copy(source, target.at[pl.ds(b * rows, rows)], sems.at[n])

    for z in range(planes):

        @pl.when(plane_ref[0] == z)
        def _(z=z):
            for b in range(blocks):
                fetch(b, hops[b * planes + z], left_ref, 1 + 2 * b).start()
                fetch(b, hops[b * planes + planes - 1 - z], right_ref, 2 + 2 * b).start()

    move_x.wait()
    for b in range(blocks):
        fetch(b, hops[b * planes], left_ref, 1 + 2 * b).wait()
        fetch(b, hops[b * planes], right_ref, 2 + 2 * b).wait()

    def store(step, slot):
        at = pl.ds(pl.multiple_of(step * tile, tile), tile)
        return [
            pltpu.make_async_copy(ref.at[slot], out.at[at], out_sems.at[slot, n])
            for n, (ref, out) in enumerate(((q_ref, out_q), (k_ref, out_k), (v_ref, out_v)))
        ]

    steps = x_ref.shape[1] // tile

    def body(step, carry):
        slot = step % 2

        @pl.when(step >= 2)
        def _():
            for move in store(step, slot):
                move.wait()

        x_t = x_ref[:, pl.ds(pl.multiple_of(step * tile, tile), tile)].T
        for side, ref in enumerate((left_ref, right_ref)):
            result = jnp.dot(x_t, ref[...], preferred_element_type=jnp.float32)
            k_ref[slot, :, side * DH : (side + 1) * DH] = result[:, :DH]
            v_ref[slot, :, side * DH : (side + 1) * DH] = result[:, DH : 2 * DH]
            q_ref[slot, :, side * half_q : (side + 1) * half_q] = result[:, 2 * DH :]
        for move in store(step, slot):
            move.start()
        return carry

    lax.fori_loop(0, steps, body, 0)
    for slot in range(2):
        for move in store(slot, slot):
            move.wait()


def weight_grads(plane, x, hops, planes, shapes):
    total, width = x.shape
    blocks = len(hops)
    flat = [array for group in hops for array in group]
    tile = 256
    f32, bf16 = jnp.float32, jnp.bfloat16
    hbm = pl.BlockSpec(memory_space=pl.ANY)
    columns = flat[0].shape[1]
    return pl.pallas_call(
        functools.partial(weight_grad_kernel, planes=planes, blocks=blocks),
        in_specs=[pl.BlockSpec(memory_space=pltpu.SMEM)] + [hbm] * (1 + len(flat)),
        out_specs=[hbm] * 3,
        out_shape=[jax.ShapeDtypeStruct(s, f32) for s in shapes],
        scratch_shapes=[
            pltpu.VMEM((total, width), bf16),
            pltpu.VMEM((total, columns), bf16),
            pltpu.VMEM((total, columns), bf16),
        ]
        + [pltpu.VMEM((2, tile, s[1]), f32) for s in shapes]
        + [pltpu.SemaphoreType.DMA((1 + 2 * blocks,)), pltpu.SemaphoreType.DMA((2, 3))],
        cost_estimate=pl.CostEstimate(flops=4 * total * width * columns, bytes_accessed=8 * total * width, transcendentals=0),
    )(plane.astype(jnp.int32).reshape(1), x, *flat)


def place_kernel(at_ref, *refs):
    pieces, out_ref, sems = refs[:-2], refs[-2], refs[-1]
    rows = pieces[0].shape[0]
    moves = [
        pltpu.make_async_copy(piece, out_ref.at[pl.ds(pl.multiple_of(at_ref[n] * rows, rows), rows)], sems.at[n])
        for n, piece in enumerate(pieces)
    ]
    for move in moves:
        move.start()
    for move in moves:
        move.wait()


def place_pieces(slots, pieces):
    rows, width = pieces[0].shape
    return pl.pallas_call(
        place_kernel,
        in_specs=[pl.BlockSpec(memory_space=pltpu.SMEM)] + [pl.BlockSpec(memory_space=pl.ANY)] * len(pieces),
        out_specs=pl.BlockSpec(memory_space=pltpu.VMEM),
        out_shape=jax.ShapeDtypeStruct((rows * len(pieces), width), pieces[0].dtype),
        scratch_shapes=[pltpu.SemaphoreType.DMA((len(pieces),))],
        cost_estimate=pl.CostEstimate(flops=0, bytes_accessed=4 * rows * width * len(pieces), transcendentals=0),
    )(slots, *pieces)


def stationary_body(sizes, *arrays):
    return stationary(sizes, *arrays)


def stationary(sizes, layer_input, query_weight, key_weight, value_weight, out_grad, doc_ids):
    planes, across, cores = sizes
    spread = across * cores
    f32, bf16 = jnp.float32, jnp.bfloat16
    tok, width = layer_input.shape
    total = tok * planes
    half_q, half_k = query_weight.shape[1] // 2, key_weight.shape[1] // 2
    plane = lax.axis_index("srv")
    side, core = lax.axis_index("hid"), lax.axis_index("rep")
    last = planes - 1
    blocks = planes
    near_left = plane < planes // 2
    is_end = (plane == 0) | (plane == last)
    trio = ("srv", "hid", "rep")
    pairs = [(t, f) for t in range(planes) for f in range(spread)]
    straight = [(t * spread + f, f * spread + t) for t, f in pairs]
    crossed = [(t * spread + f, (f + cores) % spread * spread + t) for t, f in pairs]

    def climb(early):
        moves = []
        for t, f in pairs:
            x = f // cores
            target = f if (t % 2 == 0) == early else (f + cores) % spread
            moves.append((t * spread + f, target * spread + x * cores + t * cores // planes))
        return moves

    rise, fall = climb(True), climb(False)
    outer = [(0, 1), (1, 0), (last - 1, last), (last, last - 1)]
    line = [[(k, k + 1), (last - k, last - k - 1)] for k in range(last)]
    far_at, near_at = jnp.where(near_left, 1, 0), jnp.where(near_left, 0, 1)

    def part(array, at, size):
        return lax.dynamic_slice_in_dim(array, at * size, size, 1)

    pair_weight = lambda at: jnp.concatenate([part(key_weight, at, half_k), part(value_weight, at, half_k)], axis=1)
    wp_near, wp_far = pair_weight(near_at), pair_weight(far_at)
    wq_near, wq_far = part(query_weight, near_at, half_q), part(query_weight, far_at, half_q)
    g_near, g_far = part(out_grad, near_at, half_q), part(out_grad, far_at, half_q)
    begins = jnp.sum((doc_ids[None, :] < doc_ids[:, None]).astype(jnp.int32), axis=1).reshape(1, total)
    flags = jnp.stack([is_end, plane == 0]).astype(jnp.int32)

    part_rows = tok // across
    mine = lax.dynamic_slice_in_dim(layer_input, side * part_rows, part_rows, 0)
    other = lax.dynamic_slice_in_dim(layer_input, (1 - side) * part_rows, part_rows, 0)
    other = swap(other, "hid", across)
    even_plane = plane % 2 == 0
    up = lax.ppermute(jnp.where(even_plane, mine, other), trio, rise)
    down = lax.ppermute(jnp.where(even_plane, other, mine), trio, fall)
    straight_first = jnp.where(side == plane // cores, 0, 1)
    held = planes // cores
    slot = lambda owner, which, half: (owner * held + which) * across + half
    slots = []
    for which in (straight_first, 1 - straight_first):
        slots += [slot(core, which, side), slot(1 - core, which, side)]
        slots += [slot(core, 1 - which, 1 - side), slot(1 - core, 1 - which, 1 - side)]
    slots = jnp.stack(slots).astype(jnp.int32)
    wp_near, wp_far, wq_near, wq_far, g_near, g_far, begins, flags, slots, up = lax.optimization_barrier(
        (wp_near, wp_far, wq_near, wq_far, g_near, g_far, begins, flags, slots, up)
    )
    pieces = []
    for piece in (up, down):
        turned = swap(piece, "hid", across)
        mate = swap(piece, "rep", cores)
        turned_mate = swap(turned, "rep", cores)
        pieces += [piece, mate, turned, turned_mate]
    rows_all = place_pieces(slots, pieces)
    x_rows = [lax.slice_in_dim(rows_all, b * tok, (b + 1) * tok, axis=0) for b in range(planes)]

    g_next = lax.ppermute(jnp.where(is_end, g_far, g_near), "srv", outer)
    g_over = lax.ppermute(g_far, "srv", line[1])
    g_end = lax.ppermute(g_next, "srv", line[1])
    riders = {2: g_over, 3: g_end}
    g_pieces = [g_next]

    middle = total // 2
    chunks = [(rows_all[middle:], wp_far, wp_near), (rows_all[:middle], wp_far, wp_near)]
    chunks += [(x_rows[b], wq_far, wq_near) for b in range(blocks - 1, -1, -1)]
    landed = []
    for c, (x, w_far, w_near) in enumerate(chunks):
        far_part = jnp.dot(x, w_far, preferred_element_type=f32)
        near_part = jnp.dot(x, w_near, preferred_element_type=f32)
        moving = None
        for k in range(last):
            mine_now = far_part if k < planes // 2 else near_part
            if moving is not None:
                mine_now = mine_now + moving.astype(f32)
            mine_now = mine_now.astype(bf16)
            if k == 0 and c in riders:
                moving = lax.ppermute(jnp.where(is_end, mine_now, riders[c]), "srv", outer)
                g_pieces.append(moving)
            elif c == len(chunks) - 1 and k == last - 1:
                moving = mine_now
            else:
                moving = lax.ppermute(mine_now, "srv", line[k])
        landed.append((near_part + moving.astype(f32)).astype(bf16) if c < 2 else (near_part, moving))

    pairs_at = [(landed[1], b * tok) if b < blocks // 2 else (landed[0], b * tok - middle) for b in range(blocks)]
    all_hops = [None] * blocks
    near_q, far_q, near_kv, far_kv = [[None] * blocks for _ in range(4)]
    sums = [None] * blocks
    lead = 2 * half_k
    g_near, *g_pieces, _ = lax.optimization_barrier((g_near, *g_pieces, landed[0]))
    for b in range(blocks - 1, -1, -1):
        g_first = g_pieces[b - 1] if b > 0 else g_near
        g_last = g_pieces[last - b - 1] if b < last else g_near
        fresh_q, moved_q = landed[2 + blocks - 1 - b]
        relay = [landed[-1][1]] if b == blocks - 1 else []
        local = attend_block(flags, begins, pairs_at, fresh_q, moved_q, g_first, g_last, sums, b, middle // tok, relay)
        hops = [local]
        for k in range(last):
            if b == blocks - 1 and k == 0:
                hops.append(lax.ppermute(local, "srv", outer))
                landed[-1] = (landed[-1][0], hops[1])
            else:
                hops.append(lax.ppermute(hops[k], "srv", line[k]))
        all_hops[b] = hops
        near = jnp.where(is_end, local, hops[1])
        far = jnp.where(is_end, hops[3], hops[2])
        near_q[b], far_q[b], near_kv[b], far_kv[b] = near[:, lead:], far[:, lead:], near[:, :lead], far[:, :lead]

    nt = (((1,), (1,)), ((), ()))
    times = lambda a, w: lax.dot_general(a, w, nt, preferred_element_type=f32)
    terms = []
    for b in range(blocks):
        near_term = times(near_q[b], wq_near) + times(near_kv[b], wp_near)
        terms.append(near_term + times(far_q[b], wq_far) + times(far_kv[b], wp_far))
    summed = []
    for i in range(blocks // cores):
        even, odd = terms[cores * i], terms[cores * i + 1]
        theirs = jnp.where(core == 0, odd, even).astype(bf16)
        ours = jnp.where(core == 0, even, odd)
        summed.append((ours + swap(theirs, "rep", cores).astype(f32)).astype(bf16))
    parts = []
    for i, block in reversed(list(enumerate(summed))):
        for x in range(across):
            home = [(a, b) for a, b in (straight if x == i else crossed) if a % spread // cores == x]
            parts.append(lax.ppermute(block, trio, home).astype(f32))
    input_grad = functools.reduce(jnp.add, parts).astype(bf16)

    shapes = [(width, w.shape[1]) for w in (query_weight, key_weight, value_weight)]
    outs = weight_grads(plane, rows_all, all_hops, planes, shapes)
    return (input_grad, *outs)


def solution(mesh):
    in_specs = (
        P(("groups", "srv"), ("hid", "rep")),
        P("srv", ("hid", "rep")),
        P("srv", ("hid", "rep")),
        P("srv", ("hid", "rep")),
        P(("groups", "srv"), ("hid", "rep")),
        P("groups"),
    )
    out_specs = (
        P(("groups", "srv"), ("hid", "rep")),
        P(("groups", "srv"), ("hid", "rep")),
        P(("groups", "srv"), ("hid", "rep")),
        P(("groups", "srv"), ("hid", "rep")),
    )
    sizes = (mesh.shape["srv"], mesh.shape["hid"], mesh.shape["rep"])
    split = HK // (sizes[1] * sizes[2])
    fits = sizes[0] == sizes[1] * sizes[2] and sizes[1] == 2 and sizes[2] == 2 and split == 2
    chosen = functools.partial(stationary_body, sizes) if fits else body
    return jax.shard_map(chosen, mesh=mesh, in_specs=in_specs, out_specs=out_specs, check_vma=False)
```

```python
import functools

import jax
import jax.numpy as jnp
from jax import lax
from jax.experimental import pallas as pl
from jax.experimental.pallas import tpu as pltpu
from jax.sharding import PartitionSpec as P


HQ = 32
HK = 8
DH = 128
BLOCK = 128


NEGATIVE = -1e30


def attend(queries, cotangent, keys_all, values_all, doc_ids, block_id, carried):
    row_count = queries.shape[0]
    factor_scale = queries.shape[-1] ** (-0.5)
    offsets = jnp.arange(row_count, dtype=jnp.int32)
    query_pos = block_id * row_count + offsets
    query_doc = lax.dynamic_slice_in_dim(doc_ids, block_id * row_count, row_count)
    doc_start = jnp.sum((doc_ids < query_doc[0]).astype(jnp.int32))
    lowest = doc_start // row_count
    highest = jnp.where(True, block_id + 1, lowest)

    def scores_at(key_block):
        key_rows = lax.dynamic_slice_in_dim(keys_all, key_block * row_count, row_count, 0)
        value_rows = lax.dynamic_slice_in_dim(values_all, key_block * row_count, row_count, 0)
        key_doc = lax.dynamic_slice_in_dim(doc_ids, key_block * row_count, row_count)
        key_pos = key_block * row_count + offsets
        allowed = (key_doc[None, :] == query_doc[:, None]) & (
            key_pos[None, :] <= query_pos[:, None]
        )
        logits = (
            jnp.einsum("qgnd,kgd->gnqk", queries, key_rows, preferred_element_type=jnp.float32)
            * factor_scale
        )
        logits = jnp.where(allowed, logits, NEGATIVE)
        slopes = jnp.einsum(
            "qgnd,kgd->gnqk", cotangent, value_rows, preferred_element_type=jnp.float32
        )
        return (key_rows, allowed, logits, slopes)

    def first_pass(key_block, loop_state):
        row_peak, row_total, row_inner = loop_state
        _, allowed, logits, slopes = scores_at(key_block)
        new_peak = jnp.maximum(row_peak, jnp.max(logits, axis=-1))
        weights = jnp.where(allowed, jnp.exp(logits - new_peak[..., None]), 0.0)
        factor = jnp.exp(row_peak - new_peak)
        row_total = row_total * factor + jnp.sum(weights, axis=-1)
        row_inner = row_inner * factor + jnp.sum(weights * slopes, axis=-1)
        return (new_peak, row_total, row_inner)

    stat_shape = (queries.shape[1], queries.shape[2], row_count)
    initial = (
        jnp.full(stat_shape, NEGATIVE, jnp.float32),
        jnp.zeros(stat_shape, jnp.float32),
        jnp.zeros(stat_shape, jnp.float32),
    )
    row_peak, row_total, row_inner = lax.fori_loop(lowest, highest, first_pass, initial)
    safe_total = jnp.where(True, row_total, 1.0)
    row_delta = row_inner / safe_total
    log_total = row_peak + jnp.log(safe_total)

    def second_pass(key_block, loop_state):
        query_grad, key_accum, value_accum = loop_state
        key_rows, allowed, logits, slopes = scores_at(key_block)
        attention = jnp.where(allowed, jnp.exp(logits - log_total[..., None]), 0.0)
        score_grad = (attention * (slopes - row_delta[..., None]) * factor_scale).astype(
            jnp.bfloat16
        )
        value_part = jnp.einsum(
            "gnqk,qgnd->kgd",
            attention.astype(jnp.bfloat16),
            cotangent,
            preferred_element_type=jnp.float32,
        )
        key_part = jnp.einsum(
            "gnqk,qgnd->kgd", score_grad, queries, preferred_element_type=jnp.float32
        )
        query_grad = query_grad + jnp.einsum(
            "gnqk,kgd->qgnd", score_grad, key_rows, preferred_element_type=jnp.float32
        )
        first_row = key_block * row_count
        key_accum = lax.dynamic_update_slice_in_dim(
            key_accum,
            lax.dynamic_slice_in_dim(key_accum, first_row, row_count, 0) + key_part,
            first_row,
            0,
        )
        value_accum = lax.dynamic_update_slice_in_dim(
            value_accum,
            lax.dynamic_slice_in_dim(value_accum, first_row, row_count, 0) + value_part,
            first_row,
            0,
        )
        return (query_grad, key_accum, value_accum)

    start_grad = jnp.zeros(queries.shape, jnp.float32)
    query_grad, key_accum, value_accum = lax.fori_loop(
        lowest, highest, second_pass, (start_grad, carried[0], carried[1])
    )
    return (query_grad, (key_accum, value_accum))


def body(layer_input, query_weight, key_weight, value_weight, out_grad, doc_ids):
    tok_rows = layer_input.shape[0]
    query_width = query_weight.shape[1]
    pair_width = key_weight.shape[1]
    key_heads = pair_width // DH
    group_size = HQ // HK
    block_count = tok_rows // BLOCK
    owner_id = lax.axis_index("srv")
    weights_all = lax.all_gather(
        jnp.concatenate([query_weight, key_weight, value_weight], axis=1), "srv", axis=0, tiled=True
    )
    inputs_all = lax.all_gather(layer_input, ("hid", "rep"), axis=1, tiled=True)
    projected = jnp.dot(inputs_all, weights_all, preferred_element_type=jnp.float32).astype(
        jnp.bfloat16
    )
    queries = projected[:, :query_width].reshape(block_count, BLOCK, key_heads, group_size, DH)
    keys_local = projected[:, query_width : query_width + pair_width]
    values_local = projected[:, query_width + pair_width :]
    keys_all, values_all = (
        lax.all_gather(keys_local, "srv", axis=0, tiled=True),
        lax.all_gather(values_local, "srv", axis=0, tiled=True),
    )
    total_rows = keys_all.shape[0]
    keys_all = keys_all.reshape(total_rows, key_heads, DH)
    values_all = values_all.reshape(total_rows, key_heads, DH)
    cotangent = out_grad.reshape(block_count, BLOCK, key_heads, group_size, DH)
    empty_accum = jnp.zeros((total_rows, key_heads, DH), jnp.float32)

    def own_block(position, loop_state):
        answers, carried = loop_state
        grad_q, carried = attend(
            lax.dynamic_index_in_dim(queries, position, 0, keepdims=False),
            lax.dynamic_index_in_dim(cotangent, position, 0, keepdims=False),
            keys_all,
            values_all,
            doc_ids,
            owner_id * block_count + position,
            carried,
        )
        answers = lax.dynamic_update_index_in_dim(answers, grad_q.astype(jnp.bfloat16), position, 0)
        return (answers, carried)

    answers = jnp.zeros(queries.shape, jnp.bfloat16)
    answers, carried = lax.fori_loop(
        0, block_count, own_block, (answers, (empty_accum, empty_accum))
    )
    query_grad = answers.reshape(tok_rows, query_width)
    key_accum, value_accum = carried
    key_sum, value_sum = (
        lax.psum_scatter(key_accum, "srv", scatter_dimension=0, tiled=True),
        lax.psum_scatter(value_accum, "srv", scatter_dimension=0, tiled=True),
    )
    grads_all = jnp.concatenate(
        [
            query_grad,
            key_sum.astype(jnp.bfloat16).reshape(tok_rows, pair_width),
            value_sum.astype(jnp.bfloat16).reshape(tok_rows, pair_width),
        ],
        axis=1,
    )
    input_terms = lax.dot_general(
        grads_all, weights_all, (((1,), (1,)), ((), ())), preferred_element_type=jnp.float32
    )
    input_grad = lax.psum_scatter(
        input_terms, ("hid", "rep"), scatter_dimension=1, tiled=True
    ).astype(jnp.bfloat16)
    columns = lax.all_to_all(inputs_all, "srv", split_axis=1, concat_axis=0, tiled=True)
    weight_grad = lax.dot_general(
        columns,
        lax.all_gather(grads_all, "srv", axis=0, tiled=True),
        (((0,), (0,)), ((), ())),
        preferred_element_type=jnp.float32,
    )
    return (
        input_grad,
        weight_grad[:, :query_width],
        weight_grad[:, query_width : query_width + pair_width],
        weight_grad[:, query_width + pair_width :],
    )


LOG2E = 1.4426950408889634


def swap(array, axis, size):
    return lax.ppermute(array, axis, [(i, (i + 1) % size) for i in range(size)])


def attention_kernel(flag_ref, *refs, back, heads, block_id, held, moved_at):
    count = back + 1
    start_hbm, new_hbm, old_hbm, ga_hbm, gb_hbm = refs[:5]
    pair_hbm = refs[5 : 5 + count]
    sum_hbm = refs[5 + count : 5 + count + held]
    outs = refs[5 + count + held : 6 + count + held + back]
    start_ref, new_ref, old_ref, g_ref, pair_ref, sum_ref, q_ref, out_ref, left_ref, sems = refs[-10:]
    block = g_ref.shape[0]
    scale = DH ** (-0.5)
    nt = (((1,), (1,)), ((), ()))
    first = block_id * block
    low = first - back * block

    @pl.when(flag_ref[0] != 0)
    def _():
        moved = old_hbm.at[:, pl.ds(moved_at, old_ref.shape[1])]
        copies = [(start_hbm, start_ref), (new_hbm, new_ref), (moved, old_ref)]
        copies += [(pair_hbm[j][0].at[pl.ds(pair_hbm[j][1], block)], pair_ref.at[j]) for j in range(count)]
        copies += [(sum_hbm[n], sum_ref.at[n]) for n in range(held)]
        moves = [pltpu.make_async_copy(a, b, sems.at[n]) for n, (a, b) in enumerate(copies)]
        for move in moves:
            move.start()
        from_first = pltpu.make_async_copy(ga_hbm, g_ref, sems.at[len(moves)])
        from_last = pltpu.make_async_copy(gb_hbm, g_ref, sems.at[len(moves)])

        @pl.when(flag_ref[1] != 0)
        def _():
            from_first.start()

        @pl.when(flag_ref[1] == 0)
        def _():
            from_last.start()

        for move in moves:
            move.wait()
        from_first.wait()
        q_ref[...] = (new_ref[...] + old_ref[...].astype(jnp.float32)).astype(q_ref.dtype)
        begin = start_ref[:, first : first + block]
        query_pos = lax.broadcasted_iota(jnp.int32, (block, block), 1)
        key_pos = lax.broadcasted_iota(jnp.int32, (block, block), 0)
        allowed = []
        for j in range(count):
            inside = key_pos >= begin - (low + j * block)
            allowed.append(inside & (key_pos <= query_pos) if j == back else inside)
        keys_t = [pair_ref[j][:, :DH].T for j in range(count)]
        dk, dv = [None] * count, [None] * count

        def front(h):
            q = q_ref[:, h * DH : (h + 1) * DH]
            g = g_ref[:, h * DH : (h + 1) * DH]
            logits, slopes = [], []
            for j in range(count):
                k, v = pair_ref[j][:, :DH], pair_ref[j][:, DH:]
                term = lax.dot_general(k, q, nt, preferred_element_type=jnp.float32) * (scale * LOG2E)
                logits.append(jnp.where(allowed[j], term, NEGATIVE))
                slopes.append(lax.dot_general(v, g, nt, preferred_element_type=jnp.float32))
            return q, g, logits, slopes

        ahead = front(0)
        for h in range(heads):
            q, g, logits, slopes = ahead
            if h + 1 < heads:
                ahead = front(h + 1)
            peak = functools.reduce(jnp.maximum, [jnp.max(t, axis=0, keepdims=True) for t in logits])
            weights = [jnp.exp2(t - peak) for t in logits]
            total = functools.reduce(jnp.add, [jnp.sum(w, axis=0, keepdims=True) for w in weights])
            inner = functools.reduce(jnp.add, [jnp.sum(w * t, axis=0, keepdims=True) for w, t in zip(weights, slopes)])
            inverse = 1.0 / total
            inner = inner * inverse
            dq = None
            for j in range(count):
                attention = weights[j] * inverse
                score = (attention * (slopes[j] - inner)).astype(jnp.bfloat16)
                value_part = jnp.dot(attention.astype(jnp.bfloat16), g, preferred_element_type=jnp.float32)
                key_part = jnp.dot(score, q, preferred_element_type=jnp.float32)
                dv[j] = value_part if dv[j] is None else dv[j] + value_part
                dk[j] = key_part if dk[j] is None else dk[j] + key_part
                part = jnp.dot(keys_t[j], score, preferred_element_type=jnp.float32)
                dq = part if dq is None else dq + part
            out_ref[:, (2 + h) * DH : (3 + h) * DH] = (dq * scale).T.astype(out_ref.dtype)
        fresh = count - held
        for j in range(count):
            new_k, new_v = dk[j] * scale, dv[j]
            if j >= fresh:
                new_k = new_k + sum_ref[j - fresh][:, :DH]
                new_v = new_v + sum_ref[j - fresh][:, DH:]
            if j == back:
                out_ref[:, :DH] = new_k.astype(out_ref.dtype)
                out_ref[:, DH : 2 * DH] = new_v.astype(out_ref.dtype)
            else:
                left_ref[j, :, :DH] = new_k
                left_ref[j, :, DH:] = new_v
        moves = [pltpu.make_async_copy(out_ref, outs[0], sems.at[0])]
        moves += [pltpu.make_async_copy(left_ref.at[j], outs[1 + j], sems.at[1 + j]) for j in range(back)]
        for move in moves:
            move.start()
        for move in moves:
            move.wait()


def attend_block(flags, begins, pairs, fresh_q, moved_q, g_first, g_last, sums, block_id, reach):
    block, width = g_first.shape
    heads = width // DH
    back = min(reach, block_id)
    low = block_id - back
    count = back + 1
    held = [sums[j] for j in range(low, block_id + 1) if sums[j] is not None]
    f32, bf16 = jnp.float32, jnp.bfloat16
    hbm = pl.BlockSpec(memory_space=pl.ANY)
    sum_shape = (block, 2 * DH)
    outs = [jax.ShapeDtypeStruct((block, 2 * DH + width), bf16)] + [jax.ShapeDtypeStruct(sum_shape, f32)] * back
    rows = [pairs[j][1] for j in range(low, block_id + 1)]
    operands = [begins, fresh_q, moved_q, g_first, g_last] + [pairs[j][0] for j in range(low, block_id + 1)] + held

    def kernel(flag_ref, *refs):
        refs = list(refs)
        refs[5 : 5 + count] = list(zip(refs[5 : 5 + count], rows))
        attention_kernel(flag_ref, *refs, back=back, heads=heads, block_id=block_id, held=len(held), moved_at=moved_q.shape[1] - width)

    results = pl.pallas_call(
        kernel,
        in_specs=[pl.BlockSpec(memory_space=pltpu.SMEM)] + [hbm] * len(operands),
        out_specs=[hbm] * len(outs),
        out_shape=outs,
        scratch_shapes=[
            pltpu.VMEM(begins.shape, jnp.int32),
            pltpu.VMEM((block, width), f32),
            pltpu.VMEM((block, width), bf16),
            pltpu.VMEM((block, width), bf16),
            pltpu.VMEM((count,) + sum_shape, bf16),
            pltpu.VMEM((max(1, len(held)),) + sum_shape, f32),
            pltpu.VMEM((block, width), bf16),
            pltpu.VMEM((block, 2 * DH + width), bf16),
            pltpu.VMEM((max(1, back),) + sum_shape, f32),
            pltpu.SemaphoreType.DMA((4 + count + len(held),)),
        ],
        cost_estimate=pl.CostEstimate(
            flops=10 * heads * DH * block * block * count, bytes_accessed=3 * block * 8 * DH, transcendentals=heads * block * block * count
        ),
    )(flags, *operands)
    for j in range(back):
        sums[low + j] = results[1 + j]
    return results[0]


def weight_grad_kernel(plane_ref, *refs, planes, blocks):
    x_hbm = refs[0]
    hops = refs[1 : 1 + blocks * planes]
    out_q, out_k, out_v = refs[1 + blocks * planes : 4 + blocks * planes]
    x_ref, left_ref, right_ref, q_ref, k_ref, v_ref, sems, out_sems = refs[4 + blocks * planes :]
    rows = left_ref.shape[0] // blocks
    tile = q_ref.shape[1]
    half_q = q_ref.shape[2] // 2
    move_x = pltpu.make_async_copy(x_hbm, x_ref, sems.at[0])
    move_x.start()

    def fetch(b, source, target, n):
        return pltpu.make_async_copy(source, target.at[pl.ds(b * rows, rows)], sems.at[n])

    for z in range(planes):

        @pl.when(plane_ref[0] == z)
        def _(z=z):
            for b in range(blocks):
                fetch(b, hops[b * planes + z], left_ref, 1 + 2 * b).start()
                fetch(b, hops[b * planes + planes - 1 - z], right_ref, 2 + 2 * b).start()

    move_x.wait()
    for b in range(blocks):
        fetch(b, hops[b * planes], left_ref, 1 + 2 * b).wait()
        fetch(b, hops[b * planes], right_ref, 2 + 2 * b).wait()

    def store(step, slot):
        at = pl.ds(pl.multiple_of(step * tile, tile), tile)
        return [
            pltpu.make_async_copy(ref.at[slot], out.at[at], out_sems.at[slot, n])
            for n, (ref, out) in enumerate(((q_ref, out_q), (k_ref, out_k), (v_ref, out_v)))
        ]

    steps = x_ref.shape[1] // tile

    def body(step, carry):
        slot = step % 2

        @pl.when(step >= 2)
        def _():
            for move in store(step, slot):
                move.wait()

        x_t = x_ref[:, pl.ds(pl.multiple_of(step * tile, tile), tile)].T
        for side, ref in enumerate((left_ref, right_ref)):
            result = jnp.dot(x_t, ref[...], preferred_element_type=jnp.float32)
            k_ref[slot, :, side * DH : (side + 1) * DH] = result[:, :DH]
            v_ref[slot, :, side * DH : (side + 1) * DH] = result[:, DH : 2 * DH]
            q_ref[slot, :, side * half_q : (side + 1) * half_q] = result[:, 2 * DH :]
        for move in store(step, slot):
            move.start()
        return carry

    lax.fori_loop(0, steps, body, 0)
    for slot in range(2):
        for move in store(slot, slot):
            move.wait()


def weight_grads(plane, x, hops, planes, shapes):
    total, width = x.shape
    blocks = len(hops)
    flat = [array for group in hops for array in group]
    tile = 256
    f32, bf16 = jnp.float32, jnp.bfloat16
    hbm = pl.BlockSpec(memory_space=pl.ANY)
    columns = flat[0].shape[1]
    return pl.pallas_call(
        functools.partial(weight_grad_kernel, planes=planes, blocks=blocks),
        in_specs=[pl.BlockSpec(memory_space=pltpu.SMEM)] + [hbm] * (1 + len(flat)),
        out_specs=[hbm] * 3,
        out_shape=[jax.ShapeDtypeStruct(s, f32) for s in shapes],
        scratch_shapes=[
            pltpu.VMEM((total, width), bf16),
            pltpu.VMEM((total, columns), bf16),
            pltpu.VMEM((total, columns), bf16),
        ]
        + [pltpu.VMEM((2, tile, s[1]), f32) for s in shapes]
        + [pltpu.SemaphoreType.DMA((1 + 2 * blocks,)), pltpu.SemaphoreType.DMA((2, 3))],
        cost_estimate=pl.CostEstimate(flops=4 * total * width * columns, bytes_accessed=8 * total * width, transcendentals=0),
    )(plane.astype(jnp.int32).reshape(1), x, *flat)


def place_kernel(at_ref, *refs):
    pieces, out_ref, sems = refs[:-2], refs[-2], refs[-1]
    rows = pieces[0].shape[0]
    moves = [
        pltpu.make_async_copy(piece, out_ref.at[pl.ds(pl.multiple_of(at_ref[n] * rows, rows), rows)], sems.at[n])
        for n, piece in enumerate(pieces)
    ]
    for move in moves:
        move.start()
    for move in moves:
        move.wait()


def place_pieces(slots, pieces):
    rows, width = pieces[0].shape
    return pl.pallas_call(
        place_kernel,
        in_specs=[pl.BlockSpec(memory_space=pltpu.SMEM)] + [pl.BlockSpec(memory_space=pl.ANY)] * len(pieces),
        out_specs=pl.BlockSpec(memory_space=pltpu.VMEM),
        out_shape=jax.ShapeDtypeStruct((rows * len(pieces), width), pieces[0].dtype),
        scratch_shapes=[pltpu.SemaphoreType.DMA((len(pieces),))],
        cost_estimate=pl.CostEstimate(flops=0, bytes_accessed=4 * rows * width * len(pieces), transcendentals=0),
    )(slots, *pieces)


def stationary_body(sizes, *arrays):
    return stationary(sizes, *arrays)


def stationary(sizes, layer_input, query_weight, key_weight, value_weight, out_grad, doc_ids):
    planes, across, cores = sizes
    spread = across * cores
    f32, bf16 = jnp.float32, jnp.bfloat16
    tok, width = layer_input.shape
    total = tok * planes
    half_q, half_k = query_weight.shape[1] // 2, key_weight.shape[1] // 2
    plane = lax.axis_index("srv")
    side, core = lax.axis_index("hid"), lax.axis_index("rep")
    last = planes - 1
    blocks = planes
    near_left = plane < planes // 2
    is_end = (plane == 0) | (plane == last)
    trio = ("srv", "hid", "rep")
    pairs = [(t, f) for t in range(planes) for f in range(spread)]
    straight = [(t * spread + f, f * spread + t) for t, f in pairs]
    crossed = [(t * spread + f, (f + cores) % spread * spread + t) for t, f in pairs]

    def climb(early):
        moves = []
        for t, f in pairs:
            x = f // cores
            target = f if (t % 2 == 0) == early else (f + cores) % spread
            moves.append((t * spread + f, target * spread + x * cores + t * cores // planes))
        return moves

    rise, fall = climb(True), climb(False)
    outer = [(0, 1), (1, 0), (last - 1, last), (last, last - 1)]
    line = [[(k, k + 1), (last - k, last - k - 1)] for k in range(last)]
    far_at, near_at = jnp.where(near_left, 1, 0), jnp.where(near_left, 0, 1)

    def part(array, at, size):
        return lax.dynamic_slice_in_dim(array, at * size, size, 1)

    pair_weight = lambda at: jnp.concatenate([part(key_weight, at, half_k), part(value_weight, at, half_k)], axis=1)
    wp_near, wp_far = pair_weight(near_at), pair_weight(far_at)
    wq_near, wq_far = part(query_weight, near_at, half_q), part(query_weight, far_at, half_q)
    g_near, g_far = part(out_grad, near_at, half_q), part(out_grad, far_at, half_q)
    begins = jnp.sum((doc_ids[None, :] < doc_ids[:, None]).astype(jnp.int32), axis=1).reshape(1, total)
    flags = jnp.stack([is_end, plane == 0]).astype(jnp.int32)

    part_rows = tok // across
    mine = lax.dynamic_slice_in_dim(layer_input, side * part_rows, part_rows, 0)
    other = lax.dynamic_slice_in_dim(layer_input, (1 - side) * part_rows, part_rows, 0)
    other = swap(other, "hid", across)
    even_plane = plane % 2 == 0
    up = lax.ppermute(jnp.where(even_plane, mine, other), trio, rise)
    down = lax.ppermute(jnp.where(even_plane, other, mine), trio, fall)
    straight_first = jnp.where(side == plane // cores, 0, 1)
    held = planes // cores
    slot = lambda owner, which, half: (owner * held + which) * across + half
    slots = []
    for which in (straight_first, 1 - straight_first):
        slots += [slot(core, which, side), slot(1 - core, which, side)]
        slots += [slot(core, 1 - which, 1 - side), slot(1 - core, 1 - which, 1 - side)]
    slots = jnp.stack(slots).astype(jnp.int32)
    wp_near, wp_far, wq_near, wq_far, g_near, g_far, begins, flags, slots, up = lax.optimization_barrier(
        (wp_near, wp_far, wq_near, wq_far, g_near, g_far, begins, flags, slots, up)
    )
    pieces = []
    for piece in (up, down):
        turned = swap(piece, "hid", across)
        mate = swap(piece, "rep", cores)
        turned_mate = swap(turned, "rep", cores)
        pieces += [piece, mate, turned, turned_mate]
    rows_all = place_pieces(slots, pieces)
    x_rows = [lax.slice_in_dim(rows_all, b * tok, (b + 1) * tok, axis=0) for b in range(planes)]

    g_next = lax.ppermute(jnp.where(is_end, g_far, g_near), "srv", outer)
    g_over = lax.ppermute(g_far, "srv", line[1])
    g_end = lax.ppermute(g_next, "srv", line[1])
    riders = {2: g_over, planes + 1: g_end}
    g_pieces = [g_next]

    middle = total // 2
    chunks = [(rows_all[middle:], wp_far, wp_near), (rows_all[:middle], wp_far, wp_near)]
    chunks += [(x_rows[b], wq_far, wq_near) for b in range(blocks - 1, -1, -1)]
    landed = []
    for c, (x, w_far, w_near) in enumerate(chunks):
        far_part = jnp.dot(x, w_far, preferred_element_type=f32)
        near_part = jnp.dot(x, w_near, preferred_element_type=f32)
        moving = None
        for k in range(last):
            mine_now = far_part if k < planes // 2 else near_part
            if moving is not None:
                mine_now = mine_now + moving.astype(f32)
            mine_now = mine_now.astype(bf16)
            if k == 0 and c in riders:
                moving = lax.ppermute(jnp.where(is_end, mine_now, riders[c]), "srv", outer)
                g_pieces.append(moving)
            elif c == len(chunks) - 1 and k == last - 1:
                moving = mine_now
            else:
                moving = lax.ppermute(mine_now, "srv", line[k])
        landed.append((near_part + moving.astype(f32)).astype(bf16) if c < 2 else (near_part, moving))

    pairs_at = [(landed[1], b * tok) if b < blocks // 2 else (landed[0], b * tok - middle) for b in range(blocks)]
    all_hops = [None] * blocks
    sums = [None] * blocks
    lead = 2 * half_k
    g_near, *g_pieces, _ = lax.optimization_barrier((g_near, *g_pieces, landed[0]))
    for b in range(blocks - 1, -1, -1):
        g_first = g_pieces[b - 1] if b > 0 else g_near
        g_last = g_pieces[last - b - 1] if b < last else g_near
        fresh_q, moved_q = landed[2 + blocks - 1 - b]
        local = attend_block(flags, begins, pairs_at, fresh_q, moved_q, g_first, g_last, sums, b, middle // tok)
        hops = [local]
        for k in range(last):
            if b == blocks - 1 and k == 0:
                fresh_q, moved_q = landed[-1]
                wider = jnp.pad(moved_q, ((0, 0), (lead, 0)))
                hops.append(lax.ppermute(jnp.where(is_end, local, wider), "srv", outer))
                landed[-1] = (fresh_q, hops[1])
            else:
                hops.append(lax.ppermute(hops[k], "srv", line[k]))
        all_hops[b] = hops

    nt = (((1,), (1,)), ((), ()))
    times = lambda a, w: lax.dot_general(a, w, nt, preferred_element_type=f32)

    def columns(grads, wq, wp):
        return times(grads[:, lead:], wq) + times(grads[:, :lead], wp)

    def pair_sum(even, odd):
        theirs = jnp.where(core == 0, odd, even).astype(bf16)
        ours = jnp.where(core == 0, even, odd)
        return (ours + swap(theirs, "rep", cores).astype(f32)).astype(bf16)

    def send_home(block, i, planes_from):
        for x in range(across):
            home = [
                (a, b)
                for a, b in (straight if x == i else crossed)
                if a % spread // cores == x and a // spread in planes_from
            ]
            parts.append(lax.ppermute(block, trio, home).astype(f32))

    parts, near_terms, full = [], {}, {}
    for b in range(blocks):
        local, one_hop, _, _ = all_hops[b]
        near_terms[b] = columns(jnp.where(is_end, local, one_hop), wq_near, wp_near)
    for b in range(cores, blocks):
        far = jnp.where(is_end, all_hops[b][3], all_hops[b][2])
        full[b] = near_terms[b] + columns(far, wq_far, wp_far)
    for i in range(1, blocks // cores):
        send_home(pair_sum(full[cores * i], full[cores * i + 1]), i, range(planes))
    for hop, planes_from in ((2, range(1, last)), (3, (0, last))):
        pair = []
        for b in range(cores):
            pair.append(near_terms[b] + columns(all_hops[b][hop], wq_far, wp_far))
        send_home(pair_sum(*pair), 0, planes_from)
    input_grad = functools.reduce(jnp.add, parts).astype(bf16)

    shapes = [(width, w.shape[1]) for w in (query_weight, key_weight, value_weight)]
    outs = weight_grads(plane, rows_all, all_hops, planes, shapes)
    return (input_grad, *outs)


def solution(mesh):
    in_specs = (
        P(("groups", "srv"), ("hid", "rep")),
        P("srv", ("hid", "rep")),
        P("srv", ("hid", "rep")),
        P("srv", ("hid", "rep")),
        P(("groups", "srv"), ("hid", "rep")),
        P("groups"),
    )
    out_specs = (
        P(("groups", "srv"), ("hid", "rep")),
        P(("groups", "srv"), ("hid", "rep")),
        P(("groups", "srv"), ("hid", "rep")),
        P(("groups", "srv"), ("hid", "rep")),
    )
    sizes = (mesh.shape["srv"], mesh.shape["hid"], mesh.shape["rep"])
    split = HK // (sizes[1] * sizes[2])
    fits = sizes[0] == sizes[1] * sizes[2] and sizes[1] == 2 and sizes[2] == 2 and split == 2
    chosen = functools.partial(stationary_body, sizes) if fits else body
    return jax.shard_map(chosen, mesh=mesh, in_specs=in_specs, out_specs=out_specs, check_vma=False)
```

```python
import functools

import jax
import jax.numpy as jnp
from jax import lax
from jax.experimental import pallas as pl
from jax.experimental.pallas import tpu as pltpu
from jax.sharding import PartitionSpec as P


HQ = 32
HK = 8
DH = 128
BLOCK = 128


NEGATIVE = -1e30


def attend(queries, cotangent, keys_all, values_all, doc_ids, block_id, carried):
    row_count = queries.shape[0]
    factor_scale = queries.shape[-1] ** (-0.5)
    offsets = jnp.arange(row_count, dtype=jnp.int32)
    query_pos = block_id * row_count + offsets
    query_doc = lax.dynamic_slice_in_dim(doc_ids, block_id * row_count, row_count)
    doc_start = jnp.sum((doc_ids < query_doc[0]).astype(jnp.int32))
    lowest = doc_start // row_count
    highest = jnp.where(True, block_id + 1, lowest)

    def scores_at(key_block):
        key_rows = lax.dynamic_slice_in_dim(keys_all, key_block * row_count, row_count, 0)
        value_rows = lax.dynamic_slice_in_dim(values_all, key_block * row_count, row_count, 0)
        key_doc = lax.dynamic_slice_in_dim(doc_ids, key_block * row_count, row_count)
        key_pos = key_block * row_count + offsets
        allowed = (key_doc[None, :] == query_doc[:, None]) & (
            key_pos[None, :] <= query_pos[:, None]
        )
        logits = (
            jnp.einsum("qgnd,kgd->gnqk", queries, key_rows, preferred_element_type=jnp.float32)
            * factor_scale
        )
        logits = jnp.where(allowed, logits, NEGATIVE)
        slopes = jnp.einsum(
            "qgnd,kgd->gnqk", cotangent, value_rows, preferred_element_type=jnp.float32
        )
        return (key_rows, allowed, logits, slopes)

    def first_pass(key_block, loop_state):
        row_peak, row_total, row_inner = loop_state
        _, allowed, logits, slopes = scores_at(key_block)
        new_peak = jnp.maximum(row_peak, jnp.max(logits, axis=-1))
        weights = jnp.where(allowed, jnp.exp(logits - new_peak[..., None]), 0.0)
        factor = jnp.exp(row_peak - new_peak)
        row_total = row_total * factor + jnp.sum(weights, axis=-1)
        row_inner = row_inner * factor + jnp.sum(weights * slopes, axis=-1)
        return (new_peak, row_total, row_inner)

    stat_shape = (queries.shape[1], queries.shape[2], row_count)
    initial = (
        jnp.full(stat_shape, NEGATIVE, jnp.float32),
        jnp.zeros(stat_shape, jnp.float32),
        jnp.zeros(stat_shape, jnp.float32),
    )
    row_peak, row_total, row_inner = lax.fori_loop(lowest, highest, first_pass, initial)
    safe_total = jnp.where(True, row_total, 1.0)
    row_delta = row_inner / safe_total
    log_total = row_peak + jnp.log(safe_total)

    def second_pass(key_block, loop_state):
        query_grad, key_accum, value_accum = loop_state
        key_rows, allowed, logits, slopes = scores_at(key_block)
        attention = jnp.where(allowed, jnp.exp(logits - log_total[..., None]), 0.0)
        score_grad = (attention * (slopes - row_delta[..., None]) * factor_scale).astype(
            jnp.bfloat16
        )
        value_part = jnp.einsum(
            "gnqk,qgnd->kgd",
            attention.astype(jnp.bfloat16),
            cotangent,
            preferred_element_type=jnp.float32,
        )
        key_part = jnp.einsum(
            "gnqk,qgnd->kgd", score_grad, queries, preferred_element_type=jnp.float32
        )
        query_grad = query_grad + jnp.einsum(
            "gnqk,kgd->qgnd", score_grad, key_rows, preferred_element_type=jnp.float32
        )
        first_row = key_block * row_count
        key_accum = lax.dynamic_update_slice_in_dim(
            key_accum,
            lax.dynamic_slice_in_dim(key_accum, first_row, row_count, 0) + key_part,
            first_row,
            0,
        )
        value_accum = lax.dynamic_update_slice_in_dim(
            value_accum,
            lax.dynamic_slice_in_dim(value_accum, first_row, row_count, 0) + value_part,
            first_row,
            0,
        )
        return (query_grad, key_accum, value_accum)

    start_grad = jnp.zeros(queries.shape, jnp.float32)
    query_grad, key_accum, value_accum = lax.fori_loop(
        lowest, highest, second_pass, (start_grad, carried[0], carried[1])
    )
    return (query_grad, (key_accum, value_accum))


def body(layer_input, query_weight, key_weight, value_weight, out_grad, doc_ids):
    tok_rows = layer_input.shape[0]
    query_width = query_weight.shape[1]
    pair_width = key_weight.shape[1]
    key_heads = pair_width // DH
    group_size = HQ // HK
    block_count = tok_rows // BLOCK
    owner_id = lax.axis_index("srv")
    weights_all = lax.all_gather(
        jnp.concatenate([query_weight, key_weight, value_weight], axis=1), "srv", axis=0, tiled=True
    )
    inputs_all = lax.all_gather(layer_input, ("hid", "rep"), axis=1, tiled=True)
    projected = jnp.dot(inputs_all, weights_all, preferred_element_type=jnp.float32).astype(
        jnp.bfloat16
    )
    queries = projected[:, :query_width].reshape(block_count, BLOCK, key_heads, group_size, DH)
    keys_local = projected[:, query_width : query_width + pair_width]
    values_local = projected[:, query_width + pair_width :]
    keys_all, values_all = (
        lax.all_gather(keys_local, "srv", axis=0, tiled=True),
        lax.all_gather(values_local, "srv", axis=0, tiled=True),
    )
    total_rows = keys_all.shape[0]
    keys_all = keys_all.reshape(total_rows, key_heads, DH)
    values_all = values_all.reshape(total_rows, key_heads, DH)
    cotangent = out_grad.reshape(block_count, BLOCK, key_heads, group_size, DH)
    empty_accum = jnp.zeros((total_rows, key_heads, DH), jnp.float32)

    def own_block(position, loop_state):
        answers, carried = loop_state
        grad_q, carried = attend(
            lax.dynamic_index_in_dim(queries, position, 0, keepdims=False),
            lax.dynamic_index_in_dim(cotangent, position, 0, keepdims=False),
            keys_all,
            values_all,
            doc_ids,
            owner_id * block_count + position,
            carried,
        )
        answers = lax.dynamic_update_index_in_dim(answers, grad_q.astype(jnp.bfloat16), position, 0)
        return (answers, carried)

    answers = jnp.zeros(queries.shape, jnp.bfloat16)
    answers, carried = lax.fori_loop(
        0, block_count, own_block, (answers, (empty_accum, empty_accum))
    )
    query_grad = answers.reshape(tok_rows, query_width)
    key_accum, value_accum = carried
    key_sum, value_sum = (
        lax.psum_scatter(key_accum, "srv", scatter_dimension=0, tiled=True),
        lax.psum_scatter(value_accum, "srv", scatter_dimension=0, tiled=True),
    )
    grads_all = jnp.concatenate(
        [
            query_grad,
            key_sum.astype(jnp.bfloat16).reshape(tok_rows, pair_width),
            value_sum.astype(jnp.bfloat16).reshape(tok_rows, pair_width),
        ],
        axis=1,
    )
    input_terms = lax.dot_general(
        grads_all, weights_all, (((1,), (1,)), ((), ())), preferred_element_type=jnp.float32
    )
    input_grad = lax.psum_scatter(
        input_terms, ("hid", "rep"), scatter_dimension=1, tiled=True
    ).astype(jnp.bfloat16)
    columns = lax.all_to_all(inputs_all, "srv", split_axis=1, concat_axis=0, tiled=True)
    weight_grad = lax.dot_general(
        columns,
        lax.all_gather(grads_all, "srv", axis=0, tiled=True),
        (((0,), (0,)), ((), ())),
        preferred_element_type=jnp.float32,
    )
    return (
        input_grad,
        weight_grad[:, :query_width],
        weight_grad[:, query_width : query_width + pair_width],
        weight_grad[:, query_width + pair_width :],
    )


LOG2E = 1.4426950408889634


def swap(array, axis, size):
    return lax.ppermute(array, axis, [(i, (i + 1) % size) for i in range(size)])


def attention_kernel(flag_ref, *refs, back, heads, block_id, held, moved_at):
    count = back + 1
    start_hbm, new_hbm, old_hbm, ga_hbm, gb_hbm = refs[:5]
    pair_hbm = refs[5 : 5 + count]
    sum_hbm = refs[5 + count : 5 + count + held]
    outs = refs[5 + count + held : 6 + count + held + back]
    start_ref, new_ref, old_ref, g_ref, pair_ref, sum_ref, q_ref, out_ref, left_ref, sems = refs[-10:]
    block = g_ref.shape[0]
    scale = DH ** (-0.5)
    nt = (((1,), (1,)), ((), ()))
    first = block_id * block
    low = first - back * block

    @pl.when(flag_ref[0] != 0)
    def _():
        moved = old_hbm.at[:, pl.ds(moved_at, old_ref.shape[1])]
        copies = [(start_hbm, start_ref), (new_hbm, new_ref), (moved, old_ref)]
        copies += [(pair_hbm[j][0].at[pl.ds(pair_hbm[j][1], block)], pair_ref.at[j]) for j in range(count)]
        copies += [(sum_hbm[n], sum_ref.at[n]) for n in range(held)]
        moves = [pltpu.make_async_copy(a, b, sems.at[n]) for n, (a, b) in enumerate(copies)]
        for move in moves:
            move.start()
        from_first = pltpu.make_async_copy(ga_hbm, g_ref, sems.at[len(moves)])
        from_last = pltpu.make_async_copy(gb_hbm, g_ref, sems.at[len(moves)])

        @pl.when(flag_ref[1] != 0)
        def _():
            from_first.start()

        @pl.when(flag_ref[1] == 0)
        def _():
            from_last.start()

        for move in moves:
            move.wait()
        from_first.wait()
        q_ref[...] = (new_ref[...] + old_ref[...].astype(jnp.float32)).astype(q_ref.dtype)
        begin = start_ref[:, first : first + block]
        query_pos = lax.broadcasted_iota(jnp.int32, (block, block), 1)
        key_pos = lax.broadcasted_iota(jnp.int32, (block, block), 0)
        allowed = []
        for j in range(count):
            inside = key_pos >= begin - (low + j * block)
            allowed.append(inside & (key_pos <= query_pos) if j == back else inside)
        keys_t = [pair_ref[j][:, :DH].T for j in range(count)]
        dk, dv = [None] * count, [None] * count

        def front(h):
            q = q_ref[:, h * DH : (h + 1) * DH]
            g = g_ref[:, h * DH : (h + 1) * DH]
            logits, slopes = [], []
            for j in range(count):
                k, v = pair_ref[j][:, :DH], pair_ref[j][:, DH:]
                term = lax.dot_general(k, q, nt, preferred_element_type=jnp.float32) * (scale * LOG2E)
                logits.append(jnp.where(allowed[j], term, NEGATIVE))
                slopes.append(lax.dot_general(v, g, nt, preferred_element_type=jnp.float32))
            return q, g, logits, slopes

        ahead = front(0)
        for h in range(heads):
            q, g, logits, slopes = ahead
            if h + 1 < heads:
                ahead = front(h + 1)
            peak = functools.reduce(jnp.maximum, [jnp.max(t, axis=0, keepdims=True) for t in logits])
            weights = [jnp.exp2(t - peak) for t in logits]
            total = functools.reduce(jnp.add, [jnp.sum(w, axis=0, keepdims=True) for w in weights])
            inner = functools.reduce(jnp.add, [jnp.sum(w * t, axis=0, keepdims=True) for w, t in zip(weights, slopes)])
            inverse = 1.0 / total
            inner = inner * inverse
            dq = None
            for j in range(count):
                attention = weights[j] * inverse
                score = (attention * (slopes[j] - inner)).astype(jnp.bfloat16)
                value_part = jnp.dot(attention.astype(jnp.bfloat16), g, preferred_element_type=jnp.float32)
                key_part = jnp.dot(score, q, preferred_element_type=jnp.float32)
                dv[j] = value_part if dv[j] is None else dv[j] + value_part
                dk[j] = key_part if dk[j] is None else dk[j] + key_part
                part = jnp.dot(keys_t[j], score, preferred_element_type=jnp.float32)
                dq = part if dq is None else dq + part
            out_ref[:, (2 + h) * DH : (3 + h) * DH] = (dq * scale).T.astype(out_ref.dtype)
        fresh = count - held
        for j in range(count):
            new_k, new_v = dk[j] * scale, dv[j]
            if j >= fresh:
                new_k = new_k + sum_ref[j - fresh][:, :DH]
                new_v = new_v + sum_ref[j - fresh][:, DH:]
            if j == back:
                out_ref[:, :DH] = new_k.astype(out_ref.dtype)
                out_ref[:, DH : 2 * DH] = new_v.astype(out_ref.dtype)
            else:
                left_ref[j, :, :DH] = new_k
                left_ref[j, :, DH:] = new_v
        moves = [pltpu.make_async_copy(out_ref, outs[0], sems.at[0])]
        moves += [pltpu.make_async_copy(left_ref.at[j], outs[1 + j], sems.at[1 + j]) for j in range(back)]
        for move in moves:
            move.start()
        for move in moves:
            move.wait()


def attend_block(flags, begins, pairs, fresh_q, moved_q, g_first, g_last, sums, block_id, reach):
    block, width = g_first.shape
    heads = width // DH
    back = min(reach, block_id)
    low = block_id - back
    count = back + 1
    held = [sums[j] for j in range(low, block_id + 1) if sums[j] is not None]
    f32, bf16 = jnp.float32, jnp.bfloat16
    hbm = pl.BlockSpec(memory_space=pl.ANY)
    sum_shape = (block, 2 * DH)
    outs = [jax.ShapeDtypeStruct((block, 2 * DH + width), bf16)] + [jax.ShapeDtypeStruct(sum_shape, f32)] * back
    rows = [pairs[j][1] for j in range(low, block_id + 1)]
    operands = [begins, fresh_q, moved_q, g_first, g_last] + [pairs[j][0] for j in range(low, block_id + 1)] + held

    def kernel(flag_ref, *refs):
        refs = list(refs)
        refs[5 : 5 + count] = list(zip(refs[5 : 5 + count], rows))
        attention_kernel(flag_ref, *refs, back=back, heads=heads, block_id=block_id, held=len(held), moved_at=moved_q.shape[1] - width)

    results = pl.pallas_call(
        kernel,
        in_specs=[pl.BlockSpec(memory_space=pltpu.SMEM)] + [hbm] * len(operands),
        out_specs=[hbm] * len(outs),
        out_shape=outs,
        scratch_shapes=[
            pltpu.VMEM(begins.shape, jnp.int32),
            pltpu.VMEM((block, width), f32),
            pltpu.VMEM((block, width), bf16),
            pltpu.VMEM((block, width), bf16),
            pltpu.VMEM((count,) + sum_shape, bf16),
            pltpu.VMEM((max(1, len(held)),) + sum_shape, f32),
            pltpu.VMEM((block, width), bf16),
            pltpu.VMEM((block, 2 * DH + width), bf16),
            pltpu.VMEM((max(1, back),) + sum_shape, f32),
            pltpu.SemaphoreType.DMA((4 + count + len(held),)),
        ],
        cost_estimate=pl.CostEstimate(
            flops=10 * heads * DH * block * block * count, bytes_accessed=3 * block * 8 * DH, transcendentals=heads * block * block * count
        ),
    )(flags, *operands)
    for j in range(back):
        sums[low + j] = results[1 + j]
    return results[0]


def weight_grad_kernel(plane_ref, *refs, planes, blocks):
    x_hbm = refs[0]
    hops = refs[1 : 1 + blocks * planes]
    out_q, out_k, out_v = refs[1 + blocks * planes : 4 + blocks * planes]
    x_ref, left_ref, right_ref, q_ref, k_ref, v_ref, sems, out_sems = refs[4 + blocks * planes :]
    rows = left_ref.shape[0] // blocks
    tile = q_ref.shape[1]
    half_q = q_ref.shape[2] // 2
    move_x = pltpu.make_async_copy(x_hbm, x_ref, sems.at[0])
    move_x.start()

    def fetch(b, source, target, n):
        return pltpu.make_async_copy(source, target.at[pl.ds(b * rows, rows)], sems.at[n])

    for z in range(planes):

        @pl.when(plane_ref[0] == z)
        def _(z=z):
            for b in range(blocks):
                fetch(b, hops[b * planes + z], left_ref, 1 + 2 * b).start()
                fetch(b, hops[b * planes + planes - 1 - z], right_ref, 2 + 2 * b).start()

    move_x.wait()
    for b in range(blocks):
        fetch(b, hops[b * planes], left_ref, 1 + 2 * b).wait()
        fetch(b, hops[b * planes], right_ref, 2 + 2 * b).wait()

    def store(step, slot):
        at = pl.ds(pl.multiple_of(step * tile, tile), tile)
        return [
            pltpu.make_async_copy(ref.at[slot], out.at[at], out_sems.at[slot, n])
            for n, (ref, out) in enumerate(((q_ref, out_q), (k_ref, out_k), (v_ref, out_v)))
        ]

    steps = x_ref.shape[1] // tile

    def body(step, carry):
        slot = step % 2

        @pl.when(step >= 2)
        def _():
            for move in store(step, slot):
                move.wait()

        x_t = x_ref[:, pl.ds(pl.multiple_of(step * tile, tile), tile)].T
        for side, ref in enumerate((left_ref, right_ref)):
            result = jnp.dot(x_t, ref[...], preferred_element_type=jnp.float32)
            k_ref[slot, :, side * DH : (side + 1) * DH] = result[:, :DH]
            v_ref[slot, :, side * DH : (side + 1) * DH] = result[:, DH : 2 * DH]
            q_ref[slot, :, side * half_q : (side + 1) * half_q] = result[:, 2 * DH :]
        for move in store(step, slot):
            move.start()
        return carry

    lax.fori_loop(0, steps, body, 0)
    for slot in range(2):
        for move in store(slot, slot):
            move.wait()


def weight_grads(plane, x, hops, planes, shapes):
    total, width = x.shape
    blocks = len(hops)
    flat = [array for group in hops for array in group]
    tile = 256
    f32, bf16 = jnp.float32, jnp.bfloat16
    hbm = pl.BlockSpec(memory_space=pl.ANY)
    columns = flat[0].shape[1]
    return pl.pallas_call(
        functools.partial(weight_grad_kernel, planes=planes, blocks=blocks),
        in_specs=[pl.BlockSpec(memory_space=pltpu.SMEM)] + [hbm] * (1 + len(flat)),
        out_specs=[hbm] * 3,
        out_shape=[jax.ShapeDtypeStruct(s, f32) for s in shapes],
        scratch_shapes=[
            pltpu.VMEM((total, width), bf16),
            pltpu.VMEM((total, columns), bf16),
            pltpu.VMEM((total, columns), bf16),
        ]
        + [pltpu.VMEM((2, tile, s[1]), f32) for s in shapes]
        + [pltpu.SemaphoreType.DMA((1 + 2 * blocks,)), pltpu.SemaphoreType.DMA((2, 3))],
        cost_estimate=pl.CostEstimate(flops=4 * total * width * columns, bytes_accessed=8 * total * width, transcendentals=0),
    )(plane.astype(jnp.int32).reshape(1), x, *flat)


def place_kernel(at_ref, *refs):
    pieces, out_ref, sems = refs[:-2], refs[-2], refs[-1]
    rows = pieces[0].shape[0]
    moves = [
        pltpu.make_async_copy(piece, out_ref.at[pl.ds(pl.multiple_of(at_ref[n] * rows, rows), rows)], sems.at[n])
        for n, piece in enumerate(pieces)
    ]
    for move in moves:
        move.start()
    for move in moves:
        move.wait()


def place_pieces(slots, pieces):
    rows, width = pieces[0].shape
    return pl.pallas_call(
        place_kernel,
        in_specs=[pl.BlockSpec(memory_space=pltpu.SMEM)] + [pl.BlockSpec(memory_space=pl.ANY)] * len(pieces),
        out_specs=pl.BlockSpec(memory_space=pltpu.VMEM),
        out_shape=jax.ShapeDtypeStruct((rows * len(pieces), width), pieces[0].dtype),
        scratch_shapes=[pltpu.SemaphoreType.DMA((len(pieces),))],
        cost_estimate=pl.CostEstimate(flops=0, bytes_accessed=4 * rows * width * len(pieces), transcendentals=0),
    )(slots, *pieces)


def stationary_body(sizes, *arrays):
    return stationary(sizes, *arrays)


def stationary(sizes, layer_input, query_weight, key_weight, value_weight, out_grad, doc_ids):
    planes, across, cores = sizes
    spread = across * cores
    f32, bf16 = jnp.float32, jnp.bfloat16
    tok, width = layer_input.shape
    total = tok * planes
    half_q, half_k = query_weight.shape[1] // 2, key_weight.shape[1] // 2
    plane = lax.axis_index("srv")
    side, core = lax.axis_index("hid"), lax.axis_index("rep")
    last = planes - 1
    blocks = planes
    near_left = plane < planes // 2
    is_end = (plane == 0) | (plane == last)
    trio = ("srv", "hid", "rep")
    pairs = [(t, f) for t in range(planes) for f in range(spread)]
    straight = [(t * spread + f, f * spread + t) for t, f in pairs]
    crossed = [(t * spread + f, (f + cores) % spread * spread + t) for t, f in pairs]

    def climb(early):
        moves = []
        for t, f in pairs:
            x = f // cores
            target = f if (t % 2 == 0) == early else (f + cores) % spread
            moves.append((t * spread + f, target * spread + x * cores + t * cores // planes))
        return moves

    rise, fall = climb(True), climb(False)
    outer = [(0, 1), (1, 0), (last - 1, last), (last, last - 1)]
    line = [[(k, k + 1), (last - k, last - k - 1)] for k in range(last)]
    far_at, near_at = jnp.where(near_left, 1, 0), jnp.where(near_left, 0, 1)

    def part(array, at, size):
        return lax.dynamic_slice_in_dim(array, at * size, size, 1)

    pair_weight = lambda at: jnp.concatenate([part(key_weight, at, half_k), part(value_weight, at, half_k)], axis=1)
    wp_near, wp_far = pair_weight(near_at), pair_weight(far_at)
    wq_near, wq_far = part(query_weight, near_at, half_q), part(query_weight, far_at, half_q)
    g_near, g_far = part(out_grad, near_at, half_q), part(out_grad, far_at, half_q)
    begins = jnp.sum((doc_ids[None, :] < doc_ids[:, None]).astype(jnp.int32), axis=1).reshape(1, total)
    flags = jnp.stack([is_end, plane == 0]).astype(jnp.int32)

    part_rows = tok // across
    mine = lax.dynamic_slice_in_dim(layer_input, side * part_rows, part_rows, 0)
    other = lax.dynamic_slice_in_dim(layer_input, (1 - side) * part_rows, part_rows, 0)
    other = swap(other, "hid", across)
    even_plane = plane % 2 == 0
    up = lax.ppermute(jnp.where(even_plane, mine, other), trio, rise)
    down = lax.ppermute(jnp.where(even_plane, other, mine), trio, fall)
    straight_first = jnp.where(side == plane // cores, 0, 1)
    held = planes // cores
    slot = lambda owner, which, half: (owner * held + which) * across + half
    slots = []
    for which in (straight_first, 1 - straight_first):
        slots += [slot(core, which, side), slot(1 - core, which, side)]
        slots += [slot(core, 1 - which, 1 - side), slot(1 - core, 1 - which, 1 - side)]
    slots = jnp.stack(slots).astype(jnp.int32)
    wp_near, wp_far, wq_near, wq_far, g_near, g_far, begins, flags, slots, up = lax.optimization_barrier(
        (wp_near, wp_far, wq_near, wq_far, g_near, g_far, begins, flags, slots, up)
    )
    pieces = []
    for piece in (up, down):
        turned = swap(piece, "hid", across)
        mate = swap(piece, "rep", cores)
        turned_mate = swap(turned, "rep", cores)
        pieces += [piece, mate, turned, turned_mate]
    rows_all = place_pieces(slots, pieces)
    x_rows = [lax.slice_in_dim(rows_all, b * tok, (b + 1) * tok, axis=0) for b in range(planes)]

    g_next = lax.ppermute(jnp.where(is_end, g_far, g_near), "srv", outer)
    g_over = lax.ppermute(g_far, "srv", line[1])
    g_end = lax.ppermute(g_next, "srv", line[1])
    riders = {2: g_over, 3: g_end}
    g_pieces = [g_next]

    middle = total // 2
    chunks = [(rows_all[middle:], wp_far, wp_near), (rows_all[:middle], wp_far, wp_near)]
    chunks += [(x_rows[b], wq_far, wq_near) for b in range(blocks - 1, -1, -1)]
    landed = []
    for c, (x, w_far, w_near) in enumerate(chunks):
        far_part = jnp.dot(x, w_far, preferred_element_type=f32)
        near_part = jnp.dot(x, w_near, preferred_element_type=f32)
        moving = None
        for k in range(last):
            mine_now = far_part if k < planes // 2 else near_part
            if moving is not None:
                mine_now = mine_now + moving.astype(f32)
            mine_now = mine_now.astype(bf16)
            if k == 0 and c in riders:
                moving = lax.ppermute(jnp.where(is_end, mine_now, riders[c]), "srv", outer)
                g_pieces.append(moving)
            elif c == len(chunks) - 1 and k == last - 1:
                moving = mine_now
            else:
                moving = lax.ppermute(mine_now, "srv", line[k])
        landed.append((near_part + moving.astype(f32)).astype(bf16) if c < 2 else (near_part, moving))

    pairs_at = [(landed[1], b * tok) if b < blocks // 2 else (landed[0], b * tok - middle) for b in range(blocks)]
    all_hops = [None] * blocks
    near_q, far_q, near_kv, far_kv = [[None] * blocks for _ in range(4)]
    sums = [None] * blocks
    lead = 2 * half_k
    g_near, *g_pieces, _ = lax.optimization_barrier((g_near, *g_pieces, landed[0]))
    for b in range(blocks - 1, -1, -1):
        g_first = g_pieces[b - 1] if b > 0 else g_near
        g_last = g_pieces[last - b - 1] if b < last else g_near
        fresh_q, moved_q = landed[2 + blocks - 1 - b]
        local = attend_block(flags, begins, pairs_at, fresh_q, moved_q, g_first, g_last, sums, b, middle // tok)
        hops = [local]
        for k in range(last):
            if b == blocks - 1 and k == 0:
                fresh_q, moved_q = landed[-1]
                wider = jnp.pad(moved_q, ((0, 0), (lead, 0)))
                hops.append(lax.ppermute(jnp.where(is_end, local, wider), "srv", outer))
                landed[-1] = (fresh_q, hops[1])
            else:
                hops.append(lax.ppermute(hops[k], "srv", line[k]))
        all_hops[b] = hops
        near = jnp.where(is_end, local, hops[1])
        far = jnp.where(is_end, hops[3], hops[2])
        near_q[b], far_q[b], near_kv[b], far_kv[b] = near[:, lead:], far[:, lead:], near[:, :lead], far[:, :lead]

    nt = (((1,), (1,)), ((), ()))
    times = lambda a, w: lax.dot_general(a, w, nt, preferred_element_type=f32)
    terms = []
    for b in range(blocks):
        near_term = times(near_q[b], wq_near) + times(near_kv[b], wp_near)
        terms.append(near_term + times(far_q[b], wq_far) + times(far_kv[b], wp_far))
    summed = []
    for i in range(blocks // cores):
        even, odd = terms[cores * i], terms[cores * i + 1]
        theirs = jnp.where(core == 0, odd, even).astype(bf16)
        ours = jnp.where(core == 0, even, odd)
        summed.append((ours + swap(theirs, "rep", cores).astype(f32)).astype(bf16))
    parts = []
    for i, block in reversed(list(enumerate(summed))):
        for x in range(across):
            home = [(a, b) for a, b in (straight if x == i else crossed) if a % spread // cores == x]
            parts.append(lax.ppermute(block, trio, home).astype(f32))
    input_grad = functools.reduce(jnp.add, parts).astype(bf16)

    shapes = [(width, w.shape[1]) for w in (query_weight, key_weight, value_weight)]
    outs = weight_grads(plane, rows_all, all_hops, planes, shapes)
    return (input_grad, *outs)


def solution(mesh):
    in_specs = (
        P(("groups", "srv"), ("hid", "rep")),
        P("srv", ("hid", "rep")),
        P("srv", ("hid", "rep")),
        P("srv", ("hid", "rep")),
        P(("groups", "srv"), ("hid", "rep")),
        P("groups"),
    )
    out_specs = (
        P(("groups", "srv"), ("hid", "rep")),
        P(("groups", "srv"), ("hid", "rep")),
        P(("groups", "srv"), ("hid", "rep")),
        P(("groups", "srv"), ("hid", "rep")),
    )
    sizes = (mesh.shape["srv"], mesh.shape["hid"], mesh.shape["rep"])
    split = HK // (sizes[1] * sizes[2])
    fits = sizes[0] == sizes[1] * sizes[2] and sizes[1] == 2 and sizes[2] == 2 and split == 2
    chosen = functools.partial(stationary_body, sizes) if fits else body
    return jax.shard_map(chosen, mesh=mesh, in_specs=in_specs, out_specs=out_specs, check_vma=False)
```

```python
import functools

import jax
import jax.numpy as jnp
from jax import lax
from jax.experimental import pallas as pl
from jax.experimental.pallas import tpu as pltpu
from jax.sharding import PartitionSpec as P


HQ = 32
HK = 8
DH = 128
BLOCK = 128


NEGATIVE = -1e30


def attend(queries, cotangent, keys_all, values_all, doc_ids, block_id, carried):
    row_count = queries.shape[0]
    factor_scale = queries.shape[-1] ** (-0.5)
    offsets = jnp.arange(row_count, dtype=jnp.int32)
    query_pos = block_id * row_count + offsets
    query_doc = lax.dynamic_slice_in_dim(doc_ids, block_id * row_count, row_count)
    doc_start = jnp.sum((doc_ids < query_doc[0]).astype(jnp.int32))
    lowest = doc_start // row_count
    highest = jnp.where(True, block_id + 1, lowest)

    def scores_at(key_block):
        key_rows = lax.dynamic_slice_in_dim(keys_all, key_block * row_count, row_count, 0)
        value_rows = lax.dynamic_slice_in_dim(values_all, key_block * row_count, row_count, 0)
        key_doc = lax.dynamic_slice_in_dim(doc_ids, key_block * row_count, row_count)
        key_pos = key_block * row_count + offsets
        allowed = (key_doc[None, :] == query_doc[:, None]) & (
            key_pos[None, :] <= query_pos[:, None]
        )
        logits = (
            jnp.einsum("qgnd,kgd->gnqk", queries, key_rows, preferred_element_type=jnp.float32)
            * factor_scale
        )
        logits = jnp.where(allowed, logits, NEGATIVE)
        slopes = jnp.einsum(
            "qgnd,kgd->gnqk", cotangent, value_rows, preferred_element_type=jnp.float32
        )
        return (key_rows, allowed, logits, slopes)

    def first_pass(key_block, loop_state):
        row_peak, row_total, row_inner = loop_state
        _, allowed, logits, slopes = scores_at(key_block)
        new_peak = jnp.maximum(row_peak, jnp.max(logits, axis=-1))
        weights = jnp.where(allowed, jnp.exp(logits - new_peak[..., None]), 0.0)
        factor = jnp.exp(row_peak - new_peak)
        row_total = row_total * factor + jnp.sum(weights, axis=-1)
        row_inner = row_inner * factor + jnp.sum(weights * slopes, axis=-1)
        return (new_peak, row_total, row_inner)

    stat_shape = (queries.shape[1], queries.shape[2], row_count)
    initial = (
        jnp.full(stat_shape, NEGATIVE, jnp.float32),
        jnp.zeros(stat_shape, jnp.float32),
        jnp.zeros(stat_shape, jnp.float32),
    )
    row_peak, row_total, row_inner = lax.fori_loop(lowest, highest, first_pass, initial)
    safe_total = jnp.where(True, row_total, 1.0)
    row_delta = row_inner / safe_total
    log_total = row_peak + jnp.log(safe_total)

    def second_pass(key_block, loop_state):
        query_grad, key_accum, value_accum = loop_state
        key_rows, allowed, logits, slopes = scores_at(key_block)
        attention = jnp.where(allowed, jnp.exp(logits - log_total[..., None]), 0.0)
        score_grad = (attention * (slopes - row_delta[..., None]) * factor_scale).astype(
            jnp.bfloat16
        )
        value_part = jnp.einsum(
            "gnqk,qgnd->kgd",
            attention.astype(jnp.bfloat16),
            cotangent,
            preferred_element_type=jnp.float32,
        )
        key_part = jnp.einsum(
            "gnqk,qgnd->kgd", score_grad, queries, preferred_element_type=jnp.float32
        )
        query_grad = query_grad + jnp.einsum(
            "gnqk,kgd->qgnd", score_grad, key_rows, preferred_element_type=jnp.float32
        )
        first_row = key_block * row_count
        key_accum = lax.dynamic_update_slice_in_dim(
            key_accum,
            lax.dynamic_slice_in_dim(key_accum, first_row, row_count, 0) + key_part,
            first_row,
            0,
        )
        value_accum = lax.dynamic_update_slice_in_dim(
            value_accum,
            lax.dynamic_slice_in_dim(value_accum, first_row, row_count, 0) + value_part,
            first_row,
            0,
        )
        return (query_grad, key_accum, value_accum)

    start_grad = jnp.zeros(queries.shape, jnp.float32)
    query_grad, key_accum, value_accum = lax.fori_loop(
        lowest, highest, second_pass, (start_grad, carried[0], carried[1])
    )
    return (query_grad, (key_accum, value_accum))


def body(layer_input, query_weight, key_weight, value_weight, out_grad, doc_ids):
    tok_rows = layer_input.shape[0]
    query_width = query_weight.shape[1]
    pair_width = key_weight.shape[1]
    key_heads = pair_width // DH
    group_size = HQ // HK
    block_count = tok_rows // BLOCK
    owner_id = lax.axis_index("srv")
    weights_all = lax.all_gather(
        jnp.concatenate([query_weight, key_weight, value_weight], axis=1), "srv", axis=0, tiled=True
    )
    inputs_all = lax.all_gather(layer_input, ("hid", "rep"), axis=1, tiled=True)
    projected = jnp.dot(inputs_all, weights_all, preferred_element_type=jnp.float32).astype(
        jnp.bfloat16
    )
    queries = projected[:, :query_width].reshape(block_count, BLOCK, key_heads, group_size, DH)
    keys_local = projected[:, query_width : query_width + pair_width]
    values_local = projected[:, query_width + pair_width :]
    keys_all, values_all = (
        lax.all_gather(keys_local, "srv", axis=0, tiled=True),
        lax.all_gather(values_local, "srv", axis=0, tiled=True),
    )
    total_rows = keys_all.shape[0]
    keys_all = keys_all.reshape(total_rows, key_heads, DH)
    values_all = values_all.reshape(total_rows, key_heads, DH)
    cotangent = out_grad.reshape(block_count, BLOCK, key_heads, group_size, DH)
    empty_accum = jnp.zeros((total_rows, key_heads, DH), jnp.float32)

    def own_block(position, loop_state):
        answers, carried = loop_state
        grad_q, carried = attend(
            lax.dynamic_index_in_dim(queries, position, 0, keepdims=False),
            lax.dynamic_index_in_dim(cotangent, position, 0, keepdims=False),
            keys_all,
            values_all,
            doc_ids,
            owner_id * block_count + position,
            carried,
        )
        answers = lax.dynamic_update_index_in_dim(answers, grad_q.astype(jnp.bfloat16), position, 0)
        return (answers, carried)

    answers = jnp.zeros(queries.shape, jnp.bfloat16)
    answers, carried = lax.fori_loop(
        0, block_count, own_block, (answers, (empty_accum, empty_accum))
    )
    query_grad = answers.reshape(tok_rows, query_width)
    key_accum, value_accum = carried
    key_sum, value_sum = (
        lax.psum_scatter(key_accum, "srv", scatter_dimension=0, tiled=True),
        lax.psum_scatter(value_accum, "srv", scatter_dimension=0, tiled=True),
    )
    grads_all = jnp.concatenate(
        [
            query_grad,
            key_sum.astype(jnp.bfloat16).reshape(tok_rows, pair_width),
            value_sum.astype(jnp.bfloat16).reshape(tok_rows, pair_width),
        ],
        axis=1,
    )
    input_terms = lax.dot_general(
        grads_all, weights_all, (((1,), (1,)), ((), ())), preferred_element_type=jnp.float32
    )
    input_grad = lax.psum_scatter(
        input_terms, ("hid", "rep"), scatter_dimension=1, tiled=True
    ).astype(jnp.bfloat16)
    columns = lax.all_to_all(inputs_all, "srv", split_axis=1, concat_axis=0, tiled=True)
    weight_grad = lax.dot_general(
        columns,
        lax.all_gather(grads_all, "srv", axis=0, tiled=True),
        (((0,), (0,)), ((), ())),
        preferred_element_type=jnp.float32,
    )
    return (
        input_grad,
        weight_grad[:, :query_width],
        weight_grad[:, query_width : query_width + pair_width],
        weight_grad[:, query_width + pair_width :],
    )


LOG2E = 1.4426950408889634


def swap(array, axis, size):
    return lax.ppermute(array, axis, [(i, (i + 1) % size) for i in range(size)])


def attention_kernel(flag_ref, *refs, back, heads, block_id, held, moved_at):
    count = back + 1
    start_hbm, new_hbm, old_hbm, ga_hbm, gb_hbm = refs[:5]
    pair_hbm = refs[5 : 5 + count]
    sum_hbm = refs[5 + count : 5 + count + held]
    outs = refs[5 + count + held : 6 + count + held + back]
    start_ref, new_ref, old_ref, g_ref, pair_ref, sum_ref, q_ref, out_ref, left_ref, sems = refs[-10:]
    block = g_ref.shape[0]
    scale = DH ** (-0.5)
    nt = (((1,), (1,)), ((), ()))
    first = block_id * block
    low = first - back * block

    @pl.when(flag_ref[0] != 0)
    def _():
        moved = old_hbm.at[:, pl.ds(moved_at, old_ref.shape[1])]
        copies = [(start_hbm, start_ref), (new_hbm, new_ref), (moved, old_ref)]
        copies += [(pair_hbm[j][0].at[pl.ds(pair_hbm[j][1], block)], pair_ref.at[j]) for j in range(count)]
        copies += [(sum_hbm[n], sum_ref.at[n]) for n in range(held)]
        moves = [pltpu.make_async_copy(a, b, sems.at[n]) for n, (a, b) in enumerate(copies)]
        for move in moves:
            move.start()
        from_first = pltpu.make_async_copy(ga_hbm, g_ref, sems.at[len(moves)])
        from_last = pltpu.make_async_copy(gb_hbm, g_ref, sems.at[len(moves)])

        @pl.when(flag_ref[1] != 0)
        def _():
            from_first.start()

        @pl.when(flag_ref[1] == 0)
        def _():
            from_last.start()

        for move in moves:
            move.wait()
        from_first.wait()
        q_ref[...] = (new_ref[...] + old_ref[...].astype(jnp.float32)).astype(q_ref.dtype)
        begin = start_ref[:, first : first + block]
        query_pos = lax.broadcasted_iota(jnp.int32, (block, block), 1)
        key_pos = lax.broadcasted_iota(jnp.int32, (block, block), 0)
        allowed = []
        for j in range(count):
            inside = key_pos >= begin - (low + j * block)
            allowed.append(inside & (key_pos <= query_pos) if j == back else inside)
        keys_t = [pair_ref[j][:, :DH].T for j in range(count)]
        dk, dv = [None] * count, [None] * count

        def front(h):
            q = q_ref[:, h * DH : (h + 1) * DH]
            g = g_ref[:, h * DH : (h + 1) * DH]
            logits, slopes = [], []
            for j in range(count):
                k, v = pair_ref[j][:, :DH], pair_ref[j][:, DH:]
                term = lax.dot_general(k, q, nt, preferred_element_type=jnp.float32) * (scale * LOG2E)
                logits.append(jnp.where(allowed[j], term, NEGATIVE))
                slopes.append(lax.dot_general(v, g, nt, preferred_element_type=jnp.float32))
            return q, g, logits, slopes

        ahead = front(0)
        for h in range(heads):
            q, g, logits, slopes = ahead
            if h + 1 < heads:
                ahead = front(h + 1)
            peak = functools.reduce(jnp.maximum, [jnp.max(t, axis=0, keepdims=True) for t in logits])
            weights = [jnp.exp2(t - peak) for t in logits]
            total = functools.reduce(jnp.add, [jnp.sum(w, axis=0, keepdims=True) for w in weights])
            inner = functools.reduce(jnp.add, [jnp.sum(w * t, axis=0, keepdims=True) for w, t in zip(weights, slopes)])
            inverse = 1.0 / total
            inner = inner * inverse
            dq = None
            for j in range(count):
                attention = weights[j] * inverse
                score = (attention * (slopes[j] - inner)).astype(jnp.bfloat16)
                value_part = jnp.dot(attention.astype(jnp.bfloat16), g, preferred_element_type=jnp.float32)
                key_part = jnp.dot(score, q, preferred_element_type=jnp.float32)
                dv[j] = value_part if dv[j] is None else dv[j] + value_part
                dk[j] = key_part if dk[j] is None else dk[j] + key_part
                part = jnp.dot(keys_t[j], score, preferred_element_type=jnp.float32)
                dq = part if dq is None else dq + part
            out_ref[:, (2 + h) * DH : (3 + h) * DH] = (dq * scale).T.astype(out_ref.dtype)
        fresh = count - held
        for j in range(count):
            new_k, new_v = dk[j] * scale, dv[j]
            if j >= fresh:
                new_k = new_k + sum_ref[j - fresh][:, :DH]
                new_v = new_v + sum_ref[j - fresh][:, DH:]
            if j == back:
                out_ref[:, :DH] = new_k.astype(out_ref.dtype)
                out_ref[:, DH : 2 * DH] = new_v.astype(out_ref.dtype)
            else:
                left_ref[j, :, :DH] = new_k
                left_ref[j, :, DH:] = new_v
        moves = [pltpu.make_async_copy(out_ref, outs[0], sems.at[0])]
        moves += [pltpu.make_async_copy(left_ref.at[j], outs[1 + j], sems.at[1 + j]) for j in range(back)]
        for move in moves:
            move.start()
        for move in moves:
            move.wait()


def attend_block(flags, begins, pairs, fresh_q, moved_q, g_first, g_last, sums, block_id, reach):
    block, width = g_first.shape
    heads = width // DH
    back = min(reach, block_id)
    low = block_id - back
    count = back + 1
    held = [sums[j] for j in range(low, block_id + 1) if sums[j] is not None]
    f32, bf16 = jnp.float32, jnp.bfloat16
    hbm = pl.BlockSpec(memory_space=pl.ANY)
    sum_shape = (block, 2 * DH)
    outs = [jax.ShapeDtypeStruct((block, 2 * DH + width), bf16)] + [jax.ShapeDtypeStruct(sum_shape, f32)] * back
    rows = [pairs[j][1] for j in range(low, block_id + 1)]
    operands = [begins, fresh_q, moved_q, g_first, g_last] + [pairs[j][0] for j in range(low, block_id + 1)] + held

    def kernel(flag_ref, *refs):
        refs = list(refs)
        refs[5 : 5 + count] = list(zip(refs[5 : 5 + count], rows))
        attention_kernel(flag_ref, *refs, back=back, heads=heads, block_id=block_id, held=len(held), moved_at=moved_q.shape[1] - width)

    results = pl.pallas_call(
        kernel,
        in_specs=[pl.BlockSpec(memory_space=pltpu.SMEM)] + [hbm] * len(operands),
        out_specs=[hbm] * len(outs),
        out_shape=outs,
        scratch_shapes=[
            pltpu.VMEM(begins.shape, jnp.int32),
            pltpu.VMEM((block, width), f32),
            pltpu.VMEM((block, width), bf16),
            pltpu.VMEM((block, width), bf16),
            pltpu.VMEM((count,) + sum_shape, bf16),
            pltpu.VMEM((max(1, len(held)),) + sum_shape, f32),
            pltpu.VMEM((block, width), bf16),
            pltpu.VMEM((block, 2 * DH + width), bf16),
            pltpu.VMEM((max(1, back),) + sum_shape, f32),
            pltpu.SemaphoreType.DMA((4 + count + len(held),)),
        ],
        cost_estimate=pl.CostEstimate(
            flops=10 * heads * DH * block * block * count, bytes_accessed=3 * block * 8 * DH, transcendentals=heads * block * block * count
        ),
    )(flags, *operands)
    for j in range(back):
        sums[low + j] = results[1 + j]
    return results[0]


def weight_grad_kernel(plane_ref, *refs, planes, blocks):
    x_hbm = refs[0]
    hops = refs[1 : 1 + blocks * planes]
    out_q, out_k, out_v = refs[1 + blocks * planes : 4 + blocks * planes]
    x_ref, left_ref, right_ref, q_ref, k_ref, v_ref, sems, out_sems = refs[4 + blocks * planes :]
    rows = left_ref.shape[0] // blocks
    tile = q_ref.shape[1]
    half_q = q_ref.shape[2] // 2
    move_x = pltpu.make_async_copy(x_hbm, x_ref, sems.at[0])
    move_x.start()

    def fetch(b, source, target, n):
        return pltpu.make_async_copy(source, target.at[pl.ds(b * rows, rows)], sems.at[n])

    for z in range(planes):

        @pl.when(plane_ref[0] == z)
        def _(z=z):
            for b in range(blocks):
                fetch(b, hops[b * planes + z], left_ref, 1 + 2 * b).start()
                fetch(b, hops[b * planes + planes - 1 - z], right_ref, 2 + 2 * b).start()

    move_x.wait()
    for b in range(blocks):
        fetch(b, hops[b * planes], left_ref, 1 + 2 * b).wait()
        fetch(b, hops[b * planes], right_ref, 2 + 2 * b).wait()

    def store(step, slot):
        at = pl.ds(pl.multiple_of(step * tile, tile), tile)
        return [
            pltpu.make_async_copy(ref.at[slot], out.at[at], out_sems.at[slot, n])
            for n, (ref, out) in enumerate(((q_ref, out_q), (k_ref, out_k), (v_ref, out_v)))
        ]

    steps = x_ref.shape[1] // tile

    def body(step, carry):
        slot = step % 2

        @pl.when(step >= 2)
        def _():
            for move in store(step, slot):
                move.wait()

        x_t = x_ref[:, pl.ds(pl.multiple_of(step * tile, tile), tile)].T
        for side, ref in enumerate((left_ref, right_ref)):
            result = jnp.dot(x_t, ref[...], preferred_element_type=jnp.float32)
            k_ref[slot, :, side * DH : (side + 1) * DH] = result[:, :DH]
            v_ref[slot, :, side * DH : (side + 1) * DH] = result[:, DH : 2 * DH]
            q_ref[slot, :, side * half_q : (side + 1) * half_q] = result[:, 2 * DH :]
        for move in store(step, slot):
            move.start()
        return carry

    lax.fori_loop(0, steps, body, 0)
    for slot in range(2):
        for move in store(slot, slot):
            move.wait()


def weight_grads(plane, x, hops, planes, shapes):
    total, width = x.shape
    blocks = len(hops)
    flat = [array for group in hops for array in group]
    tile = 256
    f32, bf16 = jnp.float32, jnp.bfloat16
    hbm = pl.BlockSpec(memory_space=pl.ANY)
    columns = flat[0].shape[1]
    return pl.pallas_call(
        functools.partial(weight_grad_kernel, planes=planes, blocks=blocks),
        in_specs=[pl.BlockSpec(memory_space=pltpu.SMEM)] + [hbm] * (1 + len(flat)),
        out_specs=[hbm] * 3,
        out_shape=[jax.ShapeDtypeStruct(s, f32) for s in shapes],
        scratch_shapes=[
            pltpu.VMEM((total, width), bf16),
            pltpu.VMEM((total, columns), bf16),
            pltpu.VMEM((total, columns), bf16),
        ]
        + [pltpu.VMEM((2, tile, s[1]), f32) for s in shapes]
        + [pltpu.SemaphoreType.DMA((1 + 2 * blocks,)), pltpu.SemaphoreType.DMA((2, 3))],
        cost_estimate=pl.CostEstimate(flops=4 * total * width * columns, bytes_accessed=8 * total * width, transcendentals=0),
    )(plane.astype(jnp.int32).reshape(1), x, *flat)


def place_kernel(at_ref, w_hbm, *refs):
    pieces, (rows_hbm, first_hbm, sent_hbm, x_ref, w_ref, first_ref, sent_ref, sems) = refs[:-8], refs[-8:]
    rows, count = pieces[0].shape[0], len(pieces)
    moves = [pltpu.make_async_copy(w_hbm, w_ref, sems.at[count])]
    for n, piece in enumerate(pieces):
        row = pl.multiple_of(at_ref[n] * rows, rows)
        moves.append(pltpu.make_async_copy(piece, x_ref.at[pl.ds(row, rows)], sems.at[n]))
    for move in moves:
        move.start()
    for move in moves:
        move.wait()
    keep = pltpu.make_async_copy(x_ref, rows_hbm, sems.at[0])
    keep.start()
    middle = x_ref.shape[0] // 2
    product = jnp.dot(x_ref[middle:, :], w_ref[...], preferred_element_type=jnp.float32)
    first_ref[...] = product
    sent_ref[...] = product.astype(sent_ref.dtype)
    give = pltpu.make_async_copy(sent_ref, sent_hbm, sems.at[1])
    hold = pltpu.make_async_copy(first_ref, first_hbm, sems.at[2])
    give.start()
    hold.start()
    give.wait()
    hold.wait()
    keep.wait()


def place_pieces(slots, pieces, weight):
    rows, width = pieces[0].shape
    count = len(pieces)
    total, columns = rows * count, weight.shape[1]
    f32, bf16 = jnp.float32, jnp.bfloat16
    hbm = pl.BlockSpec(memory_space=pl.ANY)
    half = (total // 2, columns)
    return pl.pallas_call(
        place_kernel,
        in_specs=[pl.BlockSpec(memory_space=pltpu.SMEM)] + [hbm] * (1 + count),
        out_specs=[hbm] * 3,
        out_shape=[jax.ShapeDtypeStruct((total, width), bf16), jax.ShapeDtypeStruct(half, f32), jax.ShapeDtypeStruct(half, bf16)],
        scratch_shapes=[
            pltpu.VMEM((total, width), bf16),
            pltpu.VMEM(weight.shape, bf16),
            pltpu.VMEM(half, f32),
            pltpu.VMEM(half, bf16),
            pltpu.SemaphoreType.DMA((count + 1,)),
        ],
        cost_estimate=pl.CostEstimate(flops=total * width * columns, bytes_accessed=4 * total * width, transcendentals=0),
    )(slots, weight, *pieces)


def stationary_body(sizes, *arrays):
    return stationary(sizes, *arrays)


def stationary(sizes, layer_input, query_weight, key_weight, value_weight, out_grad, doc_ids):
    planes, across, cores = sizes
    spread = across * cores
    f32, bf16 = jnp.float32, jnp.bfloat16
    tok, width = layer_input.shape
    total = tok * planes
    half_q, half_k = query_weight.shape[1] // 2, key_weight.shape[1] // 2
    plane = lax.axis_index("srv")
    side, core = lax.axis_index("hid"), lax.axis_index("rep")
    last = planes - 1
    blocks = planes
    near_left = plane < planes // 2
    is_end = (plane == 0) | (plane == last)
    trio = ("srv", "hid", "rep")
    pairs = [(t, f) for t in range(planes) for f in range(spread)]
    straight = [(t * spread + f, f * spread + t) for t, f in pairs]
    crossed = [(t * spread + f, (f + cores) % spread * spread + t) for t, f in pairs]

    def climb(early):
        moves = []
        for t, f in pairs:
            x = f // cores
            target = f if (t % 2 == 0) == early else (f + cores) % spread
            moves.append((t * spread + f, target * spread + x * cores + t * cores // planes))
        return moves

    rise, fall = climb(True), climb(False)
    outer = [(0, 1), (1, 0), (last - 1, last), (last, last - 1)]
    line = [[(k, k + 1), (last - k, last - k - 1)] for k in range(last)]
    far_at, near_at = jnp.where(near_left, 1, 0), jnp.where(near_left, 0, 1)

    def part(array, at, size):
        return lax.dynamic_slice_in_dim(array, at * size, size, 1)

    pair_weight = lambda at: jnp.concatenate([part(key_weight, at, half_k), part(value_weight, at, half_k)], axis=1)
    wp_near, wp_far = pair_weight(near_at), pair_weight(far_at)
    wq_near, wq_far = part(query_weight, near_at, half_q), part(query_weight, far_at, half_q)
    g_near, g_far = part(out_grad, near_at, half_q), part(out_grad, far_at, half_q)
    begins = jnp.sum((doc_ids[None, :] < doc_ids[:, None]).astype(jnp.int32), axis=1).reshape(1, total)
    flags = jnp.stack([is_end, plane == 0]).astype(jnp.int32)

    part_rows = tok // across
    mine = lax.dynamic_slice_in_dim(layer_input, side * part_rows, part_rows, 0)
    other = lax.dynamic_slice_in_dim(layer_input, (1 - side) * part_rows, part_rows, 0)
    other = swap(other, "hid", across)
    even_plane = plane % 2 == 0
    rising = jnp.where(even_plane, mine, other)
    mine, other, rising = lax.optimization_barrier((mine, other, rising))
    up = lax.ppermute(rising, trio, rise)
    down = lax.ppermute(jnp.where(even_plane, other, mine), trio, fall)
    straight_first = jnp.where(side == plane // cores, 0, 1)
    held = planes // cores
    slot = lambda owner, which, half: (owner * held + which) * across + half
    slots = []
    for which in (straight_first, 1 - straight_first):
        slots += [slot(core, which, side), slot(1 - core, which, side)]
        slots += [slot(core, 1 - which, 1 - side), slot(1 - core, 1 - which, 1 - side)]
    slots = jnp.stack(slots).astype(jnp.int32)
    wp_near, wp_far, wq_near, wq_far, g_near, g_far, begins, flags, slots, up = lax.optimization_barrier(
        (wp_near, wp_far, wq_near, wq_far, g_near, g_far, begins, flags, slots, up)
    )
    pieces = []
    for piece in (up, down):
        turned = swap(piece, "hid", across)
        mate = swap(piece, "rep", cores)
        turned_mate = swap(turned, "rep", cores)
        pieces += [piece, mate, turned, turned_mate]
    rows_all, first_far, first_sent = place_pieces(slots, pieces, wp_far)
    x_rows = [lax.slice_in_dim(rows_all, b * tok, (b + 1) * tok, axis=0) for b in range(planes)]

    g_next = lax.ppermute(jnp.where(is_end, g_far, g_near), "srv", outer)
    g_over = lax.ppermute(g_far, "srv", line[1])
    g_end = lax.ppermute(g_next, "srv", line[1])
    riders = {2: g_over, 3: g_end}
    g_pieces = [g_next]

    middle = total // 2
    chunks = [(rows_all[middle:], wp_far, wp_near), (rows_all[:middle], wp_far, wp_near)]
    chunks += [(x_rows[b], wq_far, wq_near) for b in range(blocks - 1, -1, -1)]
    landed = []
    for c, (x, w_far, w_near) in enumerate(chunks):
        far_part = first_far if c == 0 else jnp.dot(x, w_far, preferred_element_type=f32)
        near_part = jnp.dot(x, w_near, preferred_element_type=f32)
        moving = None
        for k in range(last):
            mine_now = far_part if k < planes // 2 else near_part
            if moving is not None:
                mine_now = mine_now + moving.astype(f32)
            mine_now = first_sent if c == 0 and k == 0 else mine_now.astype(bf16)
            if k == 0 and c in riders:
                moving = lax.ppermute(jnp.where(is_end, mine_now, riders[c]), "srv", outer)
                g_pieces.append(moving)
            elif c == len(chunks) - 1 and k == last - 1:
                moving = mine_now
            else:
                moving = lax.ppermute(mine_now, "srv", line[k])
        landed.append((near_part + moving.astype(f32)).astype(bf16) if c < 2 else (near_part, moving))

    pairs_at = [(landed[1], b * tok) if b < blocks // 2 else (landed[0], b * tok - middle) for b in range(blocks)]
    all_hops = [None] * blocks
    near_q, far_q, near_kv, far_kv = [[None] * blocks for _ in range(4)]
    sums = [None] * blocks
    lead = 2 * half_k
    g_near, *g_pieces, _ = lax.optimization_barrier((g_near, *g_pieces, landed[0]))
    for b in range(blocks - 1, -1, -1):
        g_first = g_pieces[b - 1] if b > 0 else g_near
        g_last = g_pieces[last - b - 1] if b < last else g_near
        fresh_q, moved_q = landed[2 + blocks - 1 - b]
        local = attend_block(flags, begins, pairs_at, fresh_q, moved_q, g_first, g_last, sums, b, middle // tok)
        hops = [local]
        for k in range(last):
            if b == blocks - 1 and k == 0:
                fresh_q, moved_q = landed[-1]
                wider = jnp.pad(moved_q, ((0, 0), (lead, 0)))
                hops.append(lax.ppermute(jnp.where(is_end, local, wider), "srv", outer))
                landed[-1] = (fresh_q, hops[1])
            else:
                hops.append(lax.ppermute(hops[k], "srv", line[k]))
        all_hops[b] = hops
        near = jnp.where(is_end, local, hops[1])
        far = jnp.where(is_end, hops[3], hops[2])
        near_q[b], far_q[b], near_kv[b], far_kv[b] = near[:, lead:], far[:, lead:], near[:, :lead], far[:, :lead]

    nt = (((1,), (1,)), ((), ()))
    times = lambda a, w: lax.dot_general(a, w, nt, preferred_element_type=f32)
    terms = []
    for b in range(blocks):
        near_term = times(near_q[b], wq_near) + times(near_kv[b], wp_near)
        terms.append(near_term + times(far_q[b], wq_far) + times(far_kv[b], wp_far))
    summed = []
    for i in range(blocks // cores):
        even, odd = terms[cores * i], terms[cores * i + 1]
        theirs = jnp.where(core == 0, odd, even).astype(bf16)
        ours = jnp.where(core == 0, even, odd)
        summed.append((ours + swap(theirs, "rep", cores).astype(f32)).astype(bf16))
    parts = []
    for i, block in reversed(list(enumerate(summed))):
        for x in range(across):
            home = [(a, b) for a, b in (straight if x == i else crossed) if a % spread // cores == x]
            parts.append(lax.ppermute(block, trio, home).astype(f32))
    input_grad = functools.reduce(jnp.add, parts).astype(bf16)

    shapes = [(width, w.shape[1]) for w in (query_weight, key_weight, value_weight)]
    outs = weight_grads(plane, rows_all, all_hops, planes, shapes)
    return (input_grad, *outs)


def solution(mesh):
    in_specs = (
        P(("groups", "srv"), ("hid", "rep")),
        P("srv", ("hid", "rep")),
        P("srv", ("hid", "rep")),
        P("srv", ("hid", "rep")),
        P(("groups", "srv"), ("hid", "rep")),
        P("groups"),
    )
    out_specs = (
        P(("groups", "srv"), ("hid", "rep")),
        P(("groups", "srv"), ("hid", "rep")),
        P(("groups", "srv"), ("hid", "rep")),
        P(("groups", "srv"), ("hid", "rep")),
    )
    sizes = (mesh.shape["srv"], mesh.shape["hid"], mesh.shape["rep"])
    split = HK // (sizes[1] * sizes[2])
    fits = sizes[0] == sizes[1] * sizes[2] and sizes[1] == 2 and sizes[2] == 2 and split == 2
    chosen = functools.partial(stationary_body, sizes) if fits else body
    return jax.shard_map(chosen, mesh=mesh, in_specs=in_specs, out_specs=out_specs, check_vma=False)
```

```python
import functools

import jax
import jax.numpy as jnp
from jax import lax
from jax.experimental import pallas as pl
from jax.experimental.pallas import tpu as pltpu
from jax.sharding import PartitionSpec as P


HQ = 32
HK = 8
DH = 128
BLOCK = 128


NEGATIVE = -1e30


def attend(queries, cotangent, keys_all, values_all, doc_ids, block_id, carried):
    row_count = queries.shape[0]
    factor_scale = queries.shape[-1] ** (-0.5)
    offsets = jnp.arange(row_count, dtype=jnp.int32)
    query_pos = block_id * row_count + offsets
    query_doc = lax.dynamic_slice_in_dim(doc_ids, block_id * row_count, row_count)
    doc_start = jnp.sum((doc_ids < query_doc[0]).astype(jnp.int32))
    lowest = doc_start // row_count
    highest = jnp.where(True, block_id + 1, lowest)

    def scores_at(key_block):
        key_rows = lax.dynamic_slice_in_dim(keys_all, key_block * row_count, row_count, 0)
        value_rows = lax.dynamic_slice_in_dim(values_all, key_block * row_count, row_count, 0)
        key_doc = lax.dynamic_slice_in_dim(doc_ids, key_block * row_count, row_count)
        key_pos = key_block * row_count + offsets
        allowed = (key_doc[None, :] == query_doc[:, None]) & (
            key_pos[None, :] <= query_pos[:, None]
        )
        logits = (
            jnp.einsum("qgnd,kgd->gnqk", queries, key_rows, preferred_element_type=jnp.float32)
            * factor_scale
        )
        logits = jnp.where(allowed, logits, NEGATIVE)
        slopes = jnp.einsum(
            "qgnd,kgd->gnqk", cotangent, value_rows, preferred_element_type=jnp.float32
        )
        return (key_rows, allowed, logits, slopes)

    def first_pass(key_block, loop_state):
        row_peak, row_total, row_inner = loop_state
        _, allowed, logits, slopes = scores_at(key_block)
        new_peak = jnp.maximum(row_peak, jnp.max(logits, axis=-1))
        weights = jnp.where(allowed, jnp.exp(logits - new_peak[..., None]), 0.0)
        factor = jnp.exp(row_peak - new_peak)
        row_total = row_total * factor + jnp.sum(weights, axis=-1)
        row_inner = row_inner * factor + jnp.sum(weights * slopes, axis=-1)
        return (new_peak, row_total, row_inner)

    stat_shape = (queries.shape[1], queries.shape[2], row_count)
    initial = (
        jnp.full(stat_shape, NEGATIVE, jnp.float32),
        jnp.zeros(stat_shape, jnp.float32),
        jnp.zeros(stat_shape, jnp.float32),
    )
    row_peak, row_total, row_inner = lax.fori_loop(lowest, highest, first_pass, initial)
    safe_total = jnp.where(True, row_total, 1.0)
    row_delta = row_inner / safe_total
    log_total = row_peak + jnp.log(safe_total)

    def second_pass(key_block, loop_state):
        query_grad, key_accum, value_accum = loop_state
        key_rows, allowed, logits, slopes = scores_at(key_block)
        attention = jnp.where(allowed, jnp.exp(logits - log_total[..., None]), 0.0)
        score_grad = (attention * (slopes - row_delta[..., None]) * factor_scale).astype(
            jnp.bfloat16
        )
        value_part = jnp.einsum(
            "gnqk,qgnd->kgd",
            attention.astype(jnp.bfloat16),
            cotangent,
            preferred_element_type=jnp.float32,
        )
        key_part = jnp.einsum(
            "gnqk,qgnd->kgd", score_grad, queries, preferred_element_type=jnp.float32
        )
        query_grad = query_grad + jnp.einsum(
            "gnqk,kgd->qgnd", score_grad, key_rows, preferred_element_type=jnp.float32
        )
        first_row = key_block * row_count
        key_accum = lax.dynamic_update_slice_in_dim(
            key_accum,
            lax.dynamic_slice_in_dim(key_accum, first_row, row_count, 0) + key_part,
            first_row,
            0,
        )
        value_accum = lax.dynamic_update_slice_in_dim(
            value_accum,
            lax.dynamic_slice_in_dim(value_accum, first_row, row_count, 0) + value_part,
            first_row,
            0,
        )
        return (query_grad, key_accum, value_accum)

    start_grad = jnp.zeros(queries.shape, jnp.float32)
    query_grad, key_accum, value_accum = lax.fori_loop(
        lowest, highest, second_pass, (start_grad, carried[0], carried[1])
    )
    return (query_grad, (key_accum, value_accum))


def body(layer_input, query_weight, key_weight, value_weight, out_grad, doc_ids):
    tok_rows = layer_input.shape[0]
    query_width = query_weight.shape[1]
    pair_width = key_weight.shape[1]
    key_heads = pair_width // DH
    group_size = HQ // HK
    block_count = tok_rows // BLOCK
    owner_id = lax.axis_index("srv")
    weights_all = lax.all_gather(
        jnp.concatenate([query_weight, key_weight, value_weight], axis=1), "srv", axis=0, tiled=True
    )
    inputs_all = lax.all_gather(layer_input, ("hid", "rep"), axis=1, tiled=True)
    projected = jnp.dot(inputs_all, weights_all, preferred_element_type=jnp.float32).astype(
        jnp.bfloat16
    )
    queries = projected[:, :query_width].reshape(block_count, BLOCK, key_heads, group_size, DH)
    keys_local = projected[:, query_width : query_width + pair_width]
    values_local = projected[:, query_width + pair_width :]
    keys_all, values_all = (
        lax.all_gather(keys_local, "srv", axis=0, tiled=True),
        lax.all_gather(values_local, "srv", axis=0, tiled=True),
    )
    total_rows = keys_all.shape[0]
    keys_all = keys_all.reshape(total_rows, key_heads, DH)
    values_all = values_all.reshape(total_rows, key_heads, DH)
    cotangent = out_grad.reshape(block_count, BLOCK, key_heads, group_size, DH)
    empty_accum = jnp.zeros((total_rows, key_heads, DH), jnp.float32)

    def own_block(position, loop_state):
        answers, carried = loop_state
        grad_q, carried = attend(
            lax.dynamic_index_in_dim(queries, position, 0, keepdims=False),
            lax.dynamic_index_in_dim(cotangent, position, 0, keepdims=False),
            keys_all,
            values_all,
            doc_ids,
            owner_id * block_count + position,
            carried,
        )
        answers = lax.dynamic_update_index_in_dim(answers, grad_q.astype(jnp.bfloat16), position, 0)
        return (answers, carried)

    answers = jnp.zeros(queries.shape, jnp.bfloat16)
    answers, carried = lax.fori_loop(
        0, block_count, own_block, (answers, (empty_accum, empty_accum))
    )
    query_grad = answers.reshape(tok_rows, query_width)
    key_accum, value_accum = carried
    key_sum, value_sum = (
        lax.psum_scatter(key_accum, "srv", scatter_dimension=0, tiled=True),
        lax.psum_scatter(value_accum, "srv", scatter_dimension=0, tiled=True),
    )
    grads_all = jnp.concatenate(
        [
            query_grad,
            key_sum.astype(jnp.bfloat16).reshape(tok_rows, pair_width),
            value_sum.astype(jnp.bfloat16).reshape(tok_rows, pair_width),
        ],
        axis=1,
    )
    input_terms = lax.dot_general(
        grads_all, weights_all, (((1,), (1,)), ((), ())), preferred_element_type=jnp.float32
    )
    input_grad = lax.psum_scatter(
        input_terms, ("hid", "rep"), scatter_dimension=1, tiled=True
    ).astype(jnp.bfloat16)
    columns = lax.all_to_all(inputs_all, "srv", split_axis=1, concat_axis=0, tiled=True)
    weight_grad = lax.dot_general(
        columns,
        lax.all_gather(grads_all, "srv", axis=0, tiled=True),
        (((0,), (0,)), ((), ())),
        preferred_element_type=jnp.float32,
    )
    return (
        input_grad,
        weight_grad[:, :query_width],
        weight_grad[:, query_width : query_width + pair_width],
        weight_grad[:, query_width + pair_width :],
    )


LOG2E = 1.4426950408889634


def swap(array, axis, size):
    return lax.ppermute(array, axis, [(i, (i + 1) % size) for i in range(size)])


def attention_kernel(flag_ref, *refs, back, heads, block_id, held, moved_at):
    count = back + 1
    start_hbm, new_hbm, old_hbm, ga_hbm, gb_hbm = refs[:5]
    pair_hbm = refs[5 : 5 + count]
    sum_hbm = refs[5 + count : 5 + count + held]
    outs = refs[5 + count + held : 6 + count + held + back]
    start_ref, new_ref, old_ref, g_ref, pair_ref, sum_ref, q_ref, out_ref, left_ref, sems = refs[-10:]
    block = g_ref.shape[0]
    scale = DH ** (-0.5)
    nt = (((1,), (1,)), ((), ()))
    first = block_id * block
    low = first - back * block

    @pl.when(flag_ref[0] != 0)
    def _():
        moved = old_hbm.at[:, pl.ds(moved_at, old_ref.shape[1])]
        copies = [(start_hbm, start_ref), (new_hbm, new_ref), (moved, old_ref)]
        copies += [(pair_hbm[j][0].at[pl.ds(pair_hbm[j][1], block)], pair_ref.at[j]) for j in range(count)]
        copies += [(sum_hbm[n], sum_ref.at[n]) for n in range(held)]
        moves = [pltpu.make_async_copy(a, b, sems.at[n]) for n, (a, b) in enumerate(copies)]
        for move in moves:
            move.start()
        from_first = pltpu.make_async_copy(ga_hbm, g_ref, sems.at[len(moves)])
        from_last = pltpu.make_async_copy(gb_hbm, g_ref, sems.at[len(moves)])

        @pl.when(flag_ref[1] != 0)
        def _():
            from_first.start()

        @pl.when(flag_ref[1] == 0)
        def _():
            from_last.start()

        for move in moves:
            move.wait()
        from_first.wait()
        q_ref[...] = (new_ref[...] + old_ref[...].astype(jnp.float32)).astype(q_ref.dtype)
        begin = start_ref[:, first : first + block]
        query_pos = lax.broadcasted_iota(jnp.int32, (block, block), 1)
        key_pos = lax.broadcasted_iota(jnp.int32, (block, block), 0)
        allowed = []
        for j in range(count):
            inside = key_pos >= begin - (low + j * block)
            allowed.append(inside & (key_pos <= query_pos) if j == back else inside)
        keys_t = [pair_ref[j][:, :DH].T for j in range(count)]
        dk, dv = [None] * count, [None] * count

        def front(h):
            q = q_ref[:, h * DH : (h + 1) * DH]
            g = g_ref[:, h * DH : (h + 1) * DH]
            logits, slopes = [], []
            for j in range(count):
                k, v = pair_ref[j][:, :DH], pair_ref[j][:, DH:]
                term = lax.dot_general(k, q, nt, preferred_element_type=jnp.float32) * (scale * LOG2E)
                logits.append(jnp.where(allowed[j], term, NEGATIVE))
                slopes.append(lax.dot_general(v, g, nt, preferred_element_type=jnp.float32))
            return q, g, logits, slopes

        ahead = front(0)
        for h in range(heads):
            q, g, logits, slopes = ahead
            if h + 1 < heads:
                ahead = front(h + 1)
            peak = functools.reduce(jnp.maximum, [jnp.max(t, axis=0, keepdims=True) for t in logits])
            weights = [jnp.exp2(t - peak) for t in logits]
            total = functools.reduce(jnp.add, [jnp.sum(w, axis=0, keepdims=True) for w in weights])
            inner = functools.reduce(jnp.add, [jnp.sum(w * t, axis=0, keepdims=True) for w, t in zip(weights, slopes)])
            inverse = 1.0 / total
            inner = inner * inverse
            dq = None
            for j in range(count):
                attention = weights[j] * inverse
                score = (attention * (slopes[j] - inner)).astype(jnp.bfloat16)
                value_part = jnp.dot(attention.astype(jnp.bfloat16), g, preferred_element_type=jnp.float32)
                key_part = jnp.dot(score, q, preferred_element_type=jnp.float32)
                dv[j] = value_part if dv[j] is None else dv[j] + value_part
                dk[j] = key_part if dk[j] is None else dk[j] + key_part
                part = jnp.dot(keys_t[j], score, preferred_element_type=jnp.float32)
                dq = part if dq is None else dq + part
            out_ref[:, (2 + h) * DH : (3 + h) * DH] = (dq * scale).T.astype(out_ref.dtype)
        fresh = count - held
        for j in range(count):
            new_k, new_v = dk[j] * scale, dv[j]
            if j >= fresh:
                new_k = new_k + sum_ref[j - fresh][:, :DH]
                new_v = new_v + sum_ref[j - fresh][:, DH:]
            if j == back:
                out_ref[:, :DH] = new_k.astype(out_ref.dtype)
                out_ref[:, DH : 2 * DH] = new_v.astype(out_ref.dtype)
            else:
                left_ref[j, :, :DH] = new_k
                left_ref[j, :, DH:] = new_v
        moves = [pltpu.make_async_copy(out_ref, outs[0], sems.at[0])]
        moves += [pltpu.make_async_copy(left_ref.at[j], outs[1 + j], sems.at[1 + j]) for j in range(back)]
        for move in moves:
            move.start()
        for move in moves:
            move.wait()


def attend_block(flags, begins, pairs, fresh_q, moved_q, g_first, g_last, sums, block_id, reach):
    block, width = g_first.shape
    heads = width // DH
    back = min(reach, block_id)
    low = block_id - back
    count = back + 1
    held = [sums[j] for j in range(low, block_id + 1) if sums[j] is not None]
    f32, bf16 = jnp.float32, jnp.bfloat16
    hbm = pl.BlockSpec(memory_space=pl.ANY)
    sum_shape = (block, 2 * DH)
    outs = [jax.ShapeDtypeStruct((block, 2 * DH + width), bf16)] + [jax.ShapeDtypeStruct(sum_shape, f32)] * back
    rows = [pairs[j][1] for j in range(low, block_id + 1)]
    operands = [begins, fresh_q, moved_q, g_first, g_last] + [pairs[j][0] for j in range(low, block_id + 1)] + held

    def kernel(flag_ref, *refs):
        refs = list(refs)
        refs[5 : 5 + count] = list(zip(refs[5 : 5 + count], rows))
        attention_kernel(flag_ref, *refs, back=back, heads=heads, block_id=block_id, held=len(held), moved_at=moved_q.shape[1] - width)

    results = pl.pallas_call(
        kernel,
        in_specs=[pl.BlockSpec(memory_space=pltpu.SMEM)] + [hbm] * len(operands),
        out_specs=[hbm] * len(outs),
        out_shape=outs,
        scratch_shapes=[
            pltpu.VMEM(begins.shape, jnp.int32),
            pltpu.VMEM((block, width), f32),
            pltpu.VMEM((block, width), bf16),
            pltpu.VMEM((block, width), bf16),
            pltpu.VMEM((count,) + sum_shape, bf16),
            pltpu.VMEM((max(1, len(held)),) + sum_shape, f32),
            pltpu.VMEM((block, width), bf16),
            pltpu.VMEM((block, 2 * DH + width), bf16),
            pltpu.VMEM((max(1, back),) + sum_shape, f32),
            pltpu.SemaphoreType.DMA((4 + count + len(held),)),
        ],
        cost_estimate=pl.CostEstimate(
            flops=10 * heads * DH * block * block * count, bytes_accessed=3 * block * 8 * DH, transcendentals=heads * block * block * count
        ),
    )(flags, *operands)
    for j in range(back):
        sums[low + j] = results[1 + j]
    return results[0]


def weight_grad_kernel(plane_ref, *refs, planes, blocks):
    x_hbm = refs[0]
    hops = refs[1 : 1 + blocks * planes]
    out_q, out_k, out_v = refs[1 + blocks * planes : 4 + blocks * planes]
    x_ref, left_ref, right_ref, q_ref, k_ref, v_ref, sems, out_sems = refs[4 + blocks * planes :]
    rows = left_ref.shape[0] // blocks
    tile = q_ref.shape[1]
    half_q = q_ref.shape[2] // 2
    move_x = pltpu.make_async_copy(x_hbm, x_ref, sems.at[0])
    move_x.start()

    def fetch(b, source, target, n):
        return pltpu.make_async_copy(source, target.at[pl.ds(b * rows, rows)], sems.at[n])

    for z in range(planes):

        @pl.when(plane_ref[0] == z)
        def _(z=z):
            for b in range(blocks):
                fetch(b, hops[b * planes + z], left_ref, 1 + 2 * b).start()
                fetch(b, hops[b * planes + planes - 1 - z], right_ref, 2 + 2 * b).start()

    move_x.wait()
    for b in range(blocks):
        fetch(b, hops[b * planes], left_ref, 1 + 2 * b).wait()
        fetch(b, hops[b * planes], right_ref, 2 + 2 * b).wait()

    def store(step, slot):
        at = pl.ds(pl.multiple_of(step * tile, tile), tile)
        return [
            pltpu.make_async_copy(ref.at[slot], out.at[at], out_sems.at[slot, n])
            for n, (ref, out) in enumerate(((q_ref, out_q), (k_ref, out_k), (v_ref, out_v)))
        ]

    steps = x_ref.shape[1] // tile

    def body(step, carry):
        slot = step % 2

        @pl.when(step >= 2)
        def _():
            for move in store(step, slot):
                move.wait()

        x_t = x_ref[:, pl.ds(pl.multiple_of(step * tile, tile), tile)].T
        for side, ref in enumerate((left_ref, right_ref)):
            result = jnp.dot(x_t, ref[...], preferred_element_type=jnp.float32)
            k_ref[slot, :, side * DH : (side + 1) * DH] = result[:, :DH]
            v_ref[slot, :, side * DH : (side + 1) * DH] = result[:, DH : 2 * DH]
            q_ref[slot, :, side * half_q : (side + 1) * half_q] = result[:, 2 * DH :]
        for move in store(step, slot):
            move.start()
        return carry

    lax.fori_loop(0, steps, body, 0)
    for slot in range(2):
        for move in store(slot, slot):
            move.wait()


def weight_grads(plane, x, hops, planes, shapes):
    total, width = x.shape
    blocks = len(hops)
    flat = [array for group in hops for array in group]
    tile = 256
    f32, bf16 = jnp.float32, jnp.bfloat16
    hbm = pl.BlockSpec(memory_space=pl.ANY)
    columns = flat[0].shape[1]
    return pl.pallas_call(
        functools.partial(weight_grad_kernel, planes=planes, blocks=blocks),
        in_specs=[pl.BlockSpec(memory_space=pltpu.SMEM)] + [hbm] * (1 + len(flat)),
        out_specs=[hbm] * 3,
        out_shape=[jax.ShapeDtypeStruct(s, f32) for s in shapes],
        scratch_shapes=[
            pltpu.VMEM((total, width), bf16),
            pltpu.VMEM((total, columns), bf16),
            pltpu.VMEM((total, columns), bf16),
        ]
        + [pltpu.VMEM((2, tile, s[1]), f32) for s in shapes]
        + [pltpu.SemaphoreType.DMA((1 + 2 * blocks,)), pltpu.SemaphoreType.DMA((2, 3))],
        cost_estimate=pl.CostEstimate(flops=4 * total * width * columns, bytes_accessed=8 * total * width, transcendentals=0),
    )(plane.astype(jnp.int32).reshape(1), x, *flat)


def place_kernel(at_ref, w_hbm, *refs):
    pieces, (rows_hbm, first_hbm, sent_hbm, x_ref, w_ref, first_ref, sent_ref, sems) = refs[:-8], refs[-8:]
    rows, count = pieces[0].shape[0], len(pieces)
    moves = [pltpu.make_async_copy(w_hbm, w_ref, sems.at[count])]
    for n, piece in enumerate(pieces):
        row = pl.multiple_of(at_ref[n] * rows, rows)
        moves.append(pltpu.make_async_copy(piece, x_ref.at[pl.ds(row, rows)], sems.at[n]))
    for move in moves:
        move.start()
    for move in moves:
        move.wait()
    keep = pltpu.make_async_copy(x_ref, rows_hbm, sems.at[0])
    keep.start()
    middle = x_ref.shape[0] // 2
    product = jnp.dot(x_ref[middle:, :], w_ref[...], preferred_element_type=jnp.float32)
    first_ref[...] = product
    sent_ref[...] = product.astype(sent_ref.dtype)
    give = pltpu.make_async_copy(sent_ref, sent_hbm, sems.at[1])
    hold = pltpu.make_async_copy(first_ref, first_hbm, sems.at[2])
    give.start()
    hold.start()
    give.wait()
    hold.wait()
    keep.wait()


def place_pieces(slots, pieces, weight):
    rows, width = pieces[0].shape
    count = len(pieces)
    total, columns = rows * count, weight.shape[1]
    f32, bf16 = jnp.float32, jnp.bfloat16
    hbm = pl.BlockSpec(memory_space=pl.ANY)
    half = (total // 2, columns)
    return pl.pallas_call(
        place_kernel,
        in_specs=[pl.BlockSpec(memory_space=pltpu.SMEM)] + [hbm] * (1 + count),
        out_specs=[hbm] * 3,
        out_shape=[jax.ShapeDtypeStruct((total, width), bf16), jax.ShapeDtypeStruct(half, f32), jax.ShapeDtypeStruct(half, bf16)],
        scratch_shapes=[
            pltpu.VMEM((total, width), bf16),
            pltpu.VMEM(weight.shape, bf16),
            pltpu.VMEM(half, f32),
            pltpu.VMEM(half, bf16),
            pltpu.SemaphoreType.DMA((count + 1,)),
        ],
        cost_estimate=pl.CostEstimate(flops=total * width * columns, bytes_accessed=4 * total * width, transcendentals=0),
    )(slots, weight, *pieces)


def stationary_body(sizes, *arrays):
    return stationary(sizes, *arrays)


def stationary(sizes, layer_input, query_weight, key_weight, value_weight, out_grad, doc_ids):
    planes, across, cores = sizes
    spread = across * cores
    f32, bf16 = jnp.float32, jnp.bfloat16
    tok, width = layer_input.shape
    total = tok * planes
    half_q, half_k = query_weight.shape[1] // 2, key_weight.shape[1] // 2
    plane = lax.axis_index("srv")
    side, core = lax.axis_index("hid"), lax.axis_index("rep")
    last = planes - 1
    blocks = planes
    near_left = plane < planes // 2
    is_end = (plane == 0) | (plane == last)
    trio = ("srv", "hid", "rep")
    pairs = [(t, f) for t in range(planes) for f in range(spread)]
    straight = [(t * spread + f, f * spread + t) for t, f in pairs]
    crossed = [(t * spread + f, (f + cores) % spread * spread + t) for t, f in pairs]

    def climb(early):
        moves = []
        for t, f in pairs:
            x = f // cores
            target = f if (t % 2 == 0) == early else (f + cores) % spread
            moves.append((t * spread + f, target * spread + x * cores + t * cores // planes))
        return moves

    rise, fall = climb(True), climb(False)
    outer = [(0, 1), (1, 0), (last - 1, last), (last, last - 1)]
    line = [[(k, k + 1), (last - k, last - k - 1)] for k in range(last)]
    far_at, near_at = jnp.where(near_left, 1, 0), jnp.where(near_left, 0, 1)

    def part(array, at, size):
        return lax.dynamic_slice_in_dim(array, at * size, size, 1)

    pair_weight = lambda at: jnp.concatenate([part(key_weight, at, half_k), part(value_weight, at, half_k)], axis=1)
    wp_near, wp_far = pair_weight(near_at), pair_weight(far_at)
    wq_near, wq_far = part(query_weight, near_at, half_q), part(query_weight, far_at, half_q)
    g_near, g_far = part(out_grad, near_at, half_q), part(out_grad, far_at, half_q)
    begins = jnp.sum((doc_ids[None, :] < doc_ids[:, None]).astype(jnp.int32), axis=1).reshape(1, total)
    flags = jnp.stack([is_end, plane == 0]).astype(jnp.int32)

    part_rows = tok // across
    mine = lax.dynamic_slice_in_dim(layer_input, side * part_rows, part_rows, 0)
    other = lax.dynamic_slice_in_dim(layer_input, (1 - side) * part_rows, part_rows, 0)
    other = swap(other, "hid", across)
    even_plane = plane % 2 == 0
    up = lax.ppermute(jnp.where(even_plane, mine, other), trio, rise)
    down = lax.ppermute(jnp.where(even_plane, other, mine), trio, fall)
    straight_first = jnp.where(side == plane // cores, 0, 1)
    held = planes // cores
    slot = lambda owner, which, half: (owner * held + which) * across + half
    slots = []
    for which in (straight_first, 1 - straight_first):
        slots += [slot(core, which, side), slot(1 - core, which, side)]
        slots += [slot(core, 1 - which, 1 - side), slot(1 - core, 1 - which, 1 - side)]
    slots = jnp.stack(slots).astype(jnp.int32)
    wp_near, wp_far, wq_near, wq_far, g_near, g_far, begins, flags, slots, up = lax.optimization_barrier(
        (wp_near, wp_far, wq_near, wq_far, g_near, g_far, begins, flags, slots, up)
    )
    pieces = []
    for piece in (up, down):
        turned = swap(piece, "hid", across)
        mate = swap(piece, "rep", cores)
        turned_mate = swap(turned, "rep", cores)
        pieces += [piece, mate, turned, turned_mate]
    rows_all, first_far, first_sent = place_pieces(slots, pieces, wp_far)
    x_rows = [lax.slice_in_dim(rows_all, b * tok, (b + 1) * tok, axis=0) for b in range(planes)]

    g_next = lax.ppermute(jnp.where(is_end, g_far, g_near), "srv", outer)
    g_over = lax.ppermute(g_far, "srv", line[1])
    g_end = lax.ppermute(g_next, "srv", line[1])
    riders = {2: g_over, 3: g_end}
    g_pieces = [g_next]

    middle = total // 2
    chunks = [(rows_all[middle:], wp_far, wp_near), (rows_all[:middle], wp_far, wp_near)]
    chunks += [(x_rows[b], wq_far, wq_near) for b in range(blocks - 1, -1, -1)]
    landed = []
    for c, (x, w_far, w_near) in enumerate(chunks):
        far_part = first_far if c == 0 else jnp.dot(x, w_far, preferred_element_type=f32)
        near_part = jnp.dot(x, w_near, preferred_element_type=f32)
        moving = None
        for k in range(last):
            mine_now = far_part if k < planes // 2 else near_part
            if moving is not None:
                mine_now = mine_now + moving.astype(f32)
            mine_now = first_sent if c == 0 and k == 0 else mine_now.astype(bf16)
            if k == 0 and c in riders:
                moving = lax.ppermute(jnp.where(is_end, mine_now, riders[c]), "srv", outer)
                g_pieces.append(moving)
            elif c == len(chunks) - 1 and k == last - 1:
                moving = mine_now
            else:
                moving = lax.ppermute(mine_now, "srv", line[k])
        landed.append((near_part + moving.astype(f32)).astype(bf16) if c < 2 else (near_part, moving))

    pairs_at = [(landed[1], b * tok) if b < blocks // 2 else (landed[0], b * tok - middle) for b in range(blocks)]
    all_hops = [None] * blocks
    near_q, far_q, near_kv, far_kv = [[None] * blocks for _ in range(4)]
    sums = [None] * blocks
    lead = 2 * half_k
    g_near, *g_pieces, _ = lax.optimization_barrier((g_near, *g_pieces, landed[0]))
    for b in range(blocks - 1, -1, -1):
        g_first = g_pieces[b - 1] if b > 0 else g_near
        g_last = g_pieces[last - b - 1] if b < last else g_near
        fresh_q, moved_q = landed[2 + blocks - 1 - b]
        local = attend_block(flags, begins, pairs_at, fresh_q, moved_q, g_first, g_last, sums, b, middle // tok)
        hops = [local]
        for k in range(last):
            if b == blocks - 1 and k == 0:
                fresh_q, moved_q = landed[-1]
                wider = jnp.pad(moved_q, ((0, 0), (lead, 0)))
                hops.append(lax.ppermute(jnp.where(is_end, local, wider), "srv", outer))
                landed[-1] = (fresh_q, hops[1])
            elif b == blocks - 1 and k == last - 1:
                pass
            elif b == 0 and k == 0:
                hops.append(lax.ppermute(jnp.where(is_end, local, all_hops[blocks - 1][last - 1]), "srv", outer))
                all_hops[blocks - 1].append(hops[1])
            else:
                hops.append(lax.ppermute(hops[k], "srv", line[k]))
        all_hops[b] = hops
    for b in range(blocks):
        local, hops = all_hops[b][0], all_hops[b]
        near = jnp.where(is_end, local, hops[1])
        far = jnp.where(is_end, hops[3], hops[2])
        near_q[b], far_q[b], near_kv[b], far_kv[b] = near[:, lead:], far[:, lead:], near[:, :lead], far[:, :lead]

    nt = (((1,), (1,)), ((), ()))
    times = lambda a, w: lax.dot_general(a, w, nt, preferred_element_type=f32)
    terms = []
    for b in range(blocks):
        near_term = times(near_q[b], wq_near) + times(near_kv[b], wp_near)
        terms.append(near_term + times(far_q[b], wq_far) + times(far_kv[b], wp_far))
    summed = []
    for i in range(blocks // cores):
        even, odd = terms[cores * i], terms[cores * i + 1]
        theirs = jnp.where(core == 0, odd, even).astype(bf16)
        ours = jnp.where(core == 0, even, odd)
        summed.append((ours + swap(theirs, "rep", cores).astype(f32)).astype(bf16))
    parts = []
    for i, block in reversed(list(enumerate(summed))):
        for x in range(across):
            home = [(a, b) for a, b in (straight if x == i else crossed) if a % spread // cores == x]
            parts.append(lax.ppermute(block, trio, home).astype(f32))
    input_grad = functools.reduce(jnp.add, parts).astype(bf16)

    shapes = [(width, w.shape[1]) for w in (query_weight, key_weight, value_weight)]
    outs = weight_grads(plane, rows_all, all_hops, planes, shapes)
    return (input_grad, *outs)


def solution(mesh):
    in_specs = (
        P(("groups", "srv"), ("hid", "rep")),
        P("srv", ("hid", "rep")),
        P("srv", ("hid", "rep")),
        P("srv", ("hid", "rep")),
        P(("groups", "srv"), ("hid", "rep")),
        P("groups"),
    )
    out_specs = (
        P(("groups", "srv"), ("hid", "rep")),
        P(("groups", "srv"), ("hid", "rep")),
        P(("groups", "srv"), ("hid", "rep")),
        P(("groups", "srv"), ("hid", "rep")),
    )
    sizes = (mesh.shape["srv"], mesh.shape["hid"], mesh.shape["rep"])
    split = HK // (sizes[1] * sizes[2])
    fits = sizes[0] == sizes[1] * sizes[2] and sizes[1] == 2 and sizes[2] == 2 and split == 2
    chosen = functools.partial(stationary_body, sizes) if fits else body
    return jax.shard_map(chosen, mesh=mesh, in_specs=in_specs, out_specs=out_specs, check_vma=False)
```
